32 devices in a mesh: seq: 4 (over z), batch: 4 (over y, x), chan: 2 (over core).
Axes of the slice: x: 2, y: 2, z: 4, core: 2. Of those that a mesh axis runs over, the one named last changes fastest.
Arguments:
- gate_input: bfloat16 [8, 256, 4096], P('batch', 'seq', 'chan'), may hold values from -20 to 20
- key_input: bfloat16 [8, 256, 4096], P('batch', 'seq', 'chan'), may hold values from -6 to 6
- value_input: bfloat16 [8, 256, 4096], P('batch', 'seq', 'chan'), may hold values from -6 to 6
- cotangent: bfloat16 [8, 256, 4096], P('batch', 'seq', 'chan'), may hold values from -6 to 6
- filters: float32 [256, 256], P('chan'), may hold values from -0.75 to 0.75
- document_lengths: int32 [8, 2], P('batch'), may hold values from 1 to 192, 256 in all within a row
Outputs:
- gated_output: bfloat16 [8, 256, 4096], P('batch', 'seq', 'chan')
- gate_gradient: bfloat16 [8, 256, 4096], P('batch', 'seq', 'chan')
- key_gradient: bfloat16 [8, 256, 4096], P('batch', 'seq', 'chan')
- value_gradient: bfloat16 [8, 256, 4096], P('batch', 'seq', 'chan')
- filter_update: float32 [256, 256], P(('seq', 'batch'), 'chan')
The draws below stay inside these ranges and needn't reach their ends.
Inputs may be any that keep to these rules, and one draw needn't show every extreme that they name: `document_lengths`: each row lists, in order, the lengths of the documents packed end to end into one sequence; a row sums to 256.
All inputs are finite; a program needn't handle non-finite values.
Results may differ from the reference program's by a relative error of at most 0.0057.
Values may be sent and summed in bfloat16 or wider, within the bound.
A program may use at most 128 MiB of HBM per device.

```python
import math
import jax
import jax.numpy as jnp
import numpy as np
from jax import lax

D = 4096
GROUPS = 256
SPAN = 64
SEQS = 8
SEQ_LEN = 256
FILT = 256
DOC_MAX = 192
NDOCS = 2
N_SEQ = 4


def draw_gate_input(key, part):
    noise_key = jax.random.fold_in(key, 11)
    scale_key = jax.random.fold_in(key, 12)
    channel = jnp.arange(D, dtype=jnp.float32)
    factor = jnp.exp(jax.random.uniform(scale_key, (D,), minval=-0.69, maxval=0.69))
    scale = 0.25 * jnp.exp(2.302585 * channel / D) * factor
    values = jnp.clip(jax.random.normal(noise_key, (SEQS, SEQ_LEN, D)), -4.0, 4.0)
    return (values * scale[None, None, :]).astype(jnp.bfloat16)


def block_scale(key, shape, shards, least, high):
    loudness, own = 1.0, jax.random.fold_in(key, 6)
    for axis_at, parts in shards:
        heights = jnp.exp(jax.random.uniform(jax.random.fold_in(own, axis_at), (parts,), jnp.float32, least / len(shards), high / len(shards)))
        loudness = loudness * jnp.repeat(heights, shape[axis_at] // parts).reshape([-1 if axis == axis_at else 1 for axis in range(len(shape))])
    return loudness


def profile(amount, total, limit, lean):
    portions = [(1 << 20) // math.isqrt(grade ** lean) + 1 for grade in range(2, amount + 1)]
    surplus, given = total - limit - (amount - 1), [1] * (amount - 1)
    while surplus > 0:
        movable = [i for i in range(amount - 1) if given[i] < limit]
        mass, budget = sum([portions[i] for i in movable]), surplus
        for i in movable:
            extra = min(limit - given[i], max(1, budget * portions[i] // mass), surplus)
            given[i] = given[i] + extra
            surplus = surplus - extra
    return np.array([limit] + given)


def uneven_parts(rng, count, total, reach, lean):
    if count == 2:
        one = jax.random.randint(rng, (), max(1, total - reach), min(reach, total - 1) + 1)
        return jnp.stack([one, total - one])
    sizes = jnp.asarray(profile(count, total, reach, lean), jnp.int32)
    couples = (count - 1) // 2
    giver, taker = sizes[1:1 + 2 * couples:2], sizes[2:2 + 2 * couples:2]
    slack = jnp.minimum(giver - 1, reach - taker)
    shifted = jax.random.randint(jax.random.fold_in(rng, 1), (couples,), 0, 1 << 20) % (slack + 1)
    sizes = sizes.at[1:1 + 2 * couples:2].set(giver - shifted).at[2:2 + 2 * couples:2].set(taker + shifted)
    return sizes[jax.random.permutation(jax.random.fold_in(rng, 2), count)]


def centred(rng, extent, scale, most, split=(), kind=jnp.bfloat16):
    drawn = jax.random.normal(rng, extent, jnp.float32) * scale
    if len(split) > 0:
        drawn = block_scale(rng, extent, split, -0.22, 0.18) * drawn
    return jnp.clip(drawn, min=-most, max=most).astype(kind)


def setup_inputs(seed: int = 0) -> dict:
    key_of = jax.random.split(jax.random.key(seed), 7)
    return {
        "gate_input": draw_gate_input(jax.random.fold_in(key_of[6], 71), 0),
        "key_input": centred(key_of[1], (SEQS, SEQ_LEN, D), 1.0, 6.0, ((0, 4), (1, 4), (2, 2))),
        "value_input": centred(key_of[2], (SEQS, SEQ_LEN, D), 1.0, 6.0, ((0, 4), (1, 4), (2, 2))),
        "cotangent": centred(key_of[3], (SEQS, SEQ_LEN, D), 1.0, 6.0, ((0, 4), (1, 4), (2, 2))),
        "filters": centred(key_of[4], (GROUPS, FILT), SPAN ** -0.5, 0.75, ((0, 2),), jnp.float32),
        "document_lengths": jax.vmap(lambda own: uneven_parts(own, NDOCS, SEQ_LEN, DOC_MAX, 2))(jax.random.split(key_of[5], SEQS)).reshape((SEQS, NDOCS)).astype(jnp.int32),
    }


reach_blocks = 5

def span_documents(lengths, index):
    rows = jnp.arange(SPAN, dtype=jnp.int32)
    positions = index * SPAN + rows
    ends = jnp.cumsum(lengths)
    documents = lax.optimization_barrier(jnp.sum((positions[:, None] >= ends[None, :]).astype(jnp.int32), axis=1))
    inside = (positions >= 0) & (positions < SEQ_LEN)
    return (positions, documents, inside)

def pair_keep(lengths, target, source):
    target_positions, target_documents, target_in = span_documents(lengths, target)
    source_positions, source_documents, source_in = span_documents(lengths, source)
    keep = (target_documents[:, None] == source_documents[None, :]) & target_in[:, None] & source_in[None, :]
    keep = keep & (source_positions[None, :] <= target_positions[:, None])
    return keep.astype(jnp.float32)

def reference(gate_input, key_input, value_input, cotangent, filters, document_lengths):
    members = D // GROUPS
    rounded_filters = lax.optimization_barrier(filters.astype(jnp.bfloat16)).astype(jnp.float32)
    rows = jnp.arange(SPAN, dtype=jnp.int32)

    def toeplitz(lag):
        taps = lag * SPAN + rows[:, None] - rows[None, :]
        valid = (taps >= 0) & (taps < FILT)
        picked = jnp.take(rounded_filters, jnp.clip(taps, 0, FILT - 1), axis=1)
        return jnp.where(valid[None], picked, 0.0)
    blocks = jnp.stack([toeplitz(lag) for lag in range(reach_blocks)])
    units = (key_input.astype(jnp.float32) * value_input.astype(jnp.float32)).astype(jnp.bfloat16)
    gated_cotangent = (cotangent.astype(jnp.float32) * gate_input.astype(jnp.float32)).astype(jnp.bfloat16)
    margin = (reach_blocks - 1) * SPAN

    def per_sequence(operands):
        unit_seq, cotangent_seq, lengths = operands
        unit_pad = jnp.pad(unit_seq.astype(jnp.float32), ((margin, margin), (0, 0))).reshape(-1, GROUPS, members)
        cotangent_pad = jnp.pad(cotangent_seq.astype(jnp.float32), ((margin, margin), (0, 0))).reshape(-1, GROUPS, members)

        def per_span(index):
            own = lax.dynamic_slice_in_dim(cotangent_pad, index * SPAN + margin, SPAN, 0)
            forward = jnp.zeros((SPAN, GROUPS, members), jnp.float32)
            backward = jnp.zeros((SPAN, GROUPS, members), jnp.float32)
            tap_sums = jnp.zeros((FILT, GROUPS), jnp.float32)
            for lag in range(reach_blocks):
                block = blocks[lag]
                source = lax.dynamic_slice_in_dim(unit_pad, (index - lag) * SPAN + margin, SPAN, 0)
                later = lax.dynamic_slice_in_dim(cotangent_pad, (index + lag) * SPAN + margin, SPAN, 0)
                keep_forward = pair_keep(lengths, index, index - lag)
                keep_backward = pair_keep(lengths, index + lag, index)
                forward = forward + jnp.einsum('gij,jgm->igm', block * keep_forward[None], source)
                backward = backward + jnp.einsum('gij,igm->jgm', block * keep_backward[None], later)
                paired = jnp.einsum('igm,jgm->ijg', own, source) * keep_forward[:, :, None]
                taps = (lag * SPAN + rows[:, None] - rows[None, :]).reshape(-1)
                tap_sums = tap_sums + jax.ops.segment_sum(paired.reshape(SPAN * SPAN, GROUPS), jnp.clip(taps, 0, FILT - 1), num_segments=FILT)
            return (forward, backward, tap_sums)
        forward, backward, tap_sums = lax.map(per_span, jnp.arange(N_SEQ, dtype=jnp.int32))
        return (forward.reshape(SEQ_LEN, D), backward.reshape(SEQ_LEN, D), lax.optimization_barrier(jnp.sum(tap_sums, axis=0)))
    filtered, adjoint, sums = lax.map(per_sequence, (units, gated_cotangent, document_lengths))
    filter_sums = lax.optimization_barrier(jnp.sum(sums, axis=0))
    root_mean = jnp.sqrt(jnp.mean(filter_sums * filter_sums) + 1e-06)
    filter_update = filter_sums * jnp.minimum(1.0, 1.0 / root_mean)
    gated_output = (gate_input.astype(jnp.float32) * filtered).astype(jnp.bfloat16)
    gate_gradient = (cotangent.astype(jnp.float32) * filtered).astype(jnp.bfloat16)
    key_gradient = (adjoint * value_input.astype(jnp.float32)).astype(jnp.bfloat16)
    value_gradient = (adjoint * key_input.astype(jnp.float32)).astype(jnp.bfloat16)
    return (gated_output, gate_gradient, key_gradient, value_gradient, filter_update)
```

```python
import functools

import jax
import jax.numpy as jnp
from jax import lax
from jax.experimental import pallas as pl
from jax.experimental.pallas import tpu as pltpu
from jax.sharding import PartitionSpec as P

MESH = pl.DeviceIdType.MESH
LANES = 128
HELD = 4
SHARES_AT = 4


def kernel(
    dims, gate, key, value, cotangent, filters, lengths,
    gated_output, gate_gradient, key_gradient, value_gradient, filter_update,
    units, followers, reversed_own, plain, flipped, forward_block, backward_block,
    forward_mask, backward_mask, sums_mask, tap_sums, shares_out, shares_in, squares_out, squares_in,
    chan_out, chan_in,
    unit_send, unit_recv, cot_send, cot_recv, share_send, share_recv, square_send, square_recv,
    chan_send, chan_recv,
):
    n_seq, n_batch, n_chan, reach, wide, chunks, tiles, seqs, span, groups, taps, ndocs = dims
    everyone = n_seq * n_batch * n_chan
    sharers = n_seq * n_batch
    here = lax.axis_index("seq")
    batch = lax.axis_index("batch")
    chan = lax.axis_index("chan")
    me = (here * n_batch + batch) * n_chan + chan
    mine = here * n_batch + batch
    per_tile = LANES * groups // (tiles * chunks * LANES)
    members = LANES // per_tile
    lanes = tiles * LANES
    own = reach * span
    hub = reach == 2

    barrier = pltpu.get_barrier_semaphore()

    rest = wide - own - span
    for c in range(chunks):
        for s in range(seqs):
            units[c, s, pl.ds(0, own), :] = jnp.zeros((own, lanes), jnp.bfloat16)
            units[c, s, pl.ds(own + span, rest), :] = jnp.zeros((rest, lanes), jnp.bfloat16)
            followers[c, s, pl.ds(span, wide - span), :] = jnp.zeros((wide - span, lanes), jnp.bfloat16)

    def greet(i, carry):
        other = lax.rem(me + i, everyone)
        pl.semaphore_signal(
            barrier, inc=1, device_id_type=MESH,
            device_id={
                "seq": other // (n_batch * n_chan),
                "batch": lax.rem(other // n_chan, n_batch),
                "chan": lax.rem(other, n_chan),
            },
        )
        return carry

    lax.fori_loop(1, everyone, greet, 0)

    for c in range(chunks):
        at = pl.ds(c * lanes, lanes)
        for s in range(seqs):
            u = (key[s, :, at].astype(jnp.float32) * value[s, :, at].astype(jnp.float32)).astype(jnp.bfloat16)
            g = (cotangent[s, :, at].astype(jnp.float32) * gate[s, :, at].astype(jnp.float32)).astype(jnp.bfloat16)
            units[c, s, pl.ds(own, span), :] = u
            followers[c, s, pl.ds(0, span), :] = g

    def unit_copy(lag, c):
        source = units.at[c, :, pl.ds((reach - lag + 1) * span, span), :]
        target = units.at[c, :, pl.ds((reach - lag) * span, span), :]
        return pltpu.make_async_remote_copy(
            src_ref=source, dst_ref=target, send_sem=unit_send.at[lag - 1, c], recv_sem=unit_recv.at[lag - 1, c],
            device_id={"seq": here + 1}, device_id_type=MESH,
        )

    def cot_copy(lag, c):
        source = followers.at[c, :, pl.ds((lag - 1) * span, span), :]
        target = followers.at[c, :, pl.ds(lag * span, span), :]
        return pltpu.make_async_remote_copy(
            src_ref=source, dst_ref=target, send_sem=cot_send.at[lag - 1, c], recv_sem=cot_recv.at[lag - 1, c],
            device_id={"seq": here - 1}, device_id_type=MESH,
        )

    def sends_up(lag):
        return (here >= lag - 1) & (here + 1 < n_seq)

    def sends_down(lag):
        return (here + lag - 1 < n_seq) & (here >= 1)

    def send(lag, c):
        @pl.when(sends_up(lag))
        def _():
            unit_copy(lag, c).start()

        @pl.when(sends_down(lag))
        def _():
            cot_copy(lag, c).start()

    def receive(lag, c):
        @pl.when(here >= lag)
        def _():
            unit_copy(lag, c).wait_recv()

        @pl.when(here + lag < n_seq)
        def _():
            cot_copy(lag, c).wait_recv()

    pl.semaphore_wait(barrier, everyone - 1)
    for c in range(chunks):
        send(1, c)

    def documents(positions, s):
        count = jnp.zeros(positions.shape, jnp.int32)
        end = 0
        for n in range(ndocs):
            end = end + lengths[s, n]
            count = count + (positions >= end).astype(jnp.int32)
        return count

    rows = lax.broadcasted_iota(jnp.int32, (span, 1), 0)
    cols = lax.broadcasted_iota(jnp.int32, (1, wide), 1)
    for s in range(seqs):
        earlier = (here - reach) * span + cols
        later = here * span + cols
        target = here * span + rows
        back = here * span + (span - 1 - rows)
        earlier_doc = documents(earlier, s)
        later_doc = documents(later, s)
        target_doc = documents(target, s)
        back_doc = documents(back, s)
        keep = (earlier_doc == target_doc) & (earlier <= target) & (earlier >= 0)
        forward_mask[s] = jnp.where(keep, 1.0, 0.0).astype(jnp.bfloat16)
        if hub:
            first = cols < span
            origin = jnp.where(first, earlier + span, earlier)
            goal = jnp.where(first, back + span, back)
            goal_doc = jnp.where(first, documents(back + span, s), back_doc)
            keep = (documents(origin, s) == goal_doc) & (origin <= goal) & (origin >= 0) & (goal < n_seq * span)
        else:
            keep = (earlier_doc == back_doc) & (earlier <= back) & (earlier >= 0)
        sums_mask[s] = jnp.where(keep, 1.0, 0.0)
        keep = (later_doc == target_doc) & (later >= target) & (later < n_seq * span)
        backward_mask[s] = jnp.where(keep, 1.0, 0.0).astype(jnp.bfloat16)

    rounded = filters[...].astype(jnp.bfloat16)
    a = lax.broadcasted_iota(jnp.int32, (taps, wide), 0)
    b = lax.broadcasted_iota(jnp.int32, (taps, wide), 1)
    flip = own - b
    flip = jnp.where(flip < 0, flip + wide, flip)
    plain[...] = jnp.dot(rounded, jnp.where(a == b, 1.0, 0.0).astype(jnp.bfloat16), preferred_element_type=jnp.float32)
    flipped[...] = jnp.dot(rounded, jnp.where(a == flip, 1.0, 0.0).astype(jnp.bfloat16), preferred_element_type=jnp.float32)

    def build(t, carry):
        for i in range(per_tile):
            g = t * per_tile + i
            at = pl.ds(pl.multiple_of(g * span, span), span)
            row = jnp.broadcast_to(flipped[pl.ds(g, 1), :], (span, wide))
            forward_block[at, :] = pltpu.roll(row, 0, 1, stride=1, stride_axis=0).astype(jnp.bfloat16)
            row = jnp.broadcast_to(plain[pl.ds(g, 1), :], (span, wide))
            backward_block[at, :] = pltpu.roll(row, 0, 1, stride=1, stride_axis=0).astype(jnp.bfloat16)
        return carry

    order_a = lax.broadcasted_iota(jnp.int32, (span, span), 0)
    order_b = lax.broadcasted_iota(jnp.int32, (span, span), 1)
    exchange = jnp.where(order_a + order_b == span - 1, 1.0, 0.0).astype(jnp.bfloat16)
    lane = lax.broadcasted_iota(jnp.int32, (1, LANES), 1) // members

    def members_apart(block):
        return jnp.concatenate(
            [block * jnp.where(lane == i, 1.0, 0.0).astype(jnp.bfloat16) for i in range(per_tile)], axis=0
        )

    def paired(c, j, carry):
        at = pl.ds(pl.multiple_of(j * LANES, LANES), LANES)
        total = None
        for s in range(seqs):
            target = members_apart(reversed_own[c, s, pl.ds(0, span), at])
            if hub:
                target = jnp.concatenate([target, members_apart(reversed_own[c, s, pl.ds(span, span), at])], axis=1)
                past = units[c, s, pl.ds(own - span, span), at]
                blank = jnp.zeros((span, LANES), jnp.bfloat16)
                tail = jnp.zeros((wide - own - span, LANES), jnp.bfloat16)
                source = jnp.concatenate(
                    [
                        jnp.concatenate([blank, past, units[c, s, pl.ds(own, span), at], tail], axis=0),
                        jnp.concatenate([past, blank, blank, tail], axis=0),
                    ],
                    axis=1,
                )
            else:
                source = units[c, s, :, at]
            products = lax.dot_general(
                target, source, (((1,), (1,)), ((), ())), preferred_element_type=jnp.float32
            ).reshape(per_tile, span, wide)
            products = products * sums_mask[s][None]
            total = products if total is None else total + products
        for i in range(per_tile):
            aligned = pltpu.roll(total[i], 0, 1, stride=1, stride_axis=0)
            tap_sums[pl.ds((c * tiles + j) * per_tile + i, 1), :] = jnp.sum(aligned, axis=0, keepdims=True)
        return carry

    def reverse(c):
        for s in range(seqs):
            for n in range(2 if hub else 1):
                at = pl.ds(n * span, span)
                reversed_own[c, s, at, :] = jnp.dot(
                    exchange, followers[c, s, at, :], preferred_element_type=jnp.float32
                ).astype(jnp.bfloat16)

    for c in range(chunks):
        lax.fori_loop(c * tiles, (c + 1) * tiles, build, 0)
        for lag in range(1, reach):
            receive(lag, c)
            if not (hub and c >= HELD):
                send(lag + 1, c)
        if hub:
            reverse(c)
            lax.fori_loop(0, tiles, functools.partial(paired, c), 0)
    if not hub:
        for c in range(chunks):
            receive(reach, c)
            reverse(c)
            lax.fori_loop(0, tiles, functools.partial(paired, c), 0)

    a = lax.broadcasted_iota(jnp.int32, (taps, wide), 0)
    b = lax.broadcasted_iota(jnp.int32, (taps, wide), 1)
    pick = jnp.where(a + b == own + span - 1, 1.0, 0.0)
    by_tap = lax.dot_general(
        pick, tap_sums[...], (((1,), (1,)), ((), ())),
        precision=lax.Precision.HIGHEST, preferred_element_type=jnp.float32,
    )
    share = taps // sharers
    for i in range(sharers):
        shares_out[i] = by_tap[i * share : (i + 1) * share, :]

    def share_copy(i):
        other = lax.rem(mine + i, sharers)
        return pltpu.make_async_remote_copy(
            src_ref=shares_out.at[other], dst_ref=shares_in.at[i - 1],
            send_sem=share_send.at[i - 1], recv_sem=share_recv.at[i - 1],
            device_id={"seq": other // n_batch, "batch": lax.rem(other, n_batch)}, device_id_type=MESH,
        )

    def square_copy(i):
        other = lax.rem(mine + i, sharers)
        return pltpu.make_async_remote_copy(
            src_ref=squares_out, dst_ref=squares_in.at[i - 1],
            send_sem=square_send.at[i - 1], recv_sem=square_recv.at[i - 1],
            device_id={"seq": other // n_batch, "batch": lax.rem(other, n_batch)}, device_id_type=MESH,
        )

    def chan_copy(i):
        return pltpu.make_async_remote_copy(
            src_ref=chan_out, dst_ref=chan_in.at[i - 1],
            send_sem=chan_send.at[i - 1], recv_sem=chan_recv.at[i - 1],
            device_id={"chan": lax.rem(chan + i, n_chan)}, device_id_type=MESH,
        )

    def loop(low, high, act):
        if high <= 32:
            for i in range(low, high):
                act(i)
            return

        def step(i, carry):
            act(i)
            return carry

        lax.fori_loop(low, high, step, 0)

    def convolve(c, j, carry):
        at = pl.ds(pl.multiple_of(j * LANES, LANES), LANES)
        t = c * tiles + j
        out = pl.ds(pl.multiple_of(t * LANES, LANES), LANES)
        height = per_tile * span
        block = pl.ds(pl.multiple_of(t * height, height), height)

        def apply(block_ref, mask_ref, data_ref, s):
            masked = block_ref[block, :].reshape(per_tile, span, wide) * mask_ref[s][None]
            results = jnp.dot(
                masked.reshape(height, wide), data_ref[c, s, :, at], preferred_element_type=jnp.float32
            )
            picked = results[:span]
            for i in range(1, per_tile):
                picked = jnp.where(lane == i, results[i * span : (i + 1) * span], picked)
            return picked

        for s in range(seqs):
            filtered = apply(forward_block, forward_mask, units, s)
            gated_output[s, :, out] = (gate[s, :, out].astype(jnp.float32) * filtered).astype(jnp.bfloat16)
            gate_gradient[s, :, out] = (cotangent[s, :, out].astype(jnp.float32) * filtered).astype(jnp.bfloat16)
            adjoint = apply(backward_block, backward_mask, followers, s)
            key_gradient[s, :, out] = (adjoint * value[s, :, out].astype(jnp.float32)).astype(jnp.bfloat16)
            value_gradient[s, :, out] = (adjoint * key[s, :, out].astype(jnp.float32)).astype(jnp.bfloat16)
        return carry

    loop(1, sharers, lambda i: share_copy(i).start())
    if hub:
        for c in range(HELD, chunks):
            send(reach, c)
    for c in range(chunks):
        if hub:
            receive(reach, c)
        if c == SHARES_AT:
            loop(1, sharers, lambda i: share_copy(i).wait_recv())
            total = shares_out[mine] + jnp.sum(shares_in[...], axis=0)
            filter_update[...] = total
            squares_out[...] = jnp.sum(total * total, axis=0, keepdims=True)
        if c == SHARES_AT + 1:
            loop(1, sharers, lambda i: square_copy(i).start())
        lax.fori_loop(0, tiles, functools.partial(convolve, c), 0)
    loop(1, sharers, lambda i: square_copy(i).wait_recv())
    chan_out[...] = jnp.sum(squares_in[...], axis=0) + squares_out[...]
    loop(1, sharers, lambda i: share_copy(i).wait_send())
    loop(1, sharers, lambda i: square_copy(i).wait_send())
    loop(1, n_chan, lambda i: chan_copy(i).start())
    loop(1, n_chan, lambda i: chan_copy(i).wait_recv())
    squares = jnp.sum(chan_in[...], axis=0) + chan_out[...]
    mean = jnp.sum(squares, axis=1, keepdims=True) / (taps * groups * n_chan)
    filter_update[...] = filter_update[...] * jnp.minimum(1.0, 1.0 / jnp.sqrt(mean + 1e-06))
    loop(1, n_chan, lambda i: chan_copy(i).wait_send())
    for lag in range(1, reach + 1):
        @pl.when(sends_up(lag))
        def _():
            for c in range(chunks):
                unit_copy(lag, c).wait_send()

        @pl.when(sends_down(lag))
        def _():
            for c in range(chunks):
                cot_copy(lag, c).wait_send()


def wide_device(sizes, gate_input, key_input, value_input, cotangent, filters, document_lengths):
    n_seq, n_batch, n_chan = sizes
    seqs, span, width = gate_input.shape
    groups, taps = filters.shape
    ndocs = document_lengths.shape[1]
    longest = min(taps, n_seq * span - span)
    reach = (longest - 1) // span if ndocs == 2 else (longest - 2) // span + 1
    wide = -(-((reach + 2) * span - 1) // LANES) * LANES
    chunks = 8
    tiles = width // (chunks * LANES)
    lanes = tiles * LANES
    sharers = n_seq * n_batch
    share = taps // sharers
    dims = (n_seq, n_batch, n_chan, reach, wide, chunks, tiles, seqs, span, groups, taps, ndocs)
    bf16, f32 = jnp.bfloat16, jnp.float32
    vmem = pl.BlockSpec(memory_space=pltpu.VMEM)
    dma = pltpu.SemaphoreType.DMA
    like = jax.ShapeDtypeStruct(gate_input.shape, bf16)
    return pl.pallas_call(
        functools.partial(kernel, dims),
        out_shape=(like, like, like, like, jax.ShapeDtypeStruct((share, groups), f32)),
        in_specs=[vmem] * 5 + [pl.BlockSpec(memory_space=pltpu.SMEM)],
        out_specs=(vmem,) * 5,
        scratch_shapes=[
            pltpu.VMEM((chunks, seqs, wide, lanes), bf16),
            pltpu.VMEM((chunks, seqs, wide, lanes), bf16),
            pltpu.VMEM((chunks, seqs, 2 * span, lanes), bf16),
            pltpu.VMEM((groups, wide), f32),
            pltpu.VMEM((groups, wide), f32),
            pltpu.VMEM((groups * span, wide), bf16),
            pltpu.VMEM((groups * span, wide), bf16),
            pltpu.VMEM((seqs, span, wide), bf16),
            pltpu.VMEM((seqs, span, wide), bf16),
            pltpu.VMEM((seqs, span, wide), f32),
            pltpu.VMEM((groups, wide), f32),
            pltpu.VMEM((sharers, share, groups), f32),
            pltpu.VMEM((sharers - 1, share, groups), f32),
            pltpu.VMEM((1, groups), f32),
            pltpu.VMEM((sharers - 1, 1, groups), f32),
            pltpu.VMEM((1, groups), f32),
            pltpu.VMEM((n_chan - 1, 1, groups), f32),
            dma((reach, chunks)), dma((reach, chunks)), dma((reach, chunks)), dma((reach, chunks)),
            dma((sharers - 1,)), dma((sharers - 1,)), dma((sharers - 1,)), dma((sharers - 1,)),
            dma((n_chan - 1,)), dma((n_chan - 1,)),
        ],
        compiler_params=pltpu.CompilerParams(
            collective_id=0, has_side_effects=True, vmem_limit_bytes=60 * 1024 * 1024
        ),
    )(gate_input, key_input, value_input, cotangent, filters, document_lengths)


AHEAD = 3
TOGETHER = 2
LOADS = 4


def hub_kernel(
    dims, gate_hbm, key_hbm, value_hbm, cotangent_hbm, filters_hbm, lengths_hbm,
    gated_output, gate_gradient, key_gradient, value_gradient, filter_update,
    gate, key, value, cotangent, filters, lengths, units, followers, up_out, down_out,
    forward_block, backward_block, bases, wide_masks, half_masks, blends, tap_sums,
    shares_out, shares_in, squares_out, squares_in, chan_out, chan_in,
    load_sem, small_sem, up_send, up_recv, down_send, down_recv, share_send, share_recv, square_send, square_recv,
    chan_send, chan_recv,
):
    n_seq, n_batch, n_chan, tiles, seqs, span, groups, taps = dims
    sharers = n_seq * n_batch
    here = lax.axis_index("seq")
    batch = lax.axis_index("batch")
    chan = lax.axis_index("chan")
    mine = here * n_batch + batch
    per_tile = groups // tiles
    members = LANES // per_tile
    both = 2 * span
    f32, bf16 = jnp.float32, jnp.bfloat16

    part = tiles // LOADS * LANES

    def loads(q):
        at = pl.ds(q * part, part)
        pairs = ((key_hbm, key), (value_hbm, value), (cotangent_hbm, cotangent), (gate_hbm, gate))
        return [
            pltpu.make_async_copy(src.at[:, :, at], dst.at[:, :, at], load_sem.at[q, n])
            for n, (src, dst) in enumerate(pairs)
        ]

    for q in range(LOADS):
        for copy in loads(q):
            copy.start()

    filters_copy = pltpu.make_async_copy(filters_hbm, filters, small_sem.at[0])
    lengths_copy = pltpu.make_async_copy(lengths_hbm, lengths, small_sem.at[1])
    lengths_copy.start()
    filters_copy.start()
    shares_in[...] = jnp.zeros(shares_in.shape, f32)
    squares_in[...] = jnp.zeros(squares_in.shape, f32)

    barrier = pltpu.get_barrier_semaphore()

    def sharer(i):
        other = lax.rem(mine + i, sharers)
        return {"seq": other // n_batch, "batch": lax.rem(other, n_batch)}

    def greet(i, carry):
        pl.semaphore_signal(barrier, inc=1, device_id_type=MESH, device_id=sharer(i))
        return carry

    lax.fori_loop(1, sharers, greet, 0)
    for i in range(1, n_chan):
        pl.semaphore_signal(barrier, inc=1, device_id_type=MESH, device_id={"chan": lax.rem(chan + i, n_chan)})

    first, last = here == 0, here == n_seq - 1
    hub = jnp.logical_not(first | last)
    own_units = units.at[:, :, pl.ds(span, span), :]
    own_cots = followers.at[:, :, pl.ds(0, span), :]

    def up_copy(j, source=up_out):
        return pltpu.make_async_remote_copy(
            src_ref=source.at[j], dst_ref=units.at[j, :, pl.ds(0, span), :],
            send_sem=up_send.at[j], recv_sem=up_recv.at[j], device_id={"seq": here + 1}, device_id_type=MESH,
        )

    def down_copy(j, source=down_out):
        return pltpu.make_async_remote_copy(
            src_ref=source.at[j], dst_ref=followers.at[j, :, pl.ds(span, span), :],
            send_sem=down_send.at[j], recv_sem=down_recv.at[j], device_id={"seq": here - 1}, device_id_type=MESH,
        )

    def gather(j, carry):
        at = pl.ds(pl.multiple_of(j * LANES, LANES), LANES)
        for s in range(seqs):
            u = (key[s, :, at].astype(f32) * value[s, :, at].astype(f32)).astype(bf16)
            g = (cotangent[s, :, at].astype(f32) * gate[s, :, at].astype(f32)).astype(bf16)
            units[j, s, pl.ds(span, span), :] = u
            followers[j, s, pl.ds(0, span), :] = g

        @pl.when(first)
        def _():
            up_copy(j, own_units).start()
            for s in range(seqs):
                units[j, s, pl.ds(0, span), :] = jnp.zeros((span, LANES), bf16)

        @pl.when(last)
        def _():
            down_copy(j, own_cots).start()
            for s in range(seqs):
                followers[j, s, pl.ds(span, span), :] = jnp.zeros((span, LANES), bf16)

        return carry

    for q in range(LOADS):
        for copy in loads(q):
            copy.wait()
        if q == 0:
            pl.semaphore_wait(barrier, sharers - 1 + n_chan - 1)
        lax.fori_loop(q * (tiles // LOADS), (q + 1) * (tiles // LOADS), gather, 0)

    lengths_copy.wait()
    filters_copy.wait()

    main = jnp.where(here * 2 >= n_seq, 1, 0)
    rows = lax.broadcasted_iota(jnp.int32, (both, LANES), 0)
    half = lax.broadcasted_iota(jnp.int32, (span, LANES), 0)
    one, zero = jnp.ones((), f32), jnp.zeros((), f32)

    def flag(condition):
        return jnp.where(condition, one, zero)

    for s in range(seqs):
        end = lengths[s, 0]
        at = pl.ds(s * LANES, LANES)

        def is_main(positions):
            return jnp.where(positions >= end, 1, 0) == main

        in_front = end <= both
        past_held = (here == 1) | ((here == 2) & in_front)
        next_held = (here == 2) | ((here == 1) & jnp.logical_not(in_front))
        past = (here - 1) * span
        own_main = is_main(here * span + half)
        back = both - 1 - rows
        wide_masks[0, :, at] = flag(is_main(past + rows) & ((rows >= span) | past_held)).astype(bf16)
        wide_masks[1, :, at] = flag(is_main(here * span + rows) & ((rows < span) | next_held)).astype(bf16)
        wide_masks[2, :, at] = flag(is_main(past + back) & ((back >= span) | past_held)).astype(bf16)
        wide_masks[3, :, at] = flag(jnp.logical_not(is_main(past + back)) & (back >= span)).astype(bf16)
        half_masks[:, at] = flag(jnp.logical_not(own_main)).astype(bf16)
        relay = flag((here == 1) & in_front)
        blends[0, :, at] = flag(own_main)
        blends[1, :, at] = jnp.broadcast_to(relay, (span, LANES))
        blends[2, :, at] = (1.0 - relay) * flag(is_main((here + 1) * span + half))
        blends[3, :, at] = jnp.broadcast_to(flag((here == 3) | ((here == 2) & jnp.logical_not(in_front))), (span, LANES))
        relay = flag((here == 2) & jnp.logical_not(in_front))
        blends[4, :, at] = jnp.broadcast_to(relay, (span, LANES))
        blends[5, :, at] = (1.0 - relay) * flag(is_main(past + half))
        blends[6, :, at] = jnp.broadcast_to(flag((here == 0) | ((here == 1) & in_front)), (span, LANES))

    rounded = filters[...].astype(bf16)
    a = lax.broadcasted_iota(jnp.int32, (taps, both), 0)
    b = lax.broadcasted_iota(jnp.int32, (taps, both), 1)
    for n, at in enumerate((span - b, span + both - b, span + b, b - span)):
        bases[n] = jnp.dot(rounded, flag(a == at).astype(bf16), preferred_element_type=f32)

    square_rows = lax.broadcasted_iota(jnp.int32, (both, both), 0)
    square_cols = lax.broadcasted_iota(jnp.int32, (both, both), 1)
    unwrapped = square_cols < both - square_rows

    def build(t, carry):
        for i in range(per_tile):
            g = pl.ds(t * per_tile + i, 1)
            at = pl.ds(i % 2 * both, both)
            for block, n in ((forward_block, 0), (backward_block, 2)):
                row = jnp.where(unwrapped, bases[n, g, :], bases[n + 1, g, :])
                block[t, i // 2, :, at] = pltpu.roll(row, 0, 1, stride=1, stride_axis=0).astype(bf16)
        return carry

    lax.fori_loop(0, tiles, build, 0)

    pairs = per_tile // 2
    wide = seqs * LANES
    lane = lax.rem(lax.broadcasted_iota(jnp.int32, (1, wide), 1), LANES) // members
    parity = [flag(lax.rem(lane, 2) == e).astype(bf16) for e in range(2)]
    pair_masks = [flag(lane // 2 == k).astype(bf16) for k in range(pairs)]
    blank = jnp.zeros((span, wide), bf16)

    def across(ref, j, at):
        return jnp.concatenate([ref[j, s, at, :] for s in range(seqs)], axis=1)

    def own_lanes(results, height):
        picked = results[:height]
        for k in range(1, pairs):
            picked = jnp.where(lane // 2 == k, results[k * height : (k + 1) * height], picked)
        return picked

    def apply(block, data):
        height = block.shape[1]
        results = jnp.dot(block.reshape(pairs * height, 2 * both), data, preferred_element_type=f32)
        return own_lanes(results, height)

    whole, low, top = pl.ds(0, both), pl.ds(0, span), pl.ds(span, span)

    def forward(j):
        at = pl.ds(pl.multiple_of(j * LANES, LANES), LANES)
        window = across(units, j, whole)
        held = window * wide_masks[0]
        other = window[span:] * half_masks[...]
        result = apply(forward_block[j], jnp.concatenate([held * p for p in parity], axis=0))
        rest = apply(
            forward_block[j, :, low, :],
            jnp.concatenate([blank, other * parity[0], blank, other * parity[1]], axis=0),
        )
        sent = (blends[1] * window[span:].astype(f32) + blends[2] * result[span:]).astype(bf16)
        filtered = jnp.where(blends[0] > 0.5, result[:span], rest) + blends[3] * window[:span].astype(f32)
        for s in range(seqs):
            mine_at = slice(s * LANES, (s + 1) * LANES)
            up_out[j, s] = sent[:, mine_at]
            gated_output[s, :, at] = (gate[s, :, at].astype(f32) * filtered[:, mine_at]).astype(bf16)
            gate_gradient[s, :, at] = (cotangent[s, :, at].astype(f32) * filtered[:, mine_at]).astype(bf16)

    def backward(j):
        at = pl.ds(pl.multiple_of(j * LANES, LANES), LANES)
        window = across(followers, j, whole)
        held = window * wide_masks[1]
        other = window[:span] * half_masks[...]
        result = apply(backward_block[j], jnp.concatenate([held * p for p in parity], axis=0))
        rest = apply(
            backward_block[j, :, top, :],
            jnp.concatenate([other * parity[0], blank, other * parity[1], blank], axis=0),
        )
        sent = (blends[4] * window[:span].astype(f32) + blends[5] * result[:span]).astype(bf16)
        adjoint = jnp.where(blends[0] > 0.5, result[span:], rest) + blends[6] * window[span:].astype(f32)
        for s in range(seqs):
            mine_at = slice(s * LANES, (s + 1) * LANES)
            down_out[j, s] = sent[:, mine_at]
            key_gradient[s, :, at] = (adjoint[:, mine_at] * value[s, :, at].astype(f32)).astype(bf16)
            value_gradient[s, :, at] = (adjoint[:, mine_at] * key[s, :, at].astype(f32)).astype(bf16)

    exchange = flag(square_rows + square_cols == both - 1).astype(bf16)
    wrapped = flag(square_cols < square_rows)

    def paired(j, outer=False):
        source = jnp.concatenate([blank, across(units, j, top)], axis=0) if outer else across(units, j, whole)
        reversed_units = jnp.dot(exchange, source, preferred_element_type=f32).astype(bf16)
        held = reversed_units * wide_masks[2]
        other = reversed_units * wide_masks[3]
        sources = jnp.concatenate(
            [jnp.concatenate([x * p for p in parity], axis=0) for x in (held, other)], axis=1
        )
        window = across(followers, j, low if outer else whole)
        held = window * (wide_masks[1, low, :] if outer else wide_masks[1])
        other = window[:span] * half_masks[...]

        def by_pair(x):
            repeat = x.shape[1] // wide
            return jnp.concatenate([x * jnp.concatenate([m] * repeat, axis=1) for m in pair_masks], axis=0)

        contract = (((1,), (1,)), ((), ()))
        own = lax.dot_general(
            by_pair(jnp.concatenate([held[:span], other], axis=1)), sources, contract, preferred_element_type=f32
        )
        if not outer:
            next_ones = lax.dot_general(by_pair(held[span:]), sources[:, :wide], contract, preferred_element_type=f32)
        for i in range(per_tile):
            at = slice(i // 2 * span, (i // 2 + 1) * span)
            across_at = slice(i % 2 * both, (i % 2 + 1) * both)
            near = pltpu.roll(own[at, across_at], 0, 1, stride=1, stride_axis=0)
            total, high = near, near * wrapped[:span]
            if not outer:
                far = pltpu.roll(next_ones[at, across_at], span, 1, stride=1, stride_axis=0)
                total, high = total + far, high + far * wrapped[span:]
            total = jnp.sum(total, axis=0, keepdims=True)
            high = jnp.sum(high, axis=0, keepdims=True)
            tap_sums[j, pl.ds(i, 1), pl.ds(0, both)] = total - high
            tap_sums[j, pl.ds(i, 1), pl.ds(both, both)] = high

    def up_wait(j):
        @pl.when(jnp.logical_not(first))
        def _():
            up_copy(j).wait_recv()

    def down_wait(j):
        @pl.when(jnp.logical_not(last))
        def _():
            down_copy(j).wait_recv()

    def up_start(j):
        @pl.when(hub)
        def _():
            up_copy(j).start()

    def down_start(j):
        @pl.when(hub)
        def _():
            down_copy(j).start()

    def sweep(near, far):
        near_wait, near_math, near_start = near
        far_wait, far_math, far_start = far

        def batch_of(n):
            return [n * TOGETHER + k for k in range(TOGETHER)]

        def enter(n, carry):
            for act in near:
                for j in batch_of(n):
                    act(j)
            return carry

        def step(n, carry):
            for j in batch_of(n):
                near_wait(j + AHEAD * TOGETHER)
                far_wait(j)
            for j in batch_of(n):
                near_math(j + AHEAD * TOGETHER)
                far_math(j)
                paired(j)
            for j in batch_of(n):
                near_start(j + AHEAD * TOGETHER)
                far_start(j)
            return carry

        def leave(n, carry):
            for j in batch_of(n):
                far_wait(j)
            for j in batch_of(n):
                far_math(j)
                paired(j)
            for j in batch_of(n):
                far_start(j)
            return carry

        steps = tiles // TOGETHER
        lax.fori_loop(0, AHEAD, enter, 0)
        lax.fori_loop(0, steps - AHEAD, step, 0)
        lax.fori_loop(steps - AHEAD, steps, leave, 0)

    a = lax.broadcasted_iota(jnp.int32, (taps, 2 * both), 0)
    b = lax.broadcasted_iota(jnp.int32, (taps, 2 * both), 1)
    pick = flag(((a == b - (span - 1)) & (b < both)) | ((a == b - both + span + 1) & (b >= both)))
    share = taps // sharers

    def share_copy(z, n):
        return pltpu.make_async_remote_copy(
            src_ref=shares_out.at[z * n_batch + n], dst_ref=shares_in.at[mine],
            send_sem=share_send.at[z * n_batch + n], recv_sem=share_recv.at[mine],
            device_id={"seq": z, "batch": n}, device_id_type=MESH,
        )

    def share_arrival(z, n):
        at = z * n_batch + n
        return pltpu.make_async_remote_copy(
            src_ref=shares_out.at[at], dst_ref=shares_in.at[at], send_sem=share_send.at[at],
            recv_sem=share_recv.at[at], device_id={"seq": z, "batch": n}, device_id_type=MESH,
        )

    def square_copy(z, n):
        return pltpu.make_async_remote_copy(
            src_ref=squares_out, dst_ref=squares_in.at[mine],
            send_sem=square_send.at[z * n_batch + n], recv_sem=square_recv.at[mine],
            device_id={"seq": z, "batch": n}, device_id_type=MESH,
        )

    def square_arrival(z, n):
        at = z * n_batch + n
        return pltpu.make_async_remote_copy(
            src_ref=squares_out, dst_ref=squares_in.at[at], send_sem=square_send.at[at],
            recv_sem=square_recv.at[at], device_id={"seq": z, "batch": n}, device_id_type=MESH,
        )

    def others(act, low, high, allowed):
        for z in range(low, high):
            for n in range(n_batch):
                @pl.when(allowed(z) & (mine != z * n_batch + n))
                def _():
                    act(z, n)

    def shares_to(z):
        return hub if z > 0 else hub | first | last

    def shares_from(z):
        return (first | hub) & (here < n_seq - 1) if 0 < z < n_seq - 1 else first

    def send_shares():
        by_tap = lax.dot_general(
            pick, tap_sums[...].reshape(groups, 2 * both), (((1,), (1,)), ((), ())),
            precision=lax.Precision.HIGHEST, preferred_element_type=f32,
        )
        for i in range(sharers):
            shares_out[i] = by_tap[i * share : (i + 1) * share, :]
        others(lambda z, n: share_copy(z, n).start(), 0, n_seq - 1, shares_to)

    def alone(near, far):
        near_wait, near_math, near_start = near
        far_wait, far_math, far_start = far

        def local(n, carry):
            for k in range(TOGETHER):
                near_math(n * TOGETHER + k)
                paired(n * TOGETHER + k, outer=True)
            return carry

        def finish(n, carry):
            for k in range(TOGETHER):
                far_wait(n * TOGETHER + k)
            for k in range(TOGETHER):
                far_math(n * TOGETHER + k)
            return carry

        lax.fori_loop(0, tiles // TOGETHER, local, 0)
        send_shares()
        lax.fori_loop(0, tiles // TOGETHER, finish, 0)

    up_stage = (up_wait, forward, up_start)
    down_stage = (down_wait, backward, down_start)

    @pl.when(first)
    def _():
        alone(up_stage, down_stage)

    @pl.when(last)
    def _():
        alone(down_stage, up_stage)

    @pl.when(here == 1)
    def _():
        sweep(up_stage, down_stage)
        send_shares()

    @pl.when(here == 2)
    def _():
        sweep(down_stage, up_stage)
        send_shares()

    def chan_copy(i):
        return pltpu.make_async_remote_copy(
            src_ref=chan_out, dst_ref=chan_in.at[i - 1],
            send_sem=chan_send.at[i - 1], recv_sem=chan_recv.at[i - 1],
            device_id={"chan": lax.rem(chan + i, n_chan)}, device_id_type=MESH,
        )

    others(lambda z, n: share_arrival(z, n).wait_recv(), 0, n_seq, shares_from)
    total = shares_out[mine] + jnp.sum(shares_in[...], axis=0)
    squares_out[...] = jnp.sum(total * total, axis=0, keepdims=True)
    squared = jnp.logical_not(last)
    others(lambda z, n: square_copy(z, n).start(), 0, n_seq, lambda z: squared)
    others(lambda z, n: square_arrival(z, n).wait_recv(), 0, n_seq - 1, lambda z: here >= 0)
    chan_out[...] = jnp.sum(squares_in[...], axis=0) + squares_out[...]
    for i in range(1, n_chan):
        chan_copy(i).start()
    for i in range(1, n_chan):
        chan_copy(i).wait_recv()
    squares = jnp.sum(chan_in[...], axis=0) + chan_out[...]
    mean = jnp.sum(squares, axis=1, keepdims=True) / (taps * groups * n_chan)
    filter_update[...] = total * jnp.minimum(1.0, 1.0 / jnp.sqrt(mean + 1e-06))

    others(lambda z, n: share_copy(z, n).wait_send(), 0, n_seq - 1, shares_to)
    others(lambda z, n: square_copy(z, n).wait_send(), 0, n_seq, lambda z: squared)
    for i in range(1, n_chan):
        chan_copy(i).wait_send()

    def drain(copy):
        def step(j, carry):
            copy(j).wait_send()
            return carry

        lax.fori_loop(0, tiles, step, 0)

    @pl.when(here + 1 < n_seq)
    def _():
        drain(up_copy)

    @pl.when(here >= 1)
    def _():
        drain(down_copy)


def store_kernel(count, *refs):
    sources, targets, sems = refs[:count], refs[count : 2 * count], refs[2 * count]
    copies = [pltpu.make_async_copy(sources[n], targets[n], sems.at[n]) for n in range(count)]
    for copy in copies:
        copy.start()
    for copy in copies:
        copy.wait()


def hub_device(sizes, gate_input, key_input, value_input, cotangent, filters, document_lengths):
    n_seq, n_batch, n_chan = sizes
    seqs, span, width = gate_input.shape
    groups, taps = filters.shape
    tiles = width // LANES
    sharers = n_seq * n_batch
    share = taps // sharers
    both = 2 * span
    per_tile = groups // tiles
    dims = (n_seq, n_batch, n_chan, tiles, seqs, span, groups, taps)
    bf16, f32 = jnp.bfloat16, jnp.float32
    vmem, anywhere = pl.BlockSpec(memory_space=pltpu.VMEM), pl.BlockSpec(memory_space=pl.ANY)
    dma = pltpu.SemaphoreType.DMA
    shape = gate_input.shape
    results = pl.pallas_call(
        functools.partial(hub_kernel, dims),
        out_shape=(pltpu.VMEM(shape, bf16),) * 4 + (pltpu.VMEM((share, groups), f32),),
        in_specs=[pl.BlockSpec(memory_space=pltpu.HBM)] * 6,
        out_specs=(vmem,) * 5,
        scratch_shapes=[
            pltpu.VMEM(shape, bf16), pltpu.VMEM(shape, bf16), pltpu.VMEM(shape, bf16), pltpu.VMEM(shape, bf16),
            pltpu.VMEM((groups, taps), f32), pltpu.SMEM(document_lengths.shape, jnp.int32),
            pltpu.VMEM((tiles, seqs, both, LANES), bf16),
            pltpu.VMEM((tiles, seqs, both, LANES), bf16),
            pltpu.VMEM((tiles, seqs, span, LANES), bf16),
            pltpu.VMEM((tiles, seqs, span, LANES), bf16),
            pltpu.VMEM((tiles, per_tile // 2, both, 2 * both), bf16),
            pltpu.VMEM((tiles, per_tile // 2, both, 2 * both), bf16),
            pltpu.VMEM((4, groups, both), f32),
            pltpu.VMEM((4, both, seqs * LANES), bf16),
            pltpu.VMEM((span, seqs * LANES), bf16),
            pltpu.VMEM((7, span, seqs * LANES), f32),
            pltpu.VMEM((tiles, per_tile, 2 * both), f32),
            pltpu.VMEM((sharers, share, groups), f32),
            pltpu.VMEM((sharers, share, groups), f32),
            pltpu.VMEM((1, groups), f32),
            pltpu.VMEM((sharers, 1, groups), f32),
            pltpu.VMEM((1, groups), f32),
            pltpu.VMEM((n_chan - 1, 1, groups), f32),
            dma((LOADS, 4)), dma((2,)),
            dma((tiles,)), dma((tiles,)), dma((tiles,)), dma((tiles,)),
            dma((sharers,)), dma((sharers,)), dma((sharers,)), dma((sharers,)),
            dma((n_chan - 1,)), dma((n_chan - 1,)),
        ],
        compiler_params=pltpu.CompilerParams(
            collective_id=0, has_side_effects=True, vmem_limit_bytes=40 * 1024 * 1024
        ),
    )(*[
        pltpu.with_memory_space_constraint(x, pltpu.HBM)
        for x in (gate_input, key_input, value_input, cotangent, filters, document_lengths)
    ])
    like = jax.ShapeDtypeStruct(shape, bf16)
    return pl.pallas_call(
        functools.partial(store_kernel, 5),
        out_shape=(like, like, like, like, jax.ShapeDtypeStruct((share, groups), f32)),
        in_specs=[vmem] * 5,
        out_specs=(anywhere,) * 5,
        scratch_shapes=[dma((5,))],
    )(*[pltpu.with_memory_space_constraint(x, pltpu.VMEM) for x in results])


def per_device(sizes, gate_input, key_input, value_input, cotangent, filters, document_lengths):
    n_seq = sizes[0]
    span, width = gate_input.shape[1:]
    groups, taps = filters.shape
    two = document_lengths.shape[1] == 2 and n_seq == 4 and taps == n_seq * span and taps % (n_seq * sizes[1]) == 0
    if two and 2 * span == LANES and (width // LANES) % LOADS == 0:
        device = hub_device
    else:
        device = wide_device
    return device(sizes, gate_input, key_input, value_input, cotangent, filters, document_lengths)


def solution(mesh):
    block = P("batch", "seq", "chan")
    sizes = (mesh.shape["seq"], mesh.shape["batch"], mesh.shape["chan"])
    return jax.shard_map(
        functools.partial(per_device, sizes),
        mesh=mesh,
        in_specs=(block, block, block, block, P("chan", None), P("batch", None)),
        out_specs=(block, block, block, block, P(("seq", "batch"), "chan")),
        check_vma=False,
    )
```

```python
import functools

import jax
import jax.numpy as jnp
from jax import lax
from jax.experimental import pallas as pl
from jax.experimental.pallas import tpu as pltpu
from jax.sharding import PartitionSpec as P

MESH = pl.DeviceIdType.MESH
LANES = 128
HELD = 4
SHARES_AT = 4


def kernel(
    dims, gate, key, value, cotangent, filters, lengths,
    gated_output, gate_gradient, key_gradient, value_gradient, filter_update,
    units, followers, reversed_own, plain, flipped, forward_block, backward_block,
    forward_mask, backward_mask, sums_mask, tap_sums, shares_out, shares_in, squares_out, squares_in,
    chan_out, chan_in,
    unit_send, unit_recv, cot_send, cot_recv, share_send, share_recv, square_send, square_recv,
    chan_send, chan_recv,
):
    n_seq, n_batch, n_chan, reach, wide, chunks, tiles, seqs, span, groups, taps, ndocs = dims
    everyone = n_seq * n_batch * n_chan
    sharers = n_seq * n_batch
    here = lax.axis_index("seq")
    batch = lax.axis_index("batch")
    chan = lax.axis_index("chan")
    me = (here * n_batch + batch) * n_chan + chan
    mine = here * n_batch + batch
    per_tile = LANES * groups // (tiles * chunks * LANES)
    members = LANES // per_tile
    lanes = tiles * LANES
    own = reach * span
    hub = reach == 2

    barrier = pltpu.get_barrier_semaphore()

    rest = wide - own - span
    for c in range(chunks):
        for s in range(seqs):
            units[c, s, pl.ds(0, own), :] = jnp.zeros((own, lanes), jnp.bfloat16)
            units[c, s, pl.ds(own + span, rest), :] = jnp.zeros((rest, lanes), jnp.bfloat16)
            followers[c, s, pl.ds(span, wide - span), :] = jnp.zeros((wide - span, lanes), jnp.bfloat16)

    def greet(i, carry):
        other = lax.rem(me + i, everyone)
        pl.semaphore_signal(
            barrier, inc=1, device_id_type=MESH,
            device_id={
                "seq": other // (n_batch * n_chan),
                "batch": lax.rem(other // n_chan, n_batch),
                "chan": lax.rem(other, n_chan),
            },
        )
        return carry

    lax.fori_loop(1, everyone, greet, 0)

    for c in range(chunks):
        at = pl.ds(c * lanes, lanes)
        for s in range(seqs):
            u = (key[s, :, at].astype(jnp.float32) * value[s, :, at].astype(jnp.float32)).astype(jnp.bfloat16)
            g = (cotangent[s, :, at].astype(jnp.float32) * gate[s, :, at].astype(jnp.float32)).astype(jnp.bfloat16)
            units[c, s, pl.ds(own, span), :] = u
            followers[c, s, pl.ds(0, span), :] = g

    def unit_copy(lag, c):
        source = units.at[c, :, pl.ds((reach - lag + 1) * span, span), :]
        target = units.at[c, :, pl.ds((reach - lag) * span, span), :]
        return pltpu.make_async_remote_copy(
            src_ref=source, dst_ref=target, send_sem=unit_send.at[lag - 1, c], recv_sem=unit_recv.at[lag - 1, c],
            device_id={"seq": here + 1}, device_id_type=MESH,
        )

    def cot_copy(lag, c):
        source = followers.at[c, :, pl.ds((lag - 1) * span, span), :]
        target = followers.at[c, :, pl.ds(lag * span, span), :]
        return pltpu.make_async_remote_copy(
            src_ref=source, dst_ref=target, send_sem=cot_send.at[lag - 1, c], recv_sem=cot_recv.at[lag - 1, c],
            device_id={"seq": here - 1}, device_id_type=MESH,
        )

    def sends_up(lag):
        return (here >= lag - 1) & (here + 1 < n_seq)

    def sends_down(lag):
        return (here + lag - 1 < n_seq) & (here >= 1)

    def send(lag, c):
        @pl.when(sends_up(lag))
        def _():
            unit_copy(lag, c).start()

        @pl.when(sends_down(lag))
        def _():
            cot_copy(lag, c).start()

    def receive(lag, c):
        @pl.when(here >= lag)
        def _():
            unit_copy(lag, c).wait_recv()

        @pl.when(here + lag < n_seq)
        def _():
            cot_copy(lag, c).wait_recv()

    pl.semaphore_wait(barrier, everyone - 1)
    for c in range(chunks):
        send(1, c)

    def documents(positions, s):
        count = jnp.zeros(positions.shape, jnp.int32)
        end = 0
        for n in range(ndocs):
            end = end + lengths[s, n]
            count = count + (positions >= end).astype(jnp.int32)
        return count

    rows = lax.broadcasted_iota(jnp.int32, (span, 1), 0)
    cols = lax.broadcasted_iota(jnp.int32, (1, wide), 1)
    for s in range(seqs):
        earlier = (here - reach) * span + cols
        later = here * span + cols
        target = here * span + rows
        back = here * span + (span - 1 - rows)
        earlier_doc = documents(earlier, s)
        later_doc = documents(later, s)
        target_doc = documents(target, s)
        back_doc = documents(back, s)
        keep = (earlier_doc == target_doc) & (earlier <= target) & (earlier >= 0)
        forward_mask[s] = jnp.where(keep, 1.0, 0.0).astype(jnp.bfloat16)
        if hub:
            first = cols < span
            origin = jnp.where(first, earlier + span, earlier)
            goal = jnp.where(first, back + span, back)
            goal_doc = jnp.where(first, documents(back + span, s), back_doc)
            keep = (documents(origin, s) == goal_doc) & (origin <= goal) & (origin >= 0) & (goal < n_seq * span)
        else:
            keep = (earlier_doc == back_doc) & (earlier <= back) & (earlier >= 0)
        sums_mask[s] = jnp.where(keep, 1.0, 0.0)
        keep = (later_doc == target_doc) & (later >= target) & (later < n_seq * span)
        backward_mask[s] = jnp.where(keep, 1.0, 0.0).astype(jnp.bfloat16)

    rounded = filters[...].astype(jnp.bfloat16)
    a = lax.broadcasted_iota(jnp.int32, (taps, wide), 0)
    b = lax.broadcasted_iota(jnp.int32, (taps, wide), 1)
    flip = own - b
    flip = jnp.where(flip < 0, flip + wide, flip)
    plain[...] = jnp.dot(rounded, jnp.where(a == b, 1.0, 0.0).astype(jnp.bfloat16), preferred_element_type=jnp.float32)
    flipped[...] = jnp.dot(rounded, jnp.where(a == flip, 1.0, 0.0).astype(jnp.bfloat16), preferred_element_type=jnp.float32)

    def build(t, carry):
        for i in range(per_tile):
            g = t * per_tile + i
            at = pl.ds(pl.multiple_of(g * span, span), span)
            row = jnp.broadcast_to(flipped[pl.ds(g, 1), :], (span, wide))
            forward_block[at, :] = pltpu.roll(row, 0, 1, stride=1, stride_axis=0).astype(jnp.bfloat16)
            row = jnp.broadcast_to(plain[pl.ds(g, 1), :], (span, wide))
            backward_block[at, :] = pltpu.roll(row, 0, 1, stride=1, stride_axis=0).astype(jnp.bfloat16)
        return carry

    order_a = lax.broadcasted_iota(jnp.int32, (span, span), 0)
    order_b = lax.broadcasted_iota(jnp.int32, (span, span), 1)
    exchange = jnp.where(order_a + order_b == span - 1, 1.0, 0.0).astype(jnp.bfloat16)
    lane = lax.broadcasted_iota(jnp.int32, (1, LANES), 1) // members

    def members_apart(block):
        return jnp.concatenate(
            [block * jnp.where(lane == i, 1.0, 0.0).astype(jnp.bfloat16) for i in range(per_tile)], axis=0
        )

    def paired(c, j, carry):
        at = pl.ds(pl.multiple_of(j * LANES, LANES), LANES)
        total = None
        for s in range(seqs):
            target = members_apart(reversed_own[c, s, pl.ds(0, span), at])
            if hub:
                target = jnp.concatenate([target, members_apart(reversed_own[c, s, pl.ds(span, span), at])], axis=1)
                past = units[c, s, pl.ds(own - span, span), at]
                blank = jnp.zeros((span, LANES), jnp.bfloat16)
                tail = jnp.zeros((wide - own - span, LANES), jnp.bfloat16)
                source = jnp.concatenate(
                    [
                        jnp.concatenate([blank, past, units[c, s, pl.ds(own, span), at], tail], axis=0),
                        jnp.concatenate([past, blank, blank, tail], axis=0),
                    ],
                    axis=1,
                )
            else:
                source = units[c, s, :, at]
            products = lax.dot_general(
                target, source, (((1,), (1,)), ((), ())), preferred_element_type=jnp.float32
            ).reshape(per_tile, span, wide)
            products = products * sums_mask[s][None]
            total = products if total is None else total + products
        for i in range(per_tile):
            aligned = pltpu.roll(total[i], 0, 1, stride=1, stride_axis=0)
            tap_sums[pl.ds((c * tiles + j) * per_tile + i, 1), :] = jnp.sum(aligned, axis=0, keepdims=True)
        return carry

    def reverse(c):
        for s in range(seqs):
            for n in range(2 if hub else 1):
                at = pl.ds(n * span, span)
                reversed_own[c, s, at, :] = jnp.dot(
                    exchange, followers[c, s, at, :], preferred_element_type=jnp.float32
                ).astype(jnp.bfloat16)

    for c in range(chunks):
        lax.fori_loop(c * tiles, (c + 1) * tiles, build, 0)
        for lag in range(1, reach):
            receive(lag, c)
            if not (hub and c >= HELD):
                send(lag + 1, c)
        if hub:
            reverse(c)
            lax.fori_loop(0, tiles, functools.partial(paired, c), 0)
    if not hub:
        for c in range(chunks):
            receive(reach, c)
            reverse(c)
            lax.fori_loop(0, tiles, functools.partial(paired, c), 0)

    a = lax.broadcasted_iota(jnp.int32, (taps, wide), 0)
    b = lax.broadcasted_iota(jnp.int32, (taps, wide), 1)
    pick = jnp.where(a + b == own + span - 1, 1.0, 0.0)
    by_tap = lax.dot_general(
        pick, tap_sums[...], (((1,), (1,)), ((), ())),
        precision=lax.Precision.HIGHEST, preferred_element_type=jnp.float32,
    )
    share = taps // sharers
    for i in range(sharers):
        shares_out[i] = by_tap[i * share : (i + 1) * share, :]

    def share_copy(i):
        other = lax.rem(mine + i, sharers)
        return pltpu.make_async_remote_copy(
            src_ref=shares_out.at[other], dst_ref=shares_in.at[i - 1],
            send_sem=share_send.at[i - 1], recv_sem=share_recv.at[i - 1],
            device_id={"seq": other // n_batch, "batch": lax.rem(other, n_batch)}, device_id_type=MESH,
        )

    def square_copy(i):
        other = lax.rem(mine + i, sharers)
        return pltpu.make_async_remote_copy(
            src_ref=squares_out, dst_ref=squares_in.at[i - 1],
            send_sem=square_send.at[i - 1], recv_sem=square_recv.at[i - 1],
            device_id={"seq": other // n_batch, "batch": lax.rem(other, n_batch)}, device_id_type=MESH,
        )

    def chan_copy(i):
        return pltpu.make_async_remote_copy(
            src_ref=chan_out, dst_ref=chan_in.at[i - 1],
            send_sem=chan_send.at[i - 1], recv_sem=chan_recv.at[i - 1],
            device_id={"chan": lax.rem(chan + i, n_chan)}, device_id_type=MESH,
        )

    def loop(low, high, act):
        if high <= 32:
            for i in range(low, high):
                act(i)
            return

        def step(i, carry):
            act(i)
            return carry

        lax.fori_loop(low, high, step, 0)

    def convolve(c, j, carry):
        at = pl.ds(pl.multiple_of(j * LANES, LANES), LANES)
        t = c * tiles + j
        out = pl.ds(pl.multiple_of(t * LANES, LANES), LANES)
        height = per_tile * span
        block = pl.ds(pl.multiple_of(t * height, height), height)

        def apply(block_ref, mask_ref, data_ref, s):
            masked = block_ref[block, :].reshape(per_tile, span, wide) * mask_ref[s][None]
            results = jnp.dot(
                masked.reshape(height, wide), data_ref[c, s, :, at], preferred_element_type=jnp.float32
            )
            picked = results[:span]
            for i in range(1, per_tile):
                picked = jnp.where(lane == i, results[i * span : (i + 1) * span], picked)
            return picked

        for s in range(seqs):
            filtered = apply(forward_block, forward_mask, units, s)
            gated_output[s, :, out] = (gate[s, :, out].astype(jnp.float32) * filtered).astype(jnp.bfloat16)
            gate_gradient[s, :, out] = (cotangent[s, :, out].astype(jnp.float32) * filtered).astype(jnp.bfloat16)
            adjoint = apply(backward_block, backward_mask, followers, s)
            key_gradient[s, :, out] = (adjoint * value[s, :, out].astype(jnp.float32)).astype(jnp.bfloat16)
            value_gradient[s, :, out] = (adjoint * key[s, :, out].astype(jnp.float32)).astype(jnp.bfloat16)
        return carry

    loop(1, sharers, lambda i: share_copy(i).start())
    if hub:
        for c in range(HELD, chunks):
            send(reach, c)
    for c in range(chunks):
        if hub:
            receive(reach, c)
        if c == SHARES_AT:
            loop(1, sharers, lambda i: share_copy(i).wait_recv())
            total = shares_out[mine] + jnp.sum(shares_in[...], axis=0)
            filter_update[...] = total
            squares_out[...] = jnp.sum(total * total, axis=0, keepdims=True)
        if c == SHARES_AT + 1:
            loop(1, sharers, lambda i: square_copy(i).start())
        lax.fori_loop(0, tiles, functools.partial(convolve, c), 0)
    loop(1, sharers, lambda i: square_copy(i).wait_recv())
    chan_out[...] = jnp.sum(squares_in[...], axis=0) + squares_out[...]
    loop(1, sharers, lambda i: share_copy(i).wait_send())
    loop(1, sharers, lambda i: square_copy(i).wait_send())
    loop(1, n_chan, lambda i: chan_copy(i).start())
    loop(1, n_chan, lambda i: chan_copy(i).wait_recv())
    squares = jnp.sum(chan_in[...], axis=0) + chan_out[...]
    mean = jnp.sum(squares, axis=1, keepdims=True) / (taps * groups * n_chan)
    filter_update[...] = filter_update[...] * jnp.minimum(1.0, 1.0 / jnp.sqrt(mean + 1e-06))
    loop(1, n_chan, lambda i: chan_copy(i).wait_send())
    for lag in range(1, reach + 1):
        @pl.when(sends_up(lag))
        def _():
            for c in range(chunks):
                unit_copy(lag, c).wait_send()

        @pl.when(sends_down(lag))
        def _():
            for c in range(chunks):
                cot_copy(lag, c).wait_send()


def wide_device(sizes, gate_input, key_input, value_input, cotangent, filters, document_lengths):
    n_seq, n_batch, n_chan = sizes
    seqs, span, width = gate_input.shape
    groups, taps = filters.shape
    ndocs = document_lengths.shape[1]
    longest = min(taps, n_seq * span - span)
    reach = (longest - 1) // span if ndocs == 2 else (longest - 2) // span + 1
    wide = -(-((reach + 2) * span - 1) // LANES) * LANES
    chunks = 8
    tiles = width // (chunks * LANES)
    lanes = tiles * LANES
    sharers = n_seq * n_batch
    share = taps // sharers
    dims = (n_seq, n_batch, n_chan, reach, wide, chunks, tiles, seqs, span, groups, taps, ndocs)
    bf16, f32 = jnp.bfloat16, jnp.float32
    vmem = pl.BlockSpec(memory_space=pltpu.VMEM)
    dma = pltpu.SemaphoreType.DMA
    like = jax.ShapeDtypeStruct(gate_input.shape, bf16)
    return pl.pallas_call(
        functools.partial(kernel, dims),
        out_shape=(like, like, like, like, jax.ShapeDtypeStruct((share, groups), f32)),
        in_specs=[vmem] * 5 + [pl.BlockSpec(memory_space=pltpu.SMEM)],
        out_specs=(vmem,) * 5,
        scratch_shapes=[
            pltpu.VMEM((chunks, seqs, wide, lanes), bf16),
            pltpu.VMEM((chunks, seqs, wide, lanes), bf16),
            pltpu.VMEM((chunks, seqs, 2 * span, lanes), bf16),
            pltpu.VMEM((groups, wide), f32),
            pltpu.VMEM((groups, wide), f32),
            pltpu.VMEM((groups * span, wide), bf16),
            pltpu.VMEM((groups * span, wide), bf16),
            pltpu.VMEM((seqs, span, wide), bf16),
            pltpu.VMEM((seqs, span, wide), bf16),
            pltpu.VMEM((seqs, span, wide), f32),
            pltpu.VMEM((groups, wide), f32),
            pltpu.VMEM((sharers, share, groups), f32),
            pltpu.VMEM((sharers - 1, share, groups), f32),
            pltpu.VMEM((1, groups), f32),
            pltpu.VMEM((sharers - 1, 1, groups), f32),
            pltpu.VMEM((1, groups), f32),
            pltpu.VMEM((n_chan - 1, 1, groups), f32),
            dma((reach, chunks)), dma((reach, chunks)), dma((reach, chunks)), dma((reach, chunks)),
            dma((sharers - 1,)), dma((sharers - 1,)), dma((sharers - 1,)), dma((sharers - 1,)),
            dma((n_chan - 1,)), dma((n_chan - 1,)),
        ],
        compiler_params=pltpu.CompilerParams(
            collective_id=0, has_side_effects=True, vmem_limit_bytes=60 * 1024 * 1024
        ),
    )(gate_input, key_input, value_input, cotangent, filters, document_lengths)


AHEAD = 3
TOGETHER = 2
LOADS = 8
EARLY = 4


def hub_kernel(
    dims, gate_hbm, key_hbm, value_hbm, cotangent_hbm, filters_hbm, lengths_hbm,
    gated_output, gate_gradient, key_gradient, value_gradient, filter_update,
    gate, key, value, cotangent, filters, lengths, units, followers, up_out, down_out,
    forward_block, backward_block, bases, wide_masks, half_masks, blends, tap_sums, kept, late_in,
    shares_out, shares_in, squares_out, squares_in, chan_out, chan_in,
    load_sem, small_sem, up_send, up_recv, down_send, down_recv, late_send, late_recv, share_send, share_recv, square_send, square_recv,
    chan_send, chan_recv, up_call, down_call,
):
    n_seq, n_batch, n_chan, tiles, seqs, span, groups, taps = dims
    sharers = n_seq * n_batch
    here = lax.axis_index("seq")
    batch = lax.axis_index("batch")
    chan = lax.axis_index("chan")
    mine = here * n_batch + batch
    per_tile = groups // tiles
    members = LANES // per_tile
    both = 2 * span
    f32, bf16 = jnp.float32, jnp.bfloat16

    part = tiles // LOADS * LANES

    def loads(q):
        at = pl.ds(q * part, part)
        pairs = ((key_hbm, key), (value_hbm, value), (cotangent_hbm, cotangent), (gate_hbm, gate))
        return [
            pltpu.make_async_copy(src.at[:, :, at], dst.at[:, :, at], load_sem.at[q, n])
            for n, (src, dst) in enumerate(pairs)
        ]

    for q in range(LOADS):
        for copy in loads(q):
            copy.start()

    filters_copy = pltpu.make_async_copy(filters_hbm, filters, small_sem.at[0])
    lengths_copy = pltpu.make_async_copy(lengths_hbm, lengths, small_sem.at[1])
    lengths_copy.start()
    filters_copy.start()
    shares_in[...] = jnp.zeros(shares_in.shape, f32)
    squares_in[...] = jnp.zeros(squares_in.shape, f32)

    first, last = here == 0, here == n_seq - 1
    barrier = pltpu.get_barrier_semaphore()

    def greet(device):
        pl.semaphore_signal(barrier, inc=1, device_id_type=MESH, device_id=device)

    @pl.when(jnp.logical_not(first))
    def _():
        greet({"seq": here - 1})

    @pl.when(jnp.logical_not(last))
    def _():
        greet({"seq": here + 1})

    for i in range(1, n_batch):
        greet({"batch": lax.rem(batch + i, n_batch)})
    for i in range(1, n_chan):
        greet({"chan": lax.rem(chan + i, n_chan)})
    greeted = n_batch - 1 + n_chan - 1 + jnp.where(first | last, 1, 2)

    def call(semaphore, target):
        pl.semaphore_signal(semaphore, inc=1, device_id_type=MESH, device_id={"seq": target})

    def open_calls():
        @pl.when(first)
        def _():
            call(up_call, here + 1)

        @pl.when(last)
        def _():
            call(down_call, here - 1)

    def pass_calls():
        pl.semaphore_wait(up_call, 1)
        call(up_call, here + 1)
        pl.semaphore_wait(down_call, 1)
        call(down_call, here - 1)

    def close_calls():
        @pl.when(first)
        def _():
            pl.semaphore_wait(down_call, 1)

        @pl.when(last)
        def _():
            pl.semaphore_wait(up_call, 1)

    hub = jnp.logical_not(first | last)
    own_units = units.at[:, :, pl.ds(span, span), :]
    own_cots = followers.at[:, :, pl.ds(0, span), :]

    def up_copy(j, source=up_out):
        return pltpu.make_async_remote_copy(
            src_ref=source.at[j], dst_ref=units.at[j, :, pl.ds(0, span), :],
            send_sem=up_send.at[j], recv_sem=up_recv.at[j], device_id={"seq": here + 1}, device_id_type=MESH,
        )

    def down_copy(j, source=down_out):
        return pltpu.make_async_remote_copy(
            src_ref=source.at[j], dst_ref=followers.at[j, :, pl.ds(span, span), :],
            send_sem=down_send.at[j], recv_sem=down_recv.at[j], device_id={"seq": here - 1}, device_id_type=MESH,
        )

    held_back = tiles - EARLY

    def late_copy(k):
        return pltpu.make_async_remote_copy(
            src_ref=down_out.at[held_back + k], dst_ref=late_in.at[k],
            send_sem=late_send.at[k], recv_sem=late_recv.at[k], device_id={"seq": here - 1}, device_id_type=MESH,
        )

    def gather(j, carry):
        at = pl.ds(pl.multiple_of(j * LANES, LANES), LANES)
        for s in range(seqs):
            u = (key[s, :, at].astype(f32) * value[s, :, at].astype(f32)).astype(bf16)
            g = (cotangent[s, :, at].astype(f32) * gate[s, :, at].astype(f32)).astype(bf16)
            units[j, s, pl.ds(span, span), :] = u
            followers[j, s, pl.ds(0, span), :] = g

        @pl.when(first)
        def _():
            up_copy(j, own_units).start()
            for s in range(seqs):
                units[j, s, pl.ds(0, span), :] = jnp.zeros((span, LANES), bf16)

        @pl.when(last)
        def _():
            down_copy(j, own_cots).start()
            for s in range(seqs):
                followers[j, s, pl.ds(span, span), :] = jnp.zeros((span, LANES), bf16)

        @pl.when((here == 2) & (j >= held_back))
        def _():
            down_copy(j, own_cots).start()

        return carry

    for q in range(LOADS):
        for copy in loads(q):
            copy.wait()
        if q == 0:
            pl.semaphore_wait(barrier, greeted)
            open_calls()
        lax.fori_loop(q * (tiles // LOADS), (q + 1) * (tiles // LOADS), gather, 0)

    lengths_copy.wait()
    filters_copy.wait()

    main = jnp.where(here * 2 >= n_seq, 1, 0)
    rows = lax.broadcasted_iota(jnp.int32, (both, LANES), 0)
    half = lax.broadcasted_iota(jnp.int32, (span, LANES), 0)
    one, zero = jnp.ones((), f32), jnp.zeros((), f32)

    def flag(condition):
        return jnp.where(condition, one, zero)

    for s in range(seqs):
        end = lengths[s, 0]
        at = pl.ds(s * LANES, LANES)

        def is_main(positions):
            return jnp.where(positions >= end, 1, 0) == main

        in_front = end <= both
        past_held = (here == 1) | ((here == 2) & in_front)
        next_held = (here == 2) | ((here == 1) & jnp.logical_not(in_front))
        past = (here - 1) * span
        own_main = is_main(here * span + half)
        back = both - 1 - rows
        wide_masks[0, :, at] = flag(is_main(past + rows) & ((rows >= span) | past_held)).astype(bf16)
        wide_masks[1, :, at] = flag(is_main(here * span + rows) & ((rows < span) | next_held)).astype(bf16)
        wide_masks[2, :, at] = flag(is_main(past + back) & ((back >= span) | past_held)).astype(bf16)
        wide_masks[3, :, at] = flag(jnp.logical_not(is_main(past + back)) & (back >= span)).astype(bf16)
        half_masks[:, at] = flag(jnp.logical_not(own_main)).astype(bf16)
        relay = flag((here == 1) & in_front)
        blends[0, :, at] = flag(own_main)
        blends[1, :, at] = jnp.broadcast_to(relay, (span, LANES))
        blends[2, :, at] = (1.0 - relay) * flag(is_main((here + 1) * span + half))
        blends[3, :, at] = jnp.broadcast_to(flag((here == 3) | ((here == 2) & jnp.logical_not(in_front))), (span, LANES))
        relay = flag((here == 2) & jnp.logical_not(in_front))
        blends[4, :, at] = jnp.broadcast_to(relay, (span, LANES))
        blends[5, :, at] = (1.0 - relay) * flag(is_main(past + half))
        blends[6, :, at] = jnp.broadcast_to(flag((here == 0) | ((here == 1) & in_front)), (span, LANES))

    rounded = filters[...].astype(bf16)
    a = lax.broadcasted_iota(jnp.int32, (taps, both), 0)
    b = lax.broadcasted_iota(jnp.int32, (taps, both), 1)
    for n, at in enumerate((span - b, span + both - b, span + b, b - span)):
        bases[n] = jnp.dot(rounded, flag(a == at).astype(bf16), preferred_element_type=f32)

    square_rows = lax.broadcasted_iota(jnp.int32, (both, both), 0)
    square_cols = lax.broadcasted_iota(jnp.int32, (both, both), 1)
    unwrapped = square_cols < both - square_rows

    def build(block, n):
        def tile(t, carry):
            for i in range(per_tile):
                g = pl.ds(t * per_tile + i, 1)
                row = jnp.where(unwrapped, bases[n, g, :], bases[n + 1, g, :])
                rolled = pltpu.roll(row, 0, 1, stride=1, stride_axis=0)
                block[t, i // 2, :, pl.ds(i % 2 * both, both)] = rolled.astype(bf16)
            return carry

        return tile

    pairs = per_tile // 2
    wide = seqs * LANES
    lane = lax.rem(lax.broadcasted_iota(jnp.int32, (1, wide), 1), LANES) // members
    parity = [flag(lax.rem(lane, 2) == e).astype(bf16) for e in range(2)]
    pair_masks = [flag(lane // 2 == k).astype(bf16) for k in range(pairs)]
    blank = jnp.zeros((span, wide), bf16)

    def across(ref, j, at):
        return jnp.concatenate([ref[j, s, at, :] for s in range(seqs)], axis=1)

    def own_lanes(results, height):
        picked = results[:height]
        for k in range(1, pairs):
            picked = jnp.where(lane // 2 == k, results[k * height : (k + 1) * height], picked)
        return picked

    def apply(block, data):
        height = block.shape[1]
        results = jnp.dot(block.reshape(pairs * height, 2 * both), data, preferred_element_type=f32)
        return own_lanes(results, height)

    whole, low, top = pl.ds(0, both), pl.ds(0, span), pl.ds(span, span)

    def forward(j):
        at = pl.ds(pl.multiple_of(j * LANES, LANES), LANES)
        window = across(units, j, whole)
        held = window * wide_masks[0]
        other = window[span:] * half_masks[...]
        result = apply(forward_block[j], jnp.concatenate([held * p for p in parity], axis=0))
        rest = apply(
            forward_block[j, :, low, :],
            jnp.concatenate([blank, other * parity[0], blank, other * parity[1]], axis=0),
        )
        sent = (blends[1] * window[span:].astype(f32) + blends[2] * result[span:]).astype(bf16)
        filtered = jnp.where(blends[0] > 0.5, result[:span], rest) + blends[3] * window[:span].astype(f32)
        for s in range(seqs):
            mine_at = slice(s * LANES, (s + 1) * LANES)
            up_out[j, s] = sent[:, mine_at]
            gated_output[s, :, at] = (gate[s, :, at].astype(f32) * filtered[:, mine_at]).astype(bf16)
            gate_gradient[s, :, at] = (cotangent[s, :, at].astype(f32) * filtered[:, mine_at]).astype(bf16)

    def backward(j):
        at = pl.ds(pl.multiple_of(j * LANES, LANES), LANES)
        window = across(followers, j, whole)
        held = window * wide_masks[1]
        other = window[:span] * half_masks[...]
        result = apply(backward_block[j], jnp.concatenate([held * p for p in parity], axis=0))
        rest = apply(
            backward_block[j, :, top, :],
            jnp.concatenate([other * parity[0], blank, other * parity[1], blank], axis=0),
        )
        late = jnp.where(j >= held_back, one, zero)
        relayed = (1.0 - late) * blends[4]
        added = (1.0 - late * flag(here == 1)) * blends[6]
        sent = (relayed * window[:span].astype(f32) + blends[5] * result[:span]).astype(bf16)
        adjoint = jnp.where(blends[0] > 0.5, result[span:], rest) + added * window[span:].astype(f32)
        kept[j] = adjoint
        for s in range(seqs):
            mine_at = slice(s * LANES, (s + 1) * LANES)
            down_out[j, s] = sent[:, mine_at]
            key_gradient[s, :, at] = (adjoint[:, mine_at] * value[s, :, at].astype(f32)).astype(bf16)
            value_gradient[s, :, at] = (adjoint[:, mine_at] * key[s, :, at].astype(f32)).astype(bf16)

    def conclude(k, carry):
        late_copy(k).wait_recv()
        j = held_back + k
        at = pl.ds(pl.multiple_of(j * LANES, LANES), LANES)
        for s in range(seqs):
            adjoint = kept[j, :, pl.ds(s * LANES, LANES)] + late_in[k, s].astype(f32)
            key_gradient[s, :, at] = (adjoint * value[s, :, at].astype(f32)).astype(bf16)
            value_gradient[s, :, at] = (adjoint * key[s, :, at].astype(f32)).astype(bf16)
        return carry

    exchange = flag(square_rows + square_cols == both - 1).astype(bf16)
    wrapped = flag(square_cols < square_rows)

    def paired(j, outer=False):
        source = jnp.concatenate([blank, across(units, j, top)], axis=0) if outer else across(units, j, whole)
        reversed_units = jnp.dot(exchange, source, preferred_element_type=f32).astype(bf16)
        held = reversed_units * wide_masks[2]
        other = reversed_units * wide_masks[3]
        sources = jnp.concatenate(
            [jnp.concatenate([x * p for p in parity], axis=0) for x in (held, other)], axis=1
        )
        window = across(followers, j, low if outer else whole)
        held = window * (wide_masks[1, low, :] if outer else wide_masks[1])
        other = window[:span] * half_masks[...]

        def by_pair(x):
            repeat = x.shape[1] // wide
            return jnp.concatenate([x * jnp.concatenate([m] * repeat, axis=1) for m in pair_masks], axis=0)

        contract = (((1,), (1,)), ((), ()))
        own = lax.dot_general(
            by_pair(jnp.concatenate([held[:span], other], axis=1)), sources, contract, preferred_element_type=f32
        )
        if not outer:
            next_ones = lax.dot_general(by_pair(held[span:]), sources[:, :wide], contract, preferred_element_type=f32)
        for i in range(per_tile):
            at = slice(i // 2 * span, (i // 2 + 1) * span)
            across_at = slice(i % 2 * both, (i % 2 + 1) * both)
            near = pltpu.roll(own[at, across_at], 0, 1, stride=1, stride_axis=0)
            total, high = near, near * wrapped[:span]
            if not outer:
                far = pltpu.roll(next_ones[at, across_at], span, 1, stride=1, stride_axis=0)
                total, high = total + far, high + far * wrapped[span:]
            total = jnp.sum(total, axis=0, keepdims=True)
            high = jnp.sum(high, axis=0, keepdims=True)
            tap_sums[j, pl.ds(i, 1), pl.ds(0, both)] = total - high
            tap_sums[j, pl.ds(i, 1), pl.ds(both, both)] = high

    def up_wait(j):
        @pl.when(jnp.logical_not(first))
        def _():
            up_copy(j).wait_recv()

    def down_wait(j):
        @pl.when(jnp.logical_not(last))
        def _():
            down_copy(j).wait_recv()

    def up_start(j):
        @pl.when(hub)
        def _():
            up_copy(j).start()

    def down_start(j):
        @pl.when((here == 1) | ((here == 2) & (j < held_back)))
        def _():
            down_copy(j).start()

        @pl.when((here == 2) & (j >= held_back))
        def _():
            late_copy(jnp.maximum(j - held_back, 0)).start()

    steps = tiles // TOGETHER
    early_steps = EARLY // TOGETHER

    def forwards(n):
        return [n * TOGETHER + k for k in range(TOGETHER)]

    def rotated(n):
        return forwards(lax.rem(n + steps - early_steps, steps))

    def sweep(near, far, order, far_block, far_base, lag):
        near_wait, near_math, near_start = near
        far_wait, far_math, far_start = far
        portion = -(-tiles // AHEAD)

        def run(low, high, near_at=None, far_at=None, paired_at=()):
            def step(n, carry):
                nears = forwards(n + near_at) if near_at is not None else []
                fars = order(n) if far_at is not None else []
                pairings = [j for offset in paired_at for j in forwards(n + offset)]
                for j in nears:
                    near_wait(j)
                for j in fars:
                    far_wait(j)
                for j in nears:
                    near_math(j)
                for j in fars:
                    far_math(j)
                for j in pairings:
                    paired(j)
                for j in nears:
                    near_start(j)
                for j in fars:
                    far_start(j)
                if not fars:
                    lax.fori_loop(
                        n * portion, jnp.minimum((n + 1) * portion, tiles), build(far_block, far_base), 0
                    )
                return carry

            lax.fori_loop(low, high, step, 0)

        run(0, AHEAD, near_at=0)
        pass_calls()
        run(0, lag, near_at=AHEAD, far_at=0)
        run(lag, steps - AHEAD, near_at=AHEAD, far_at=0, paired_at=(-lag,))
        run(steps - AHEAD, steps - AHEAD + lag, far_at=0, paired_at=(-lag, AHEAD - lag) if lag else (0,))
        run(steps - AHEAD + lag, steps, far_at=0, paired_at=(-lag,))

    a = lax.broadcasted_iota(jnp.int32, (taps, 2 * both), 0)
    b = lax.broadcasted_iota(jnp.int32, (taps, 2 * both), 1)
    pick = flag(((a == b - (span - 1)) & (b < both)) | ((a == b - both + span + 1) & (b >= both)))
    share = taps // sharers

    def share_copy(z, n):
        return pltpu.make_async_remote_copy(
            src_ref=shares_out.at[z * n_batch + n], dst_ref=shares_in.at[mine],
            send_sem=share_send.at[z * n_batch + n], recv_sem=share_recv.at[mine],
            device_id={"seq": z, "batch": n}, device_id_type=MESH,
        )

    def share_arrival(z, n):
        at = z * n_batch + n
        return pltpu.make_async_remote_copy(
            src_ref=shares_out.at[at], dst_ref=shares_in.at[at], send_sem=share_send.at[at],
            recv_sem=share_recv.at[at], device_id={"seq": z, "batch": n}, device_id_type=MESH,
        )

    def square_copy(z, n):
        return pltpu.make_async_remote_copy(
            src_ref=squares_out, dst_ref=squares_in.at[mine],
            send_sem=square_send.at[z * n_batch + n], recv_sem=square_recv.at[mine],
            device_id={"seq": z, "batch": n}, device_id_type=MESH,
        )

    def square_arrival(z, n):
        at = z * n_batch + n
        return pltpu.make_async_remote_copy(
            src_ref=squares_out, dst_ref=squares_in.at[at], send_sem=square_send.at[at],
            recv_sem=square_recv.at[at], device_id={"seq": z, "batch": n}, device_id_type=MESH,
        )

    def others(act, low, high, allowed):
        for z in range(low, high):
            for n in range(n_batch):
                @pl.when(allowed(z) & (mine != z * n_batch + n))
                def _():
                    act(z, n)

    def shares_to(z):
        return hub if z > 0 else hub | first | last

    def shares_from(z):
        return (first | hub) & (here < n_seq - 1) if 0 < z < n_seq - 1 else first

    def send_shares():
        by_tap = lax.dot_general(
            pick, tap_sums[...].reshape(groups, 2 * both), (((1,), (1,)), ((), ())),
            precision=lax.Precision.HIGHEST, preferred_element_type=f32,
        )
        for i in range(sharers):
            shares_out[i] = by_tap[i * share : (i + 1) * share, :]
        others(lambda z, n: share_copy(z, n).start(), 0, n_seq - 1, shares_to)

    def alone(near, far, order):
        near_wait, near_math, near_start = near
        far_wait, far_math, far_start = far

        def local(n, carry):
            for j in forwards(n):
                near_math(j)
                paired(j, outer=True)
            return carry

        def finish(n, carry):
            for j in order(n):
                far_wait(j)
            for j in order(n):
                far_math(j)
            return carry

        lax.fori_loop(0, tiles, build(forward_block, 0), 0)
        lax.fori_loop(0, tiles, build(backward_block, 2), 0)
        lax.fori_loop(0, steps, local, 0)
        close_calls()
        send_shares()
        lax.fori_loop(0, steps, finish, 0)

    up_stage = (up_wait, forward, up_start)
    down_stage = (down_wait, backward, down_start)

    @pl.when(first)
    def _():
        alone(up_stage, down_stage, rotated)

    @pl.when(last)
    def _():
        alone(down_stage, up_stage, forwards)

    @pl.when(here == 1)
    def _():
        lax.fori_loop(0, tiles, build(forward_block, 0), 0)
        sweep(up_stage, down_stage, rotated, backward_block, 2, early_steps)
        send_shares()
        lax.fori_loop(0, EARLY, conclude, 0)

    @pl.when(here == 2)
    def _():
        lax.fori_loop(0, tiles, build(backward_block, 2), 0)
        sweep(down_stage, up_stage, forwards, forward_block, 0, 0)
        send_shares()

    def chan_copy(i):
        return pltpu.make_async_remote_copy(
            src_ref=chan_out, dst_ref=chan_in.at[i - 1],
            send_sem=chan_send.at[i - 1], recv_sem=chan_recv.at[i - 1],
            device_id={"chan": lax.rem(chan + i, n_chan)}, device_id_type=MESH,
        )

    others(lambda z, n: share_arrival(z, n).wait_recv(), 0, n_seq, shares_from)
    total = shares_out[mine] + jnp.sum(shares_in[...], axis=0)
    squares_out[...] = jnp.sum(total * total, axis=0, keepdims=True)
    squared = jnp.logical_not(last)
    others(lambda z, n: square_copy(z, n).start(), 0, n_seq, lambda z: squared)
    others(lambda z, n: square_arrival(z, n).wait_recv(), 0, n_seq - 1, lambda z: here >= 0)
    chan_out[...] = jnp.sum(squares_in[...], axis=0) + squares_out[...]
    for i in range(1, n_chan):
        chan_copy(i).start()
    for i in range(1, n_chan):
        chan_copy(i).wait_recv()
    squares = jnp.sum(chan_in[...], axis=0) + chan_out[...]
    mean = jnp.sum(squares, axis=1, keepdims=True) / (taps * groups * n_chan)
    filter_update[...] = total * jnp.minimum(1.0, 1.0 / jnp.sqrt(mean + 1e-06))

    others(lambda z, n: share_copy(z, n).wait_send(), 0, n_seq - 1, shares_to)
    others(lambda z, n: square_copy(z, n).wait_send(), 0, n_seq, lambda z: squared)
    for i in range(1, n_chan):
        chan_copy(i).wait_send()

    def drain(copy, count=tiles):
        def step(j, carry):
            copy(j).wait_send()
            return carry

        lax.fori_loop(0, count, step, 0)

    @pl.when(here == 2)
    def _():
        drain(late_copy, EARLY)

    @pl.when(here + 1 < n_seq)
    def _():
        drain(up_copy)

    @pl.when(here >= 1)
    def _():
        drain(down_copy)


def store_kernel(count, *refs):
    sources, targets, sems = refs[:count], refs[count : 2 * count], refs[2 * count]
    copies = [pltpu.make_async_copy(sources[n], targets[n], sems.at[n]) for n in range(count)]
    for copy in copies:
        copy.start()
    for copy in copies:
        copy.wait()


def hub_device(sizes, gate_input, key_input, value_input, cotangent, filters, document_lengths):
    n_seq, n_batch, n_chan = sizes
    seqs, span, width = gate_input.shape
    groups, taps = filters.shape
    tiles = width // LANES
    sharers = n_seq * n_batch
    share = taps // sharers
    both = 2 * span
    per_tile = groups // tiles
    dims = (n_seq, n_batch, n_chan, tiles, seqs, span, groups, taps)
    bf16, f32 = jnp.bfloat16, jnp.float32
    vmem, anywhere = pl.BlockSpec(memory_space=pltpu.VMEM), pl.BlockSpec(memory_space=pl.ANY)
    dma = pltpu.SemaphoreType.DMA
    shape = gate_input.shape
    results = pl.pallas_call(
        functools.partial(hub_kernel, dims),
        out_shape=(pltpu.VMEM(shape, bf16),) * 4 + (pltpu.VMEM((share, groups), f32),),
        in_specs=[pl.BlockSpec(memory_space=pltpu.HBM)] * 6,
        out_specs=(vmem,) * 5,
        scratch_shapes=[
            pltpu.VMEM(shape, bf16), pltpu.VMEM(shape, bf16), pltpu.VMEM(shape, bf16), pltpu.VMEM(shape, bf16),
            pltpu.VMEM((groups, taps), f32), pltpu.SMEM(document_lengths.shape, jnp.int32),
            pltpu.VMEM((tiles, seqs, both, LANES), bf16),
            pltpu.VMEM((tiles, seqs, both, LANES), bf16),
            pltpu.VMEM((tiles, seqs, span, LANES), bf16),
            pltpu.VMEM((tiles, seqs, span, LANES), bf16),
            pltpu.VMEM((tiles, per_tile // 2, both, 2 * both), bf16),
            pltpu.VMEM((tiles, per_tile // 2, both, 2 * both), bf16),
            pltpu.VMEM((4, groups, both), f32),
            pltpu.VMEM((4, both, seqs * LANES), bf16),
            pltpu.VMEM((span, seqs * LANES), bf16),
            pltpu.VMEM((7, span, seqs * LANES), f32),
            pltpu.VMEM((tiles, per_tile, 2 * both), f32),
            pltpu.VMEM((tiles, span, seqs * LANES), f32),
            pltpu.VMEM((EARLY, seqs, span, LANES), bf16),
            pltpu.VMEM((sharers, share, groups), f32),
            pltpu.VMEM((sharers, share, groups), f32),
            pltpu.VMEM((1, groups), f32),
            pltpu.VMEM((sharers, 1, groups), f32),
            pltpu.VMEM((1, groups), f32),
            pltpu.VMEM((n_chan - 1, 1, groups), f32),
            dma((LOADS, 4)), dma((2,)),
            dma((tiles,)), dma((tiles,)), dma((tiles,)), dma((tiles,)), dma((EARLY,)), dma((EARLY,)),
            dma((sharers,)), dma((sharers,)), dma((sharers,)), dma((sharers,)),
            dma((n_chan - 1,)), dma((n_chan - 1,)),
            pltpu.SemaphoreType.REGULAR, pltpu.SemaphoreType.REGULAR,
        ],
        compiler_params=pltpu.CompilerParams(
            collective_id=0, has_side_effects=True, vmem_limit_bytes=40 * 1024 * 1024
        ),
    )(*[
        pltpu.with_memory_space_constraint(x, pltpu.HBM)
        for x in (gate_input, key_input, value_input, cotangent, filters, document_lengths)
    ])
    like = jax.ShapeDtypeStruct(shape, bf16)
    return pl.pallas_call(
        functools.partial(store_kernel, 5),
        out_shape=(like, like, like, like, jax.ShapeDtypeStruct((share, groups), f32)),
        in_specs=[vmem] * 5,
        out_specs=(anywhere,) * 5,
        scratch_shapes=[dma((5,))],
    )(*[pltpu.with_memory_space_constraint(x, pltpu.VMEM) for x in results])


def per_device(sizes, gate_input, key_input, value_input, cotangent, filters, document_lengths):
    n_seq = sizes[0]
    span, width = gate_input.shape[1:]
    groups, taps = filters.shape
    two = document_lengths.shape[1] == 2 and n_seq == 4 and taps == n_seq * span and taps % (n_seq * sizes[1]) == 0
    if two and 2 * span == LANES and (width // LANES) % LOADS == 0 and width // LANES > AHEAD * TOGETHER + EARLY:
        device = hub_device
    else:
        device = wide_device
    return device(sizes, gate_input, key_input, value_input, cotangent, filters, document_lengths)


def solution(mesh):
    block = P("batch", "seq", "chan")
    sizes = (mesh.shape["seq"], mesh.shape["batch"], mesh.shape["chan"])
    return jax.shard_map(
        functools.partial(per_device, sizes),
        mesh=mesh,
        in_specs=(block, block, block, block, P("chan", None), P("batch", None)),
        out_specs=(block, block, block, block, P(("seq", "batch"), "chan")),
        check_vma=False,
    )
```

```python
import functools

import jax
import jax.numpy as jnp
from jax import lax
from jax.experimental import pallas as pl
from jax.experimental.pallas import tpu as pltpu
from jax.sharding import PartitionSpec as P

MESH = pl.DeviceIdType.MESH
LANES = 128
HELD = 4
SHARES_AT = 4


def kernel(
    dims, gate, key, value, cotangent, filters, lengths,
    gated_output, gate_gradient, key_gradient, value_gradient, filter_update,
    units, followers, reversed_own, plain, flipped, forward_block, backward_block,
    forward_mask, backward_mask, sums_mask, tap_sums, shares_out, shares_in, squares_out, squares_in,
    chan_out, chan_in,
    unit_send, unit_recv, cot_send, cot_recv, share_send, share_recv, square_send, square_recv,
    chan_send, chan_recv,
):
    n_seq, n_batch, n_chan, reach, wide, chunks, tiles, seqs, span, groups, taps, ndocs = dims
    everyone = n_seq * n_batch * n_chan
    sharers = n_seq * n_batch
    here = lax.axis_index("seq")
    batch = lax.axis_index("batch")
    chan = lax.axis_index("chan")
    me = (here * n_batch + batch) * n_chan + chan
    mine = here * n_batch + batch
    per_tile = LANES * groups // (tiles * chunks * LANES)
    members = LANES // per_tile
    lanes = tiles * LANES
    own = reach * span
    hub = reach == 2

    barrier = pltpu.get_barrier_semaphore()

    rest = wide - own - span
    for c in range(chunks):
        for s in range(seqs):
            units[c, s, pl.ds(0, own), :] = jnp.zeros((own, lanes), jnp.bfloat16)
            units[c, s, pl.ds(own + span, rest), :] = jnp.zeros((rest, lanes), jnp.bfloat16)
            followers[c, s, pl.ds(span, wide - span), :] = jnp.zeros((wide - span, lanes), jnp.bfloat16)

    def greet(i, carry):
        other = lax.rem(me + i, everyone)
        pl.semaphore_signal(
            barrier, inc=1, device_id_type=MESH,
            device_id={
                "seq": other // (n_batch * n_chan),
                "batch": lax.rem(other // n_chan, n_batch),
                "chan": lax.rem(other, n_chan),
            },
        )
        return carry

    lax.fori_loop(1, everyone, greet, 0)

    for c in range(chunks):
        at = pl.ds(c * lanes, lanes)
        for s in range(seqs):
            u = (key[s, :, at].astype(jnp.float32) * value[s, :, at].astype(jnp.float32)).astype(jnp.bfloat16)
            g = (cotangent[s, :, at].astype(jnp.float32) * gate[s, :, at].astype(jnp.float32)).astype(jnp.bfloat16)
            units[c, s, pl.ds(own, span), :] = u
            followers[c, s, pl.ds(0, span), :] = g

    def unit_copy(lag, c):
        source = units.at[c, :, pl.ds((reach - lag + 1) * span, span), :]
        target = units.at[c, :, pl.ds((reach - lag) * span, span), :]
        return pltpu.make_async_remote_copy(
            src_ref=source, dst_ref=target, send_sem=unit_send.at[lag - 1, c], recv_sem=unit_recv.at[lag - 1, c],
            device_id={"seq": here + 1}, device_id_type=MESH,
        )

    def cot_copy(lag, c):
        source = followers.at[c, :, pl.ds((lag - 1) * span, span), :]
        target = followers.at[c, :, pl.ds(lag * span, span), :]
        return pltpu.make_async_remote_copy(
            src_ref=source, dst_ref=target, send_sem=cot_send.at[lag - 1, c], recv_sem=cot_recv.at[lag - 1, c],
            device_id={"seq": here - 1}, device_id_type=MESH,
        )

    def sends_up(lag):
        return (here >= lag - 1) & (here + 1 < n_seq)

    def sends_down(lag):
        return (here + lag - 1 < n_seq) & (here >= 1)

    def send(lag, c):
        @pl.when(sends_up(lag))
        def _():
            unit_copy(lag, c).start()

        @pl.when(sends_down(lag))
        def _():
            cot_copy(lag, c).start()

    def receive(lag, c):
        @pl.when(here >= lag)
        def _():
            unit_copy(lag, c).wait_recv()

        @pl.when(here + lag < n_seq)
        def _():
            cot_copy(lag, c).wait_recv()

    pl.semaphore_wait(barrier, everyone - 1)
    for c in range(chunks):
        send(1, c)

    def documents(positions, s):
        count = jnp.zeros(positions.shape, jnp.int32)
        end = 0
        for n in range(ndocs):
            end = end + lengths[s, n]
            count = count + (positions >= end).astype(jnp.int32)
        return count

    rows = lax.broadcasted_iota(jnp.int32, (span, 1), 0)
    cols = lax.broadcasted_iota(jnp.int32, (1, wide), 1)
    for s in range(seqs):
        earlier = (here - reach) * span + cols
        later = here * span + cols
        target = here * span + rows
        back = here * span + (span - 1 - rows)
        earlier_doc = documents(earlier, s)
        later_doc = documents(later, s)
        target_doc = documents(target, s)
        back_doc = documents(back, s)
        keep = (earlier_doc == target_doc) & (earlier <= target) & (earlier >= 0)
        forward_mask[s] = jnp.where(keep, 1.0, 0.0).astype(jnp.bfloat16)
        if hub:
            first = cols < span
            origin = jnp.where(first, earlier + span, earlier)
            goal = jnp.where(first, back + span, back)
            goal_doc = jnp.where(first, documents(back + span, s), back_doc)
            keep = (documents(origin, s) == goal_doc) & (origin <= goal) & (origin >= 0) & (goal < n_seq * span)
        else:
            keep = (earlier_doc == back_doc) & (earlier <= back) & (earlier >= 0)
        sums_mask[s] = jnp.where(keep, 1.0, 0.0)
        keep = (later_doc == target_doc) & (later >= target) & (later < n_seq * span)
        backward_mask[s] = jnp.where(keep, 1.0, 0.0).astype(jnp.bfloat16)

    rounded = filters[...].astype(jnp.bfloat16)
    a = lax.broadcasted_iota(jnp.int32, (taps, wide), 0)
    b = lax.broadcasted_iota(jnp.int32, (taps, wide), 1)
    flip = own - b
    flip = jnp.where(flip < 0, flip + wide, flip)
    plain[...] = jnp.dot(rounded, jnp.where(a == b, 1.0, 0.0).astype(jnp.bfloat16), preferred_element_type=jnp.float32)
    flipped[...] = jnp.dot(rounded, jnp.where(a == flip, 1.0, 0.0).astype(jnp.bfloat16), preferred_element_type=jnp.float32)

    def build(t, carry):
        for i in range(per_tile):
            g = t * per_tile + i
            at = pl.ds(pl.multiple_of(g * span, span), span)
            row = jnp.broadcast_to(flipped[pl.ds(g, 1), :], (span, wide))
            forward_block[at, :] = pltpu.roll(row, 0, 1, stride=1, stride_axis=0).astype(jnp.bfloat16)
            row = jnp.broadcast_to(plain[pl.ds(g, 1), :], (span, wide))
            backward_block[at, :] = pltpu.roll(row, 0, 1, stride=1, stride_axis=0).astype(jnp.bfloat16)
        return carry

    order_a = lax.broadcasted_iota(jnp.int32, (span, span), 0)
    order_b = lax.broadcasted_iota(jnp.int32, (span, span), 1)
    exchange = jnp.where(order_a + order_b == span - 1, 1.0, 0.0).astype(jnp.bfloat16)
    lane = lax.broadcasted_iota(jnp.int32, (1, LANES), 1) // members

    def members_apart(block):
        return jnp.concatenate(
            [block * jnp.where(lane == i, 1.0, 0.0).astype(jnp.bfloat16) for i in range(per_tile)], axis=0
        )

    def paired(c, j, carry):
        at = pl.ds(pl.multiple_of(j * LANES, LANES), LANES)
        total = None
        for s in range(seqs):
            target = members_apart(reversed_own[c, s, pl.ds(0, span), at])
            if hub:
                target = jnp.concatenate([target, members_apart(reversed_own[c, s, pl.ds(span, span), at])], axis=1)
                past = units[c, s, pl.ds(own - span, span), at]
                blank = jnp.zeros((span, LANES), jnp.bfloat16)
                tail = jnp.zeros((wide - own - span, LANES), jnp.bfloat16)
                source = jnp.concatenate(
                    [
                        jnp.concatenate([blank, past, units[c, s, pl.ds(own, span), at], tail], axis=0),
                        jnp.concatenate([past, blank, blank, tail], axis=0),
                    ],
                    axis=1,
                )
            else:
                source = units[c, s, :, at]
            products = lax.dot_general(
                target, source, (((1,), (1,)), ((), ())), preferred_element_type=jnp.float32
            ).reshape(per_tile, span, wide)
            products = products * sums_mask[s][None]
            total = products if total is None else total + products
        for i in range(per_tile):
            aligned = pltpu.roll(total[i], 0, 1, stride=1, stride_axis=0)
            tap_sums[pl.ds((c * tiles + j) * per_tile + i, 1), :] = jnp.sum(aligned, axis=0, keepdims=True)
        return carry

    def reverse(c):
        for s in range(seqs):
            for n in range(2 if hub else 1):
                at = pl.ds(n * span, span)
                reversed_own[c, s, at, :] = jnp.dot(
                    exchange, followers[c, s, at, :], preferred_element_type=jnp.float32
                ).astype(jnp.bfloat16)

    for c in range(chunks):
        lax.fori_loop(c * tiles, (c + 1) * tiles, build, 0)
        for lag in range(1, reach):
            receive(lag, c)
            if not (hub and c >= HELD):
                send(lag + 1, c)
        if hub:
            reverse(c)
            lax.fori_loop(0, tiles, functools.partial(paired, c), 0)
    if not hub:
        for c in range(chunks):
            receive(reach, c)
            reverse(c)
            lax.fori_loop(0, tiles, functools.partial(paired, c), 0)

    a = lax.broadcasted_iota(jnp.int32, (taps, wide), 0)
    b = lax.broadcasted_iota(jnp.int32, (taps, wide), 1)
    pick = jnp.where(a + b == own + span - 1, 1.0, 0.0)
    by_tap = lax.dot_general(
        pick, tap_sums[...], (((1,), (1,)), ((), ())),
        precision=lax.Precision.HIGHEST, preferred_element_type=jnp.float32,
    )
    share = taps // sharers
    for i in range(sharers):
        shares_out[i] = by_tap[i * share : (i + 1) * share, :]

    def share_copy(i):
        other = lax.rem(mine + i, sharers)
        return pltpu.make_async_remote_copy(
            src_ref=shares_out.at[other], dst_ref=shares_in.at[i - 1],
            send_sem=share_send.at[i - 1], recv_sem=share_recv.at[i - 1],
            device_id={"seq": other // n_batch, "batch": lax.rem(other, n_batch)}, device_id_type=MESH,
        )

    def square_copy(i):
        other = lax.rem(mine + i, sharers)
        return pltpu.make_async_remote_copy(
            src_ref=squares_out, dst_ref=squares_in.at[i - 1],
            send_sem=square_send.at[i - 1], recv_sem=square_recv.at[i - 1],
            device_id={"seq": other // n_batch, "batch": lax.rem(other, n_batch)}, device_id_type=MESH,
        )

    def chan_copy(i):
        return pltpu.make_async_remote_copy(
            src_ref=chan_out, dst_ref=chan_in.at[i - 1],
            send_sem=chan_send.at[i - 1], recv_sem=chan_recv.at[i - 1],
            device_id={"chan": lax.rem(chan + i, n_chan)}, device_id_type=MESH,
        )

    def loop(low, high, act):
        if high <= 32:
            for i in range(low, high):
                act(i)
            return

        def step(i, carry):
            act(i)
            return carry

        lax.fori_loop(low, high, step, 0)

    def convolve(c, j, carry):
        at = pl.ds(pl.multiple_of(j * LANES, LANES), LANES)
        t = c * tiles + j
        out = pl.ds(pl.multiple_of(t * LANES, LANES), LANES)
        height = per_tile * span
        block = pl.ds(pl.multiple_of(t * height, height), height)

        def apply(block_ref, mask_ref, data_ref, s):
            masked = block_ref[block, :].reshape(per_tile, span, wide) * mask_ref[s][None]
            results = jnp.dot(
                masked.reshape(height, wide), data_ref[c, s, :, at], preferred_element_type=jnp.float32
            )
            picked = results[:span]
            for i in range(1, per_tile):
                picked = jnp.where(lane == i, results[i * span : (i + 1) * span], picked)
            return picked

        for s in range(seqs):
            filtered = apply(forward_block, forward_mask, units, s)
            gated_output[s, :, out] = (gate[s, :, out].astype(jnp.float32) * filtered).astype(jnp.bfloat16)
            gate_gradient[s, :, out] = (cotangent[s, :, out].astype(jnp.float32) * filtered).astype(jnp.bfloat16)
            adjoint = apply(backward_block, backward_mask, followers, s)
            key_gradient[s, :, out] = (adjoint * value[s, :, out].astype(jnp.float32)).astype(jnp.bfloat16)
            value_gradient[s, :, out] = (adjoint * key[s, :, out].astype(jnp.float32)).astype(jnp.bfloat16)
        return carry

    loop(1, sharers, lambda i: share_copy(i).start())
    if hub:
        for c in range(HELD, chunks):
            send(reach, c)
    for c in range(chunks):
        if hub:
            receive(reach, c)
        if c == SHARES_AT:
            loop(1, sharers, lambda i: share_copy(i).wait_recv())
            total = shares_out[mine] + jnp.sum(shares_in[...], axis=0)
            filter_update[...] = total
            squares_out[...] = jnp.sum(total * total, axis=0, keepdims=True)
        if c == SHARES_AT + 1:
            loop(1, sharers, lambda i: square_copy(i).start())
        lax.fori_loop(0, tiles, functools.partial(convolve, c), 0)
    loop(1, sharers, lambda i: square_copy(i).wait_recv())
    chan_out[...] = jnp.sum(squares_in[...], axis=0) + squares_out[...]
    loop(1, sharers, lambda i: share_copy(i).wait_send())
    loop(1, sharers, lambda i: square_copy(i).wait_send())
    loop(1, n_chan, lambda i: chan_copy(i).start())
    loop(1, n_chan, lambda i: chan_copy(i).wait_recv())
    squares = jnp.sum(chan_in[...], axis=0) + chan_out[...]
    mean = jnp.sum(squares, axis=1, keepdims=True) / (taps * groups * n_chan)
    filter_update[...] = filter_update[...] * jnp.minimum(1.0, 1.0 / jnp.sqrt(mean + 1e-06))
    loop(1, n_chan, lambda i: chan_copy(i).wait_send())
    for lag in range(1, reach + 1):
        @pl.when(sends_up(lag))
        def _():
            for c in range(chunks):
                unit_copy(lag, c).wait_send()

        @pl.when(sends_down(lag))
        def _():
            for c in range(chunks):
                cot_copy(lag, c).wait_send()


def wide_device(sizes, gate_input, key_input, value_input, cotangent, filters, document_lengths):
    n_seq, n_batch, n_chan = sizes
    seqs, span, width = gate_input.shape
    groups, taps = filters.shape
    ndocs = document_lengths.shape[1]
    longest = min(taps, n_seq * span - span)
    reach = (longest - 1) // span if ndocs == 2 else (longest - 2) // span + 1
    wide = -(-((reach + 2) * span - 1) // LANES) * LANES
    chunks = 8
    tiles = width // (chunks * LANES)
    lanes = tiles * LANES
    sharers = n_seq * n_batch
    share = taps // sharers
    dims = (n_seq, n_batch, n_chan, reach, wide, chunks, tiles, seqs, span, groups, taps, ndocs)
    bf16, f32 = jnp.bfloat16, jnp.float32
    vmem = pl.BlockSpec(memory_space=pltpu.VMEM)
    dma = pltpu.SemaphoreType.DMA
    like = jax.ShapeDtypeStruct(gate_input.shape, bf16)
    return pl.pallas_call(
        functools.partial(kernel, dims),
        out_shape=(like, like, like, like, jax.ShapeDtypeStruct((share, groups), f32)),
        in_specs=[vmem] * 5 + [pl.BlockSpec(memory_space=pltpu.SMEM)],
        out_specs=(vmem,) * 5,
        scratch_shapes=[
            pltpu.VMEM((chunks, seqs, wide, lanes), bf16),
            pltpu.VMEM((chunks, seqs, wide, lanes), bf16),
            pltpu.VMEM((chunks, seqs, 2 * span, lanes), bf16),
            pltpu.VMEM((groups, wide), f32),
            pltpu.VMEM((groups, wide), f32),
            pltpu.VMEM((groups * span, wide), bf16),
            pltpu.VMEM((groups * span, wide), bf16),
            pltpu.VMEM((seqs, span, wide), bf16),
            pltpu.VMEM((seqs, span, wide), bf16),
            pltpu.VMEM((seqs, span, wide), f32),
            pltpu.VMEM((groups, wide), f32),
            pltpu.VMEM((sharers, share, groups), f32),
            pltpu.VMEM((sharers - 1, share, groups), f32),
            pltpu.VMEM((1, groups), f32),
            pltpu.VMEM((sharers - 1, 1, groups), f32),
            pltpu.VMEM((1, groups), f32),
            pltpu.VMEM((n_chan - 1, 1, groups), f32),
            dma((reach, chunks)), dma((reach, chunks)), dma((reach, chunks)), dma((reach, chunks)),
            dma((sharers - 1,)), dma((sharers - 1,)), dma((sharers - 1,)), dma((sharers - 1,)),
            dma((n_chan - 1,)), dma((n_chan - 1,)),
        ],
        compiler_params=pltpu.CompilerParams(
            collective_id=0, has_side_effects=True, vmem_limit_bytes=60 * 1024 * 1024
        ),
    )(gate_input, key_input, value_input, cotangent, filters, document_lengths)


AHEAD = 3
BEHIND = 2
TOGETHER = 2
LOADS = 8
EARLY = 6


def hub_kernel(
    dims, gate_hbm, key_hbm, value_hbm, cotangent_hbm, filters_hbm, lengths_hbm,
    gated_output, gate_gradient, key_gradient, value_gradient, filter_update,
    gate, key, value, cotangent, filters, lengths, units, followers, up_out, down_out,
    forward_block, backward_block, bases, wide_masks, half_masks, blends, tap_sums, kept, late_in,
    shares_out, shares_in, squares_out, squares_in, chan_out, chan_in,
    load_sem, small_sem, up_send, up_recv, down_send, down_recv, late_send, late_recv, share_send, share_recv, square_send, square_recv,
    chan_send, chan_recv, up_call, down_call,
):
    n_seq, n_batch, n_chan, tiles, seqs, span, groups, taps = dims
    sharers = n_seq * n_batch
    here = lax.axis_index("seq")
    batch = lax.axis_index("batch")
    chan = lax.axis_index("chan")
    mine = here * n_batch + batch
    per_tile = groups // tiles
    members = LANES // per_tile
    both = 2 * span
    f32, bf16 = jnp.float32, jnp.bfloat16

    part = tiles // LOADS * LANES

    def loads(q):
        at = pl.ds(q * part, part)
        pairs = ((key_hbm, key), (value_hbm, value), (cotangent_hbm, cotangent), (gate_hbm, gate))
        return [
            pltpu.make_async_copy(src.at[:, :, at], dst.at[:, :, at], load_sem.at[q, n])
            for n, (src, dst) in enumerate(pairs)
        ]

    for q in range(LOADS):
        for copy in loads(q):
            copy.start()

    filters_copy = pltpu.make_async_copy(filters_hbm, filters, small_sem.at[0])
    lengths_copy = pltpu.make_async_copy(lengths_hbm, lengths, small_sem.at[1])
    lengths_copy.start()
    filters_copy.start()
    shares_in[...] = jnp.zeros(shares_in.shape, f32)
    squares_in[...] = jnp.zeros(squares_in.shape, f32)
    beyond = (n_seq - 1) * n_batch
    shares_out[pl.ds(beyond, n_batch)] = jnp.zeros((n_batch,) + shares_out.shape[1:], f32)

    first, last = here == 0, here == n_seq - 1
    barrier = pltpu.get_barrier_semaphore()

    def greet(device):
        pl.semaphore_signal(barrier, inc=1, device_id_type=MESH, device_id=device)

    @pl.when(jnp.logical_not(first))
    def _():
        greet({"seq": here - 1})

    @pl.when(jnp.logical_not(last))
    def _():
        greet({"seq": here + 1})

    for i in range(1, n_batch):
        greet({"batch": lax.rem(batch + i, n_batch)})
    for i in range(1, n_chan):
        greet({"chan": lax.rem(chan + i, n_chan)})
    greeted = n_batch - 1 + n_chan - 1 + jnp.where(first | last, 1, 2)

    def call(semaphore, target):
        pl.semaphore_signal(semaphore, inc=1, device_id_type=MESH, device_id={"seq": target})

    def open_calls():
        @pl.when(first)
        def _():
            call(up_call, here + 1)

        @pl.when(last)
        def _():
            call(down_call, here - 1)

    def pass_calls():
        pl.semaphore_wait(up_call, 1)
        call(up_call, here + 1)
        pl.semaphore_wait(down_call, 1)
        call(down_call, here - 1)

    def close_calls():
        @pl.when(first)
        def _():
            pl.semaphore_wait(down_call, 1)

        @pl.when(last)
        def _():
            pl.semaphore_wait(up_call, 1)

    hub = jnp.logical_not(first | last)
    own_units = units.at[:, :, pl.ds(span, span), :]
    own_cots = followers.at[:, :, pl.ds(0, span), :]

    def up_copy(j, source=up_out):
        return pltpu.make_async_remote_copy(
            src_ref=source.at[j], dst_ref=units.at[j, :, pl.ds(0, span), :],
            send_sem=up_send.at[j], recv_sem=up_recv.at[j], device_id={"seq": here + 1}, device_id_type=MESH,
        )

    def down_copy(j, source=down_out):
        return pltpu.make_async_remote_copy(
            src_ref=source.at[j], dst_ref=followers.at[j, :, pl.ds(span, span), :],
            send_sem=down_send.at[j], recv_sem=down_recv.at[j], device_id={"seq": here - 1}, device_id_type=MESH,
        )

    held_back = tiles - EARLY

    def late_copy(k):
        return pltpu.make_async_remote_copy(
            src_ref=down_out.at[held_back + k], dst_ref=late_in.at[k],
            send_sem=late_send.at[k], recv_sem=late_recv.at[k], device_id={"seq": here - 1}, device_id_type=MESH,
        )

    def gather(j, carry):
        at = pl.ds(pl.multiple_of(j * LANES, LANES), LANES)
        for s in range(seqs):
            u = (key[s, :, at].astype(f32) * value[s, :, at].astype(f32)).astype(bf16)
            g = (cotangent[s, :, at].astype(f32) * gate[s, :, at].astype(f32)).astype(bf16)
            units[j, s, pl.ds(span, span), :] = u
            followers[j, s, pl.ds(0, span), :] = g

        @pl.when(first)
        def _():
            up_copy(j, own_units).start()
            for s in range(seqs):
                units[j, s, pl.ds(0, span), :] = jnp.zeros((span, LANES), bf16)

        @pl.when(last)
        def _():
            down_copy(j, own_cots).start()
            for s in range(seqs):
                followers[j, s, pl.ds(span, span), :] = jnp.zeros((span, LANES), bf16)

        @pl.when((here == 2) & (j >= held_back))
        def _():
            down_copy(j, own_cots).start()

        return carry

    for q in range(LOADS):
        for copy in loads(q):
            copy.wait()
        if q == 0:
            pl.semaphore_wait(barrier, greeted)
            open_calls()
        lax.fori_loop(q * (tiles // LOADS), (q + 1) * (tiles // LOADS), gather, 0)

    lengths_copy.wait()
    filters_copy.wait()

    main = jnp.where(here * 2 >= n_seq, 1, 0)
    rows = lax.broadcasted_iota(jnp.int32, (both, LANES), 0)
    half = lax.broadcasted_iota(jnp.int32, (span, LANES), 0)
    one, zero = jnp.ones((), f32), jnp.zeros((), f32)

    def flag(condition):
        return jnp.where(condition, one, zero)

    for s in range(seqs):
        end = lengths[s, 0]
        at = pl.ds(s * LANES, LANES)

        def is_main(positions):
            return jnp.where(positions >= end, 1, 0) == main

        in_front = end <= both
        past_held = (here == 1) | ((here == 2) & in_front)
        next_held = (here == 2) | ((here == 1) & jnp.logical_not(in_front))
        past = (here - 1) * span
        own_main = is_main(here * span + half)
        back = both - 1 - rows
        wide_masks[0, :, at] = flag(is_main(past + rows) & ((rows >= span) | past_held)).astype(bf16)
        wide_masks[1, :, at] = flag(is_main(here * span + rows) & ((rows < span) | next_held)).astype(bf16)
        wide_masks[2, :, at] = flag(is_main(past + back) & ((back >= span) | past_held)).astype(bf16)
        wide_masks[3, :, at] = flag(jnp.logical_not(is_main(past + back)) & (back >= span)).astype(bf16)
        half_masks[:, at] = flag(jnp.logical_not(own_main)).astype(bf16)
        relay = flag((here == 1) & in_front)
        blends[0, :, at] = flag(own_main)
        blends[1, :, at] = jnp.broadcast_to(relay, (span, LANES))
        blends[2, :, at] = (1.0 - relay) * flag(is_main((here + 1) * span + half))
        blends[3, :, at] = jnp.broadcast_to(flag((here == 3) | ((here == 2) & jnp.logical_not(in_front))), (span, LANES))
        relay = flag((here == 2) & jnp.logical_not(in_front))
        blends[4, :, at] = jnp.broadcast_to(relay, (span, LANES))
        blends[5, :, at] = (1.0 - relay) * flag(is_main(past + half))
        blends[6, :, at] = jnp.broadcast_to(flag((here == 0) | ((here == 1) & in_front)), (span, LANES))

    rounded = filters[...].astype(bf16)
    a = lax.broadcasted_iota(jnp.int32, (taps, both), 0)
    b = lax.broadcasted_iota(jnp.int32, (taps, both), 1)
    for n, at in enumerate((span - b, span + both - b, span + b, b - span)):
        bases[n] = jnp.dot(rounded, flag(a == at).astype(bf16), preferred_element_type=f32)

    square_rows = lax.broadcasted_iota(jnp.int32, (both, both), 0)
    square_cols = lax.broadcasted_iota(jnp.int32, (both, both), 1)
    unwrapped = square_cols < both - square_rows

    def build(block, n):
        def tile(t, carry):
            for i in range(per_tile):
                g = pl.ds(t * per_tile + i, 1)
                row = jnp.where(unwrapped, bases[n, g, :], bases[n + 1, g, :])
                rolled = pltpu.roll(row, 0, 1, stride=1, stride_axis=0)
                block[t, i // 2, :, pl.ds(i % 2 * both, both)] = rolled.astype(bf16)
            return carry

        return tile

    pairs = per_tile // 2
    wide = seqs * LANES
    lane = lax.rem(lax.broadcasted_iota(jnp.int32, (1, wide), 1), LANES) // members
    parity = [flag(lax.rem(lane, 2) == e).astype(bf16) for e in range(2)]
    pair_masks = [flag(lane // 2 == k).astype(bf16) for k in range(pairs)]
    blank = jnp.zeros((span, wide), bf16)

    def across(ref, j, at):
        return jnp.concatenate([ref[j, s, at, :] for s in range(seqs)], axis=1)

    def own_lanes(results, height):
        picked = results[:height]
        for k in range(1, pairs):
            picked = jnp.where(lane // 2 == k, results[k * height : (k + 1) * height], picked)
        return picked

    def apply(block, data):
        height = block.shape[1]
        results = jnp.dot(block.reshape(pairs * height, 2 * both), data, preferred_element_type=f32)
        return own_lanes(results, height)

    whole, low, top = pl.ds(0, both), pl.ds(0, span), pl.ds(span, span)

    def forward(j):
        at = pl.ds(pl.multiple_of(j * LANES, LANES), LANES)
        window = across(units, j, whole)
        held = window * wide_masks[0]
        other = window[span:] * half_masks[...]
        result = apply(forward_block[j], jnp.concatenate([held * p for p in parity], axis=0))
        rest = apply(
            forward_block[j, :, low, :],
            jnp.concatenate([blank, other * parity[0], blank, other * parity[1]], axis=0),
        )
        sent = (blends[1] * window[span:].astype(f32) + blends[2] * result[span:]).astype(bf16)
        filtered = jnp.where(blends[0] > 0.5, result[:span], rest) + blends[3] * window[:span].astype(f32)
        for s in range(seqs):
            mine_at = slice(s * LANES, (s + 1) * LANES)
            up_out[j, s] = sent[:, mine_at]
            gated_output[s, :, at] = (gate[s, :, at].astype(f32) * filtered[:, mine_at]).astype(bf16)
            gate_gradient[s, :, at] = (cotangent[s, :, at].astype(f32) * filtered[:, mine_at]).astype(bf16)

    def backward(j):
        at = pl.ds(pl.multiple_of(j * LANES, LANES), LANES)
        window = across(followers, j, whole)
        held = window * wide_masks[1]
        other = window[:span] * half_masks[...]
        result = apply(backward_block[j], jnp.concatenate([held * p for p in parity], axis=0))
        rest = apply(
            backward_block[j, :, top, :],
            jnp.concatenate([other * parity[0], blank, other * parity[1], blank], axis=0),
        )
        late = jnp.where(j >= held_back, one, zero)
        relayed = (1.0 - late) * blends[4]
        added = (1.0 - late * flag(here == 1)) * blends[6]
        sent = (relayed * window[:span].astype(f32) + blends[5] * result[:span]).astype(bf16)
        adjoint = jnp.where(blends[0] > 0.5, result[span:], rest) + added * window[span:].astype(f32)
        kept[j] = adjoint
        for s in range(seqs):
            mine_at = slice(s * LANES, (s + 1) * LANES)
            down_out[j, s] = sent[:, mine_at]
            key_gradient[s, :, at] = (adjoint[:, mine_at] * value[s, :, at].astype(f32)).astype(bf16)
            value_gradient[s, :, at] = (adjoint[:, mine_at] * key[s, :, at].astype(f32)).astype(bf16)

    def conclude(k, carry):
        late_copy(k).wait_recv()
        j = held_back + k
        at = pl.ds(pl.multiple_of(j * LANES, LANES), LANES)
        for s in range(seqs):
            adjoint = kept[j, :, pl.ds(s * LANES, LANES)] + late_in[k, s].astype(f32)
            key_gradient[s, :, at] = (adjoint * value[s, :, at].astype(f32)).astype(bf16)
            value_gradient[s, :, at] = (adjoint * key[s, :, at].astype(f32)).astype(bf16)
        return carry

    exchange = flag(square_rows + square_cols == both - 1).astype(bf16)
    wrapped = flag(square_cols < square_rows)

    def paired(j, outer=False):
        source = jnp.concatenate([blank, across(units, j, top)], axis=0) if outer else across(units, j, whole)
        reversed_units = jnp.dot(exchange, source, preferred_element_type=f32).astype(bf16)
        held = reversed_units * wide_masks[2]
        other = reversed_units * wide_masks[3]
        sources = jnp.concatenate(
            [jnp.concatenate([x * p for p in parity], axis=0) for x in (held, other)], axis=1
        )
        window = across(followers, j, low if outer else whole)
        held = window * (wide_masks[1, low, :] if outer else wide_masks[1])
        other = window[:span] * half_masks[...]

        def by_pair(x):
            repeat = x.shape[1] // wide
            return jnp.concatenate([x * jnp.concatenate([m] * repeat, axis=1) for m in pair_masks], axis=0)

        contract = (((1,), (1,)), ((), ()))
        own = lax.dot_general(
            by_pair(jnp.concatenate([held[:span], other], axis=1)), sources, contract, preferred_element_type=f32
        )
        if not outer:
            next_ones = lax.dot_general(by_pair(held[span:]), sources[:, :wide], contract, preferred_element_type=f32)
        for i in range(per_tile):
            at = slice(i // 2 * span, (i // 2 + 1) * span)
            across_at = slice(i % 2 * both, (i % 2 + 1) * both)
            near = pltpu.roll(own[at, across_at], 0, 1, stride=1, stride_axis=0)
            total, high = near, near * wrapped[:span]
            if not outer:
                far = pltpu.roll(next_ones[at, across_at], span, 1, stride=1, stride_axis=0)
                total, high = total + far, high + far * wrapped[span:]
            total = jnp.sum(total, axis=0, keepdims=True)
            high = jnp.sum(high, axis=0, keepdims=True)
            tap_sums[j, pl.ds(i, 1), pl.ds(0, both)] = total - high
            tap_sums[j, pl.ds(i, 1), pl.ds(both, both)] = high

    def up_wait(j):
        @pl.when(jnp.logical_not(first))
        def _():
            up_copy(j).wait_recv()

    def down_wait(j):
        @pl.when(jnp.logical_not(last))
        def _():
            down_copy(j).wait_recv()

    def up_start(j):
        @pl.when(hub)
        def _():
            up_copy(j).start()

    def down_start(j):
        @pl.when((here == 1) | ((here == 2) & (j < held_back)))
        def _():
            down_copy(j).start()

        @pl.when((here == 2) & (j >= held_back))
        def _():
            late_copy(jnp.maximum(j - held_back, 0)).start()

    steps = tiles // TOGETHER
    early_steps = EARLY // TOGETHER

    def forwards(n):
        return [n * TOGETHER + k for k in range(TOGETHER)]

    def rotated(n):
        return forwards(lax.rem(n + steps - early_steps, steps))

    spread = (n_seq - 1) * span
    a = lax.broadcasted_iota(jnp.int32, (spread, 2 * both), 0)
    b = lax.broadcasted_iota(jnp.int32, (spread, 2 * both), 1)
    pick = flag(((a == b - (span - 1)) & (b < both)) | ((a == b - both + span + 1) & (b >= both))).astype(bf16)
    share = taps // sharers

    def share_copy(z, n):
        return pltpu.make_async_remote_copy(
            src_ref=shares_out.at[z * n_batch + n], dst_ref=shares_in.at[mine],
            send_sem=share_send.at[z * n_batch + n], recv_sem=share_recv.at[mine],
            device_id={"seq": z, "batch": n}, device_id_type=MESH,
        )

    def share_arrival(z, n):
        at = z * n_batch + n
        return pltpu.make_async_remote_copy(
            src_ref=shares_out.at[at], dst_ref=shares_in.at[at], send_sem=share_send.at[at],
            recv_sem=share_recv.at[at], device_id={"seq": z, "batch": n}, device_id_type=MESH,
        )

    def square_copy(z, n):
        return pltpu.make_async_remote_copy(
            src_ref=squares_out, dst_ref=squares_in.at[mine],
            send_sem=square_send.at[z * n_batch + n], recv_sem=square_recv.at[mine],
            device_id={"seq": z, "batch": n}, device_id_type=MESH,
        )

    def square_arrival(z, n):
        at = z * n_batch + n
        return pltpu.make_async_remote_copy(
            src_ref=squares_out, dst_ref=squares_in.at[at], send_sem=square_send.at[at],
            recv_sem=square_recv.at[at], device_id={"seq": z, "batch": n}, device_id_type=MESH,
        )

    def others(act, low, high, allowed):
        for z in range(low, high):
            for n in range(n_batch):
                @pl.when(allowed(z) & (mine != z * n_batch + n))
                def _():
                    act(z, n)

    def shares_to(z):
        return hub if z > 0 else hub | first | last

    def shares_from(z):
        return (first | hub) & (here < n_seq - 1) if 0 < z < n_seq - 1 else first

    def send_shares():
        sums = tap_sums[...].reshape(groups, 2 * both)
        by_tap = jnp.zeros((spread, groups), f32)
        for _ in range(3):
            piece = sums.astype(bf16)
            sums = sums - piece.astype(f32)
            by_tap = by_tap + lax.dot_general(pick, piece, (((1,), (1,)), ((), ())), preferred_element_type=f32)
        for i in range(spread // share):
            shares_out[i] = by_tap[i * share : (i + 1) * share, :]
        others(lambda z, n: share_copy(z, n).start(), 0, n_seq - 1, shares_to)

    def sweep(near, far, order, far_block, far_base, ahead, lag):
        near_wait, near_math, near_start = near
        far_wait, far_math, far_start = far
        portion = -(-tiles // ahead)

        def run(low, high, near_at=None, far_at=None, paired_at=()):
            def step(n, carry):
                nears = forwards(n + near_at) if near_at is not None else []
                fars = order(n) if far_at is not None else []
                pairings = [j for offset in paired_at for j in forwards(n + offset)]
                for j in nears:
                    near_wait(j)
                for j in fars:
                    far_wait(j)
                for j in nears:
                    near_math(j)
                for j in fars:
                    far_math(j)
                for j in pairings:
                    paired(j)
                for j in nears:
                    near_start(j)
                for j in fars:
                    far_start(j)
                if not fars:
                    lax.fori_loop(
                        n * portion, jnp.minimum((n + 1) * portion, tiles), build(far_block, far_base), 0
                    )
                return carry

            lax.fori_loop(low, high, step, 0)

        run(0, ahead, near_at=0)
        pass_calls()
        run(0, lag, near_at=ahead, far_at=0)
        run(lag, steps - ahead, near_at=ahead, far_at=0, paired_at=(-lag,))
        run(steps - ahead, steps - ahead + lag, far_at=0, paired_at=(-lag, ahead - lag) if lag else (0,))
        run(steps - ahead + lag, steps, far_at=0, paired_at=(-lag,))
        send_shares()

    def alone(near, far, order):
        near_wait, near_math, near_start = near
        far_wait, far_math, far_start = far

        def local(n, carry):
            for j in forwards(n):
                near_math(j)
                paired(j, outer=True)
            return carry

        def finish(n, carry):
            for j in order(n):
                far_wait(j)
            for j in order(n):
                far_math(j)
            return carry

        lax.fori_loop(0, tiles, build(forward_block, 0), 0)
        lax.fori_loop(0, tiles, build(backward_block, 2), 0)
        lax.fori_loop(0, steps, local, 0)
        close_calls()
        send_shares()
        lax.fori_loop(0, steps, finish, 0)

    up_stage = (up_wait, forward, up_start)
    down_stage = (down_wait, backward, down_start)

    @pl.when(first)
    def _():
        alone(up_stage, down_stage, rotated)

    @pl.when(last)
    def _():
        alone(down_stage, up_stage, forwards)

    @pl.when(here == 1)
    def _():
        lax.fori_loop(0, tiles, build(forward_block, 0), 0)
        sweep(up_stage, down_stage, rotated, backward_block, 2, AHEAD, early_steps)
        lax.fori_loop(0, EARLY, conclude, 0)

    @pl.when(here == 2)
    def _():
        lax.fori_loop(0, tiles, build(backward_block, 2), 0)
        sweep(down_stage, up_stage, forwards, forward_block, 0, BEHIND, 0)

    def chan_copy(i):
        return pltpu.make_async_remote_copy(
            src_ref=chan_out, dst_ref=chan_in.at[i - 1],
            send_sem=chan_send.at[i - 1], recv_sem=chan_recv.at[i - 1],
            device_id={"chan": lax.rem(chan + i, n_chan)}, device_id_type=MESH,
        )

    others(lambda z, n: share_arrival(z, n).wait_recv(), 0, n_seq, shares_from)
    total = shares_out[mine] + jnp.sum(shares_in[...], axis=0)
    squares_out[...] = jnp.sum(total * total, axis=0, keepdims=True)
    squared = jnp.logical_not(last)
    others(lambda z, n: square_copy(z, n).start(), 0, n_seq, lambda z: squared)
    others(lambda z, n: square_arrival(z, n).wait_recv(), 0, n_seq - 1, lambda z: here >= 0)
    chan_out[...] = jnp.sum(squares_in[...], axis=0) + squares_out[...]
    for i in range(1, n_chan):
        chan_copy(i).start()
    for i in range(1, n_chan):
        chan_copy(i).wait_recv()
    squares = jnp.sum(chan_in[...], axis=0) + chan_out[...]
    mean = jnp.sum(squares, axis=1, keepdims=True) / (taps * groups * n_chan)
    filter_update[...] = total * jnp.minimum(1.0, 1.0 / jnp.sqrt(mean + 1e-06))

    others(lambda z, n: share_copy(z, n).wait_send(), 0, n_seq - 1, shares_to)
    others(lambda z, n: square_copy(z, n).wait_send(), 0, n_seq, lambda z: squared)
    for i in range(1, n_chan):
        chan_copy(i).wait_send()

    def drain(copy, count=tiles):
        def step(j, carry):
            copy(j).wait_send()
            return carry

        lax.fori_loop(0, count, step, 0)

    @pl.when(here == 2)
    def _():
        drain(late_copy, EARLY)

    @pl.when(here + 1 < n_seq)
    def _():
        drain(up_copy)

    @pl.when(here >= 1)
    def _():
        drain(down_copy)


def store_kernel(count, *refs):
    sources, targets, sems = refs[:count], refs[count : 2 * count], refs[2 * count]
    copies = [pltpu.make_async_copy(sources[n], targets[n], sems.at[n]) for n in range(count)]
    for copy in copies:
        copy.start()
    for copy in copies:
        copy.wait()


def hub_device(sizes, gate_input, key_input, value_input, cotangent, filters, document_lengths):
    n_seq, n_batch, n_chan = sizes
    seqs, span, width = gate_input.shape
    groups, taps = filters.shape
    tiles = width // LANES
    sharers = n_seq * n_batch
    share = taps // sharers
    both = 2 * span
    per_tile = groups // tiles
    dims = (n_seq, n_batch, n_chan, tiles, seqs, span, groups, taps)
    bf16, f32 = jnp.bfloat16, jnp.float32
    vmem, anywhere = pl.BlockSpec(memory_space=pltpu.VMEM), pl.BlockSpec(memory_space=pl.ANY)
    dma = pltpu.SemaphoreType.DMA
    shape = gate_input.shape
    results = pl.pallas_call(
        functools.partial(hub_kernel, dims),
        out_shape=(pltpu.VMEM(shape, bf16),) * 4 + (pltpu.VMEM((share, groups), f32),),
        in_specs=[pl.BlockSpec(memory_space=pltpu.HBM)] * 6,
        out_specs=(vmem,) * 5,
        scratch_shapes=[
            pltpu.VMEM(shape, bf16), pltpu.VMEM(shape, bf16), pltpu.VMEM(shape, bf16), pltpu.VMEM(shape, bf16),
            pltpu.VMEM((groups, taps), f32), pltpu.SMEM(document_lengths.shape, jnp.int32),
            pltpu.VMEM((tiles, seqs, both, LANES), bf16),
            pltpu.VMEM((tiles, seqs, both, LANES), bf16),
            pltpu.VMEM((tiles, seqs, span, LANES), bf16),
            pltpu.VMEM((tiles, seqs, span, LANES), bf16),
            pltpu.VMEM((tiles, per_tile // 2, both, 2 * both), bf16),
            pltpu.VMEM((tiles, per_tile // 2, both, 2 * both), bf16),
            pltpu.VMEM((4, groups, both), f32),
            pltpu.VMEM((4, both, seqs * LANES), bf16),
            pltpu.VMEM((span, seqs * LANES), bf16),
            pltpu.VMEM((7, span, seqs * LANES), f32),
            pltpu.VMEM((tiles, per_tile, 2 * both), f32),
            pltpu.VMEM((tiles, span, seqs * LANES), f32),
            pltpu.VMEM((EARLY, seqs, span, LANES), bf16),
            pltpu.VMEM((sharers, share, groups), f32),
            pltpu.VMEM((sharers, share, groups), f32),
            pltpu.VMEM((1, groups), f32),
            pltpu.VMEM((sharers, 1, groups), f32),
            pltpu.VMEM((1, groups), f32),
            pltpu.VMEM((n_chan - 1, 1, groups), f32),
            dma((LOADS, 4)), dma((2,)),
            dma((tiles,)), dma((tiles,)), dma((tiles,)), dma((tiles,)), dma((EARLY,)), dma((EARLY,)),
            dma((sharers,)), dma((sharers,)), dma((sharers,)), dma((sharers,)),
            dma((n_chan - 1,)), dma((n_chan - 1,)),
            pltpu.SemaphoreType.REGULAR, pltpu.SemaphoreType.REGULAR,
        ],
        compiler_params=pltpu.CompilerParams(
            collective_id=0, has_side_effects=True, vmem_limit_bytes=40 * 1024 * 1024
        ),
    )(*[
        pltpu.with_memory_space_constraint(x, pltpu.HBM)
        for x in (gate_input, key_input, value_input, cotangent, filters, document_lengths)
    ])
    like = jax.ShapeDtypeStruct(shape, bf16)
    return pl.pallas_call(
        functools.partial(store_kernel, 5),
        out_shape=(like, like, like, like, jax.ShapeDtypeStruct((share, groups), f32)),
        in_specs=[vmem] * 5,
        out_specs=(anywhere,) * 5,
        scratch_shapes=[dma((5,))],
    )(*[pltpu.with_memory_space_constraint(x, pltpu.VMEM) for x in results])


def per_device(sizes, gate_input, key_input, value_input, cotangent, filters, document_lengths):
    n_seq = sizes[0]
    span, width = gate_input.shape[1:]
    groups, taps = filters.shape
    two = document_lengths.shape[1] == 2 and n_seq == 4 and taps == n_seq * span and taps % (n_seq * sizes[1]) == 0
    if two and 2 * span == LANES and (width // LANES) % LOADS == 0 and width // LANES > AHEAD * TOGETHER + EARLY:
        device = hub_device
    else:
        device = wide_device
    return device(sizes, gate_input, key_input, value_input, cotangent, filters, document_lengths)


def solution(mesh):
    block = P("batch", "seq", "chan")
    sizes = (mesh.shape["seq"], mesh.shape["batch"], mesh.shape["chan"])
    return jax.shard_map(
        functools.partial(per_device, sizes),
        mesh=mesh,
        in_specs=(block, block, block, block, P("chan", None), P("batch", None)),
        out_specs=(block, block, block, block, P(("seq", "batch"), "chan")),
        check_vma=False,
    )
```

```python
import functools

import jax
import jax.numpy as jnp
from jax import lax
from jax.experimental import pallas as pl
from jax.experimental.pallas import tpu as pltpu
from jax.sharding import PartitionSpec as P

MESH = pl.DeviceIdType.MESH
LANES = 128
HELD = 4
SHARES_AT = 4


def kernel(
    dims, gate, key, value, cotangent, filters, lengths,
    gated_output, gate_gradient, key_gradient, value_gradient, filter_update,
    units, followers, reversed_own, plain, flipped, forward_block, backward_block,
    forward_mask, backward_mask, sums_mask, tap_sums, shares_out, shares_in, squares_out, squares_in,
    chan_out, chan_in,
    unit_send, unit_recv, cot_send, cot_recv, share_send, share_recv, square_send, square_recv,
    chan_send, chan_recv,
):
    n_seq, n_batch, n_chan, reach, wide, chunks, tiles, seqs, span, groups, taps, ndocs = dims
    everyone = n_seq * n_batch * n_chan
    sharers = n_seq * n_batch
    here = lax.axis_index("seq")
    batch = lax.axis_index("batch")
    chan = lax.axis_index("chan")
    me = (here * n_batch + batch) * n_chan + chan
    mine = here * n_batch + batch
    per_tile = LANES * groups // (tiles * chunks * LANES)
    members = LANES // per_tile
    lanes = tiles * LANES
    own = reach * span
    hub = reach == 2

    barrier = pltpu.get_barrier_semaphore()

    rest = wide - own - span
    for c in range(chunks):
        for s in range(seqs):
            units[c, s, pl.ds(0, own), :] = jnp.zeros((own, lanes), jnp.bfloat16)
            units[c, s, pl.ds(own + span, rest), :] = jnp.zeros((rest, lanes), jnp.bfloat16)
            followers[c, s, pl.ds(span, wide - span), :] = jnp.zeros((wide - span, lanes), jnp.bfloat16)

    def greet(i, carry):
        other = lax.rem(me + i, everyone)
        pl.semaphore_signal(
            barrier, inc=1, device_id_type=MESH,
            device_id={
                "seq": other // (n_batch * n_chan),
                "batch": lax.rem(other // n_chan, n_batch),
                "chan": lax.rem(other, n_chan),
            },
        )
        return carry

    lax.fori_loop(1, everyone, greet, 0)

    for c in range(chunks):
        at = pl.ds(c * lanes, lanes)
        for s in range(seqs):
            u = (key[s, :, at].astype(jnp.float32) * value[s, :, at].astype(jnp.float32)).astype(jnp.bfloat16)
            g = (cotangent[s, :, at].astype(jnp.float32) * gate[s, :, at].astype(jnp.float32)).astype(jnp.bfloat16)
            units[c, s, pl.ds(own, span), :] = u
            followers[c, s, pl.ds(0, span), :] = g

    def unit_copy(lag, c):
        source = units.at[c, :, pl.ds((reach - lag + 1) * span, span), :]
        target = units.at[c, :, pl.ds((reach - lag) * span, span), :]
        return pltpu.make_async_remote_copy(
            src_ref=source, dst_ref=target, send_sem=unit_send.at[lag - 1, c], recv_sem=unit_recv.at[lag - 1, c],
            device_id={"seq": here + 1}, device_id_type=MESH,
        )

    def cot_copy(lag, c):
        source = followers.at[c, :, pl.ds((lag - 1) * span, span), :]
        target = followers.at[c, :, pl.ds(lag * span, span), :]
        return pltpu.make_async_remote_copy(
            src_ref=source, dst_ref=target, send_sem=cot_send.at[lag - 1, c], recv_sem=cot_recv.at[lag - 1, c],
            device_id={"seq": here - 1}, device_id_type=MESH,
        )

    def sends_up(lag):
        return (here >= lag - 1) & (here + 1 < n_seq)

    def sends_down(lag):
        return (here + lag - 1 < n_seq) & (here >= 1)

    def send(lag, c):
        @pl.when(sends_up(lag))
        def _():
            unit_copy(lag, c).start()

        @pl.when(sends_down(lag))
        def _():
            cot_copy(lag, c).start()

    def receive(lag, c):
        @pl.when(here >= lag)
        def _():
            unit_copy(lag, c).wait_recv()

        @pl.when(here + lag < n_seq)
        def _():
            cot_copy(lag, c).wait_recv()

    pl.semaphore_wait(barrier, everyone - 1)
    for c in range(chunks):
        send(1, c)

    def documents(positions, s):
        count = jnp.zeros(positions.shape, jnp.int32)
        end = 0
        for n in range(ndocs):
            end = end + lengths[s, n]
            count = count + (positions >= end).astype(jnp.int32)
        return count

    rows = lax.broadcasted_iota(jnp.int32, (span, 1), 0)
    cols = lax.broadcasted_iota(jnp.int32, (1, wide), 1)
    for s in range(seqs):
        earlier = (here - reach) * span + cols
        later = here * span + cols
        target = here * span + rows
        back = here * span + (span - 1 - rows)
        earlier_doc = documents(earlier, s)
        later_doc = documents(later, s)
        target_doc = documents(target, s)
        back_doc = documents(back, s)
        keep = (earlier_doc == target_doc) & (earlier <= target) & (earlier >= 0)
        forward_mask[s] = jnp.where(keep, 1.0, 0.0).astype(jnp.bfloat16)
        if hub:
            first = cols < span
            origin = jnp.where(first, earlier + span, earlier)
            goal = jnp.where(first, back + span, back)
            goal_doc = jnp.where(first, documents(back + span, s), back_doc)
            keep = (documents(origin, s) == goal_doc) & (origin <= goal) & (origin >= 0) & (goal < n_seq * span)
        else:
            keep = (earlier_doc == back_doc) & (earlier <= back) & (earlier >= 0)
        sums_mask[s] = jnp.where(keep, 1.0, 0.0)
        keep = (later_doc == target_doc) & (later >= target) & (later < n_seq * span)
        backward_mask[s] = jnp.where(keep, 1.0, 0.0).astype(jnp.bfloat16)

    rounded = filters[...].astype(jnp.bfloat16)
    a = lax.broadcasted_iota(jnp.int32, (taps, wide), 0)
    b = lax.broadcasted_iota(jnp.int32, (taps, wide), 1)
    flip = own - b
    flip = jnp.where(flip < 0, flip + wide, flip)
    plain[...] = jnp.dot(rounded, jnp.where(a == b, 1.0, 0.0).astype(jnp.bfloat16), preferred_element_type=jnp.float32)
    flipped[...] = jnp.dot(rounded, jnp.where(a == flip, 1.0, 0.0).astype(jnp.bfloat16), preferred_element_type=jnp.float32)

    def build(t, carry):
        for i in range(per_tile):
            g = t * per_tile + i
            at = pl.ds(pl.multiple_of(g * span, span), span)
            row = jnp.broadcast_to(flipped[pl.ds(g, 1), :], (span, wide))
            forward_block[at, :] = pltpu.roll(row, 0, 1, stride=1, stride_axis=0).astype(jnp.bfloat16)
            row = jnp.broadcast_to(plain[pl.ds(g, 1), :], (span, wide))
            backward_block[at, :] = pltpu.roll(row, 0, 1, stride=1, stride_axis=0).astype(jnp.bfloat16)
        return carry

    order_a = lax.broadcasted_iota(jnp.int32, (span, span), 0)
    order_b = lax.broadcasted_iota(jnp.int32, (span, span), 1)
    exchange = jnp.where(order_a + order_b == span - 1, 1.0, 0.0).astype(jnp.bfloat16)
    lane = lax.broadcasted_iota(jnp.int32, (1, LANES), 1) // members

    def members_apart(block):
        return jnp.concatenate(
            [block * jnp.where(lane == i, 1.0, 0.0).astype(jnp.bfloat16) for i in range(per_tile)], axis=0
        )

    def paired(c, j, carry):
        at = pl.ds(pl.multiple_of(j * LANES, LANES), LANES)
        total = None
        for s in range(seqs):
            target = members_apart(reversed_own[c, s, pl.ds(0, span), at])
            if hub:
                target = jnp.concatenate([target, members_apart(reversed_own[c, s, pl.ds(span, span), at])], axis=1)
                past = units[c, s, pl.ds(own - span, span), at]
                blank = jnp.zeros((span, LANES), jnp.bfloat16)
                tail = jnp.zeros((wide - own - span, LANES), jnp.bfloat16)
                source = jnp.concatenate(
                    [
                        jnp.concatenate([blank, past, units[c, s, pl.ds(own, span), at], tail], axis=0),
                        jnp.concatenate([past, blank, blank, tail], axis=0),
                    ],
                    axis=1,
                )
            else:
                source = units[c, s, :, at]
            products = lax.dot_general(
                target, source, (((1,), (1,)), ((), ())), preferred_element_type=jnp.float32
            ).reshape(per_tile, span, wide)
            products = products * sums_mask[s][None]
            total = products if total is None else total + products
        for i in range(per_tile):
            aligned = pltpu.roll(total[i], 0, 1, stride=1, stride_axis=0)
            tap_sums[pl.ds((c * tiles + j) * per_tile + i, 1), :] = jnp.sum(aligned, axis=0, keepdims=True)
        return carry

    def reverse(c):
        for s in range(seqs):
            for n in range(2 if hub else 1):
                at = pl.ds(n * span, span)
                reversed_own[c, s, at, :] = jnp.dot(
                    exchange, followers[c, s, at, :], preferred_element_type=jnp.float32
                ).astype(jnp.bfloat16)

    for c in range(chunks):
        lax.fori_loop(c * tiles, (c + 1) * tiles, build, 0)
        for lag in range(1, reach):
            receive(lag, c)
            if not (hub and c >= HELD):
                send(lag + 1, c)
        if hub:
            reverse(c)
            lax.fori_loop(0, tiles, functools.partial(paired, c), 0)
    if not hub:
        for c in range(chunks):
            receive(reach, c)
            reverse(c)
            lax.fori_loop(0, tiles, functools.partial(paired, c), 0)

    a = lax.broadcasted_iota(jnp.int32, (taps, wide), 0)
    b = lax.broadcasted_iota(jnp.int32, (taps, wide), 1)
    pick = jnp.where(a + b == own + span - 1, 1.0, 0.0)
    by_tap = lax.dot_general(
        pick, tap_sums[...], (((1,), (1,)), ((), ())),
        precision=lax.Precision.HIGHEST, preferred_element_type=jnp.float32,
    )
    share = taps // sharers
    for i in range(sharers):
        shares_out[i] = by_tap[i * share : (i + 1) * share, :]

    def share_copy(i):
        other = lax.rem(mine + i, sharers)
        return pltpu.make_async_remote_copy(
            src_ref=shares_out.at[other], dst_ref=shares_in.at[i - 1],
            send_sem=share_send.at[i - 1], recv_sem=share_recv.at[i - 1],
            device_id={"seq": other // n_batch, "batch": lax.rem(other, n_batch)}, device_id_type=MESH,
        )

    def square_copy(i):
        other = lax.rem(mine + i, sharers)
        return pltpu.make_async_remote_copy(
            src_ref=squares_out, dst_ref=squares_in.at[i - 1],
            send_sem=square_send.at[i - 1], recv_sem=square_recv.at[i - 1],
            device_id={"seq": other // n_batch, "batch": lax.rem(other, n_batch)}, device_id_type=MESH,
        )

    def chan_copy(i):
        return pltpu.make_async_remote_copy(
            src_ref=chan_out, dst_ref=chan_in.at[i - 1],
            send_sem=chan_send.at[i - 1], recv_sem=chan_recv.at[i - 1],
            device_id={"chan": lax.rem(chan + i, n_chan)}, device_id_type=MESH,
        )

    def loop(low, high, act):
        if high <= 32:
            for i in range(low, high):
                act(i)
            return

        def step(i, carry):
            act(i)
            return carry

        lax.fori_loop(low, high, step, 0)

    def convolve(c, j, carry):
        at = pl.ds(pl.multiple_of(j * LANES, LANES), LANES)
        t = c * tiles + j
        out = pl.ds(pl.multiple_of(t * LANES, LANES), LANES)
        height = per_tile * span
        block = pl.ds(pl.multiple_of(t * height, height), height)

        def apply(block_ref, mask_ref, data_ref, s):
            masked = block_ref[block, :].reshape(per_tile, span, wide) * mask_ref[s][None]
            results = jnp.dot(
                masked.reshape(height, wide), data_ref[c, s, :, at], preferred_element_type=jnp.float32
            )
            picked = results[:span]
            for i in range(1, per_tile):
                picked = jnp.where(lane == i, results[i * span : (i + 1) * span], picked)
            return picked

        for s in range(seqs):
            filtered = apply(forward_block, forward_mask, units, s)
            gated_output[s, :, out] = (gate[s, :, out].astype(jnp.float32) * filtered).astype(jnp.bfloat16)
            gate_gradient[s, :, out] = (cotangent[s, :, out].astype(jnp.float32) * filtered).astype(jnp.bfloat16)
            adjoint = apply(backward_block, backward_mask, followers, s)
            key_gradient[s, :, out] = (adjoint * value[s, :, out].astype(jnp.float32)).astype(jnp.bfloat16)
            value_gradient[s, :, out] = (adjoint * key[s, :, out].astype(jnp.float32)).astype(jnp.bfloat16)
        return carry

    loop(1, sharers, lambda i: share_copy(i).start())
    if hub:
        for c in range(HELD, chunks):
            send(reach, c)
    for c in range(chunks):
        if hub:
            receive(reach, c)
        if c == SHARES_AT:
            loop(1, sharers, lambda i: share_copy(i).wait_recv())
            total = shares_out[mine] + jnp.sum(shares_in[...], axis=0)
            filter_update[...] = total
            squares_out[...] = jnp.sum(total * total, axis=0, keepdims=True)
        if c == SHARES_AT + 1:
            loop(1, sharers, lambda i: square_copy(i).start())
        lax.fori_loop(0, tiles, functools.partial(convolve, c), 0)
    loop(1, sharers, lambda i: square_copy(i).wait_recv())
    chan_out[...] = jnp.sum(squares_in[...], axis=0) + squares_out[...]
    loop(1, sharers, lambda i: share_copy(i).wait_send())
    loop(1, sharers, lambda i: square_copy(i).wait_send())
    loop(1, n_chan, lambda i: chan_copy(i).start())
    loop(1, n_chan, lambda i: chan_copy(i).wait_recv())
    squares = jnp.sum(chan_in[...], axis=0) + chan_out[...]
    mean = jnp.sum(squares, axis=1, keepdims=True) / (taps * groups * n_chan)
    filter_update[...] = filter_update[...] * jnp.minimum(1.0, 1.0 / jnp.sqrt(mean + 1e-06))
    loop(1, n_chan, lambda i: chan_copy(i).wait_send())
    for lag in range(1, reach + 1):
        @pl.when(sends_up(lag))
        def _():
            for c in range(chunks):
                unit_copy(lag, c).wait_send()

        @pl.when(sends_down(lag))
        def _():
            for c in range(chunks):
                cot_copy(lag, c).wait_send()


def wide_device(sizes, gate_input, key_input, value_input, cotangent, filters, document_lengths):
    n_seq, n_batch, n_chan = sizes
    seqs, span, width = gate_input.shape
    groups, taps = filters.shape
    ndocs = document_lengths.shape[1]
    longest = min(taps, n_seq * span - span)
    reach = (longest - 1) // span if ndocs == 2 else (longest - 2) // span + 1
    wide = -(-((reach + 2) * span - 1) // LANES) * LANES
    chunks = 8
    tiles = width // (chunks * LANES)
    lanes = tiles * LANES
    sharers = n_seq * n_batch
    share = taps // sharers
    dims = (n_seq, n_batch, n_chan, reach, wide, chunks, tiles, seqs, span, groups, taps, ndocs)
    bf16, f32 = jnp.bfloat16, jnp.float32
    vmem = pl.BlockSpec(memory_space=pltpu.VMEM)
    dma = pltpu.SemaphoreType.DMA
    like = jax.ShapeDtypeStruct(gate_input.shape, bf16)
    return pl.pallas_call(
        functools.partial(kernel, dims),
        out_shape=(like, like, like, like, jax.ShapeDtypeStruct((share, groups), f32)),
        in_specs=[vmem] * 5 + [pl.BlockSpec(memory_space=pltpu.SMEM)],
        out_specs=(vmem,) * 5,
        scratch_shapes=[
            pltpu.VMEM((chunks, seqs, wide, lanes), bf16),
            pltpu.VMEM((chunks, seqs, wide, lanes), bf16),
            pltpu.VMEM((chunks, seqs, 2 * span, lanes), bf16),
            pltpu.VMEM((groups, wide), f32),
            pltpu.VMEM((groups, wide), f32),
            pltpu.VMEM((groups * span, wide), bf16),
            pltpu.VMEM((groups * span, wide), bf16),
            pltpu.VMEM((seqs, span, wide), bf16),
            pltpu.VMEM((seqs, span, wide), bf16),
            pltpu.VMEM((seqs, span, wide), f32),
            pltpu.VMEM((groups, wide), f32),
            pltpu.VMEM((sharers, share, groups), f32),
            pltpu.VMEM((sharers - 1, share, groups), f32),
            pltpu.VMEM((1, groups), f32),
            pltpu.VMEM((sharers - 1, 1, groups), f32),
            pltpu.VMEM((1, groups), f32),
            pltpu.VMEM((n_chan - 1, 1, groups), f32),
            dma((reach, chunks)), dma((reach, chunks)), dma((reach, chunks)), dma((reach, chunks)),
            dma((sharers - 1,)), dma((sharers - 1,)), dma((sharers - 1,)), dma((sharers - 1,)),
            dma((n_chan - 1,)), dma((n_chan - 1,)),
        ],
        compiler_params=pltpu.CompilerParams(
            collective_id=0, has_side_effects=True, vmem_limit_bytes=60 * 1024 * 1024
        ),
    )(gate_input, key_input, value_input, cotangent, filters, document_lengths)


AHEAD = 3
BEHIND = 2
TOGETHER = 2
LOADS = 8
EARLY = 6


def hub_kernel(
    dims, gate_hbm, key_hbm, value_hbm, cotangent_hbm, filters_hbm, lengths_hbm,
    gated_output, gate_gradient, key_gradient, value_gradient, filter_update,
    gate, key, value, cotangent, filters, lengths, units, followers, up_out, down_out,
    forward_block, backward_block, bases, wide_masks, half_masks, blends, tap_sums, kept, late_in,
    shares_out, shares_in, squares_out, squares_in, chan_out, chan_in, cross_in,
    load_sem, small_sem, up_send, up_recv, down_send, down_recv, late_send, late_recv, share_send, share_recv, square_send, square_recv,
    chan_send, chan_recv, cross_send, cross_recv, up_call, down_call,
):
    n_seq, n_batch, n_chan, tiles, seqs, span, groups, taps = dims
    sharers = n_seq * n_batch
    here = lax.axis_index("seq")
    batch = lax.axis_index("batch")
    chan = lax.axis_index("chan")
    mine = here * n_batch + batch
    per_tile = groups // tiles
    members = LANES // per_tile
    both = 2 * span
    f32, bf16 = jnp.float32, jnp.bfloat16

    part = tiles // LOADS * LANES

    def loads(q):
        at = pl.ds(q * part, part)
        pairs = ((key_hbm, key), (value_hbm, value), (cotangent_hbm, cotangent), (gate_hbm, gate))
        return [
            pltpu.make_async_copy(src.at[:, :, at], dst.at[:, :, at], load_sem.at[q, n])
            for n, (src, dst) in enumerate(pairs)
        ]

    for q in range(LOADS):
        for copy in loads(q):
            copy.start()

    filters_copy = pltpu.make_async_copy(filters_hbm, filters, small_sem.at[0])
    lengths_copy = pltpu.make_async_copy(lengths_hbm, lengths, small_sem.at[1])
    lengths_copy.start()
    filters_copy.start()
    shares_in[...] = jnp.zeros(shares_in.shape, f32)
    squares_in[...] = jnp.zeros(squares_in.shape, f32)
    chan_in[...] = jnp.zeros(chan_in.shape, f32)
    cross_in[...] = jnp.zeros(cross_in.shape, f32)
    beyond = (n_seq - 1) * n_batch
    shares_out[pl.ds(beyond, n_batch)] = jnp.zeros((n_batch,) + shares_out.shape[1:], f32)

    first, last = here == 0, here == n_seq - 1
    barrier = pltpu.get_barrier_semaphore()

    def greet(device):
        pl.semaphore_signal(barrier, inc=1, device_id_type=MESH, device_id=device)

    @pl.when(jnp.logical_not(first))
    def _():
        greet({"seq": here - 1})

    @pl.when(jnp.logical_not(last))
    def _():
        greet({"seq": here + 1})

    for i in range(1, n_batch):
        greet({"batch": lax.rem(batch + i, n_batch)})
    for i in range(1, n_chan):
        greet({"chan": lax.rem(chan + i, n_chan)})
    greeted = n_batch - 1 + n_chan - 1 + jnp.where(first | last, 1, 2)

    def call(semaphore, target):
        pl.semaphore_signal(semaphore, inc=1, device_id_type=MESH, device_id={"seq": target})

    def open_calls():
        @pl.when(first)
        def _():
            call(up_call, here + 1)

        @pl.when(last)
        def _():
            call(down_call, here - 1)

    def pass_calls():
        pl.semaphore_wait(up_call, 1)
        call(up_call, here + 1)
        pl.semaphore_wait(down_call, 1)
        call(down_call, here - 1)

    def close_calls():
        @pl.when(first)
        def _():
            pl.semaphore_wait(down_call, 1)

        @pl.when(last)
        def _():
            pl.semaphore_wait(up_call, 1)

    hub = jnp.logical_not(first | last)
    own_units = units.at[:, :, pl.ds(span, span), :]
    own_cots = followers.at[:, :, pl.ds(0, span), :]

    def up_copy(j, source=up_out):
        return pltpu.make_async_remote_copy(
            src_ref=source.at[j], dst_ref=units.at[j, :, pl.ds(0, span), :],
            send_sem=up_send.at[j], recv_sem=up_recv.at[j], device_id={"seq": here + 1}, device_id_type=MESH,
        )

    def down_copy(j, source=down_out):
        return pltpu.make_async_remote_copy(
            src_ref=source.at[j], dst_ref=followers.at[j, :, pl.ds(span, span), :],
            send_sem=down_send.at[j], recv_sem=down_recv.at[j], device_id={"seq": here - 1}, device_id_type=MESH,
        )

    held_back = tiles - EARLY

    def late_copy(k):
        return pltpu.make_async_remote_copy(
            src_ref=down_out.at[held_back + k], dst_ref=late_in.at[k],
            send_sem=late_send.at[k], recv_sem=late_recv.at[k], device_id={"seq": here - 1}, device_id_type=MESH,
        )

    def gather(j, carry):
        at = pl.ds(pl.multiple_of(j * LANES, LANES), LANES)
        for s in range(seqs):
            u = (key[s, :, at].astype(f32) * value[s, :, at].astype(f32)).astype(bf16)
            g = (cotangent[s, :, at].astype(f32) * gate[s, :, at].astype(f32)).astype(bf16)
            units[j, s, pl.ds(span, span), :] = u
            followers[j, s, pl.ds(0, span), :] = g

        @pl.when(first)
        def _():
            up_copy(j, own_units).start()
            for s in range(seqs):
                units[j, s, pl.ds(0, span), :] = jnp.zeros((span, LANES), bf16)

        @pl.when(last)
        def _():
            down_copy(j, own_cots).start()
            for s in range(seqs):
                followers[j, s, pl.ds(span, span), :] = jnp.zeros((span, LANES), bf16)

        @pl.when((here == 2) & (j >= held_back))
        def _():
            down_copy(j, own_cots).start()

        return carry

    for q in range(LOADS):
        for copy in loads(q):
            copy.wait()
        if q == 0:
            pl.semaphore_wait(barrier, greeted)
            open_calls()
        lax.fori_loop(q * (tiles // LOADS), (q + 1) * (tiles // LOADS), gather, 0)

    lengths_copy.wait()
    filters_copy.wait()

    main = jnp.where(here * 2 >= n_seq, 1, 0)
    rows = lax.broadcasted_iota(jnp.int32, (both, LANES), 0)
    half = lax.broadcasted_iota(jnp.int32, (span, LANES), 0)
    one, zero = jnp.ones((), f32), jnp.zeros((), f32)

    def flag(condition):
        return jnp.where(condition, one, zero)

    for s in range(seqs):
        end = lengths[s, 0]
        at = pl.ds(s * LANES, LANES)

        def is_main(positions):
            return jnp.where(positions >= end, 1, 0) == main

        in_front = end <= both
        past_held = (here == 1) | ((here == 2) & in_front)
        next_held = (here == 2) | ((here == 1) & jnp.logical_not(in_front))
        past = (here - 1) * span
        own_main = is_main(here * span + half)
        back = both - 1 - rows
        wide_masks[0, :, at] = flag(is_main(past + rows) & ((rows >= span) | past_held)).astype(bf16)
        wide_masks[1, :, at] = flag(is_main(here * span + rows) & ((rows < span) | next_held)).astype(bf16)
        wide_masks[2, :, at] = flag(is_main(past + back) & ((back >= span) | past_held)).astype(bf16)
        wide_masks[3, :, at] = flag(jnp.logical_not(is_main(past + back)) & (back >= span)).astype(bf16)
        half_masks[:, at] = flag(jnp.logical_not(own_main)).astype(bf16)
        relay = flag((here == 1) & in_front)
        blends[0, :, at] = flag(own_main)
        blends[1, :, at] = jnp.broadcast_to(relay, (span, LANES))
        blends[2, :, at] = (1.0 - relay) * flag(is_main((here + 1) * span + half))
        blends[3, :, at] = jnp.broadcast_to(flag((here == 3) | ((here == 2) & jnp.logical_not(in_front))), (span, LANES))
        relay = flag((here == 2) & jnp.logical_not(in_front))
        blends[4, :, at] = jnp.broadcast_to(relay, (span, LANES))
        blends[5, :, at] = (1.0 - relay) * flag(is_main(past + half))
        blends[6, :, at] = jnp.broadcast_to(flag((here == 0) | ((here == 1) & in_front)), (span, LANES))

    rounded = filters[...].astype(bf16)
    a = lax.broadcasted_iota(jnp.int32, (taps, both), 0)
    b = lax.broadcasted_iota(jnp.int32, (taps, both), 1)
    for n, at in enumerate((span - b, span + both - b, span + b, b - span)):
        bases[n] = jnp.dot(rounded, flag(a == at).astype(bf16), preferred_element_type=f32)

    square_rows = lax.broadcasted_iota(jnp.int32, (both, both), 0)
    square_cols = lax.broadcasted_iota(jnp.int32, (both, both), 1)
    unwrapped = square_cols < both - square_rows

    def build(block, n):
        def tile(t, carry):
            for i in range(per_tile):
                g = pl.ds(t * per_tile + i, 1)
                row = jnp.where(unwrapped, bases[n, g, :], bases[n + 1, g, :])
                rolled = pltpu.roll(row, 0, 1, stride=1, stride_axis=0)
                block[t, i // 2, :, pl.ds(i % 2 * both, both)] = rolled.astype(bf16)
            return carry

        return tile

    pairs = per_tile // 2
    wide = seqs * LANES
    lane = lax.rem(lax.broadcasted_iota(jnp.int32, (1, wide), 1), LANES) // members
    parity = [flag(lax.rem(lane, 2) == e).astype(bf16) for e in range(2)]
    pair_masks = [flag(lane // 2 == k).astype(bf16) for k in range(pairs)]
    blank = jnp.zeros((span, wide), bf16)

    def across(ref, j, at):
        return jnp.concatenate([ref[j, s, at, :] for s in range(seqs)], axis=1)

    def own_lanes(results, height):
        picked = results[:height]
        for k in range(1, pairs):
            picked = jnp.where(lane // 2 == k, results[k * height : (k + 1) * height], picked)
        return picked

    def apply(block, data):
        height = block.shape[1]
        results = jnp.dot(block.reshape(pairs * height, 2 * both), data, preferred_element_type=f32)
        return own_lanes(results, height)

    whole, low, top = pl.ds(0, both), pl.ds(0, span), pl.ds(span, span)

    def forward(j):
        at = pl.ds(pl.multiple_of(j * LANES, LANES), LANES)
        window = across(units, j, whole)
        held = window * wide_masks[0]
        other = window[span:] * half_masks[...]
        result = apply(forward_block[j], jnp.concatenate([held * p for p in parity], axis=0))
        rest = apply(
            forward_block[j, :, low, :],
            jnp.concatenate([blank, other * parity[0], blank, other * parity[1]], axis=0),
        )
        sent = (blends[1] * window[span:].astype(f32) + blends[2] * result[span:]).astype(bf16)
        filtered = jnp.where(blends[0] > 0.5, result[:span], rest) + blends[3] * window[:span].astype(f32)
        for s in range(seqs):
            mine_at = slice(s * LANES, (s + 1) * LANES)
            up_out[j, s] = sent[:, mine_at]
            gated_output[s, :, at] = (gate[s, :, at].astype(f32) * filtered[:, mine_at]).astype(bf16)
            gate_gradient[s, :, at] = (cotangent[s, :, at].astype(f32) * filtered[:, mine_at]).astype(bf16)

    def backward(j):
        at = pl.ds(pl.multiple_of(j * LANES, LANES), LANES)
        window = across(followers, j, whole)
        held = window * wide_masks[1]
        other = window[:span] * half_masks[...]
        result = apply(backward_block[j], jnp.concatenate([held * p for p in parity], axis=0))
        rest = apply(
            backward_block[j, :, top, :],
            jnp.concatenate([other * parity[0], blank, other * parity[1], blank], axis=0),
        )
        late = jnp.where(j >= held_back, one, zero)
        relayed = (1.0 - late) * blends[4]
        added = (1.0 - late * flag(here == 1)) * blends[6]
        sent = (relayed * window[:span].astype(f32) + blends[5] * result[:span]).astype(bf16)
        adjoint = jnp.where(blends[0] > 0.5, result[span:], rest) + added * window[span:].astype(f32)
        kept[j] = adjoint
        for s in range(seqs):
            mine_at = slice(s * LANES, (s + 1) * LANES)
            down_out[j, s] = sent[:, mine_at]
            key_gradient[s, :, at] = (adjoint[:, mine_at] * value[s, :, at].astype(f32)).astype(bf16)
            value_gradient[s, :, at] = (adjoint[:, mine_at] * key[s, :, at].astype(f32)).astype(bf16)

    def conclude(k, carry):
        late_copy(k).wait_recv()
        j = held_back + k
        at = pl.ds(pl.multiple_of(j * LANES, LANES), LANES)
        for s in range(seqs):
            adjoint = kept[j, :, pl.ds(s * LANES, LANES)] + late_in[k, s].astype(f32)
            key_gradient[s, :, at] = (adjoint * value[s, :, at].astype(f32)).astype(bf16)
            value_gradient[s, :, at] = (adjoint * key[s, :, at].astype(f32)).astype(bf16)
        return carry

    exchange = flag(square_rows + square_cols == both - 1).astype(bf16)
    wrapped = flag(square_cols < square_rows)

    def paired(j, outer=False):
        source = jnp.concatenate([blank, across(units, j, top)], axis=0) if outer else across(units, j, whole)
        reversed_units = jnp.dot(exchange, source, preferred_element_type=f32).astype(bf16)
        held = reversed_units * wide_masks[2]
        other = reversed_units * wide_masks[3]
        sources = jnp.concatenate(
            [jnp.concatenate([x * p for p in parity], axis=0) for x in (held, other)], axis=1
        )
        window = across(followers, j, low if outer else whole)
        held = window * (wide_masks[1, low, :] if outer else wide_masks[1])
        other = window[:span] * half_masks[...]

        def by_pair(x):
            repeat = x.shape[1] // wide
            return jnp.concatenate([x * jnp.concatenate([m] * repeat, axis=1) for m in pair_masks], axis=0)

        contract = (((1,), (1,)), ((), ()))
        own = lax.dot_general(
            by_pair(jnp.concatenate([held[:span], other], axis=1)), sources, contract, preferred_element_type=f32
        )
        if not outer:
            next_ones = lax.dot_general(by_pair(held[span:]), sources[:, :wide], contract, preferred_element_type=f32)
        for i in range(per_tile):
            at = slice(i // 2 * span, (i // 2 + 1) * span)
            across_at = slice(i % 2 * both, (i % 2 + 1) * both)
            near = pltpu.roll(own[at, across_at], 0, 1, stride=1, stride_axis=0)
            total, high = near, near * wrapped[:span]
            if not outer:
                far = pltpu.roll(next_ones[at, across_at], span, 1, stride=1, stride_axis=0)
                total, high = total + far, high + far * wrapped[span:]
            total = jnp.sum(total, axis=0, keepdims=True)
            high = jnp.sum(high, axis=0, keepdims=True)
            tap_sums[j, pl.ds(i, 1), pl.ds(0, both)] = total - high
            tap_sums[j, pl.ds(i, 1), pl.ds(both, both)] = high

    def up_wait(j):
        @pl.when(jnp.logical_not(first))
        def _():
            up_copy(j).wait_recv()

    def down_wait(j):
        @pl.when(jnp.logical_not(last))
        def _():
            down_copy(j).wait_recv()

    def up_start(j):
        @pl.when(hub)
        def _():
            up_copy(j).start()

    def down_start(j):
        @pl.when((here == 1) | ((here == 2) & (j < held_back)))
        def _():
            down_copy(j).start()

        @pl.when((here == 2) & (j >= held_back))
        def _():
            late_copy(jnp.maximum(j - held_back, 0)).start()

    steps = tiles // TOGETHER
    early_steps = EARLY // TOGETHER

    def forwards(n):
        return [n * TOGETHER + k for k in range(TOGETHER)]

    def rotated(n):
        return forwards(lax.rem(n + steps - early_steps, steps))

    spread = (n_seq - 1) * span
    a = lax.broadcasted_iota(jnp.int32, (spread, 2 * both), 0)
    b = lax.broadcasted_iota(jnp.int32, (spread, 2 * both), 1)
    pick = flag(((a == b - (span - 1)) & (b < both)) | ((a == b - both + span + 1) & (b >= both))).astype(bf16)
    share = taps // sharers

    def share_copy(z, n):
        return pltpu.make_async_remote_copy(
            src_ref=shares_out.at[z * n_batch + n], dst_ref=shares_in.at[mine],
            send_sem=share_send.at[z * n_batch + n], recv_sem=share_recv.at[mine],
            device_id={"seq": z, "batch": n}, device_id_type=MESH,
        )

    def share_arrival(z, n):
        at = z * n_batch + n
        return pltpu.make_async_remote_copy(
            src_ref=shares_out.at[at], dst_ref=shares_in.at[at], send_sem=share_send.at[at],
            recv_sem=share_recv.at[at], device_id={"seq": z, "batch": n}, device_id_type=MESH,
        )

    def square_copy(z, n):
        return pltpu.make_async_remote_copy(
            src_ref=squares_out, dst_ref=squares_in.at[mine],
            send_sem=square_send.at[z * n_batch + n], recv_sem=square_recv.at[mine],
            device_id={"seq": z, "batch": n}, device_id_type=MESH,
        )

    def square_arrival(z, n):
        at = z * n_batch + n
        return pltpu.make_async_remote_copy(
            src_ref=squares_out, dst_ref=squares_in.at[at], send_sem=square_send.at[at],
            recv_sem=square_recv.at[at], device_id={"seq": z, "batch": n}, device_id_type=MESH,
        )

    def others(act, low, high, allowed):
        for z in range(low, high):
            for n in range(n_batch):
                @pl.when(allowed(z) & (mine != z * n_batch + n))
                def _():
                    act(z, n)

    def shares_to(z):
        return hub if z > 0 else hub | first | last

    def shares_from(z):
        return (first | hub) & (here < n_seq - 1) if 0 < z < n_seq - 1 else first

    def send_shares():
        sums = tap_sums[...].reshape(groups, 2 * both)
        by_tap = jnp.zeros((spread, groups), f32)
        for _ in range(3):
            piece = sums.astype(bf16)
            sums = sums - piece.astype(f32)
            by_tap = by_tap + lax.dot_general(pick, piece, (((1,), (1,)), ((), ())), preferred_element_type=f32)
        for i in range(spread // share):
            shares_out[i] = by_tap[i * share : (i + 1) * share, :]
        others(lambda z, n: share_copy(z, n).start(), 0, n_seq - 1, shares_to)

    def sweep(near, far, order, far_block, far_base, ahead, lag):
        near_wait, near_math, near_start = near
        far_wait, far_math, far_start = far
        portion = -(-tiles // ahead)

        def run(low, high, near_at=None, far_at=None, paired_at=()):
            def step(n, carry):
                nears = forwards(n + near_at) if near_at is not None else []
                fars = order(n) if far_at is not None else []
                pairings = [j for offset in paired_at for j in forwards(n + offset)]
                for j in nears:
                    near_wait(j)
                for j in fars:
                    far_wait(j)
                for j in nears:
                    near_math(j)
                for j in fars:
                    far_math(j)
                for j in pairings:
                    paired(j)
                for j in nears:
                    near_start(j)
                for j in fars:
                    far_start(j)
                if not fars:
                    lax.fori_loop(
                        n * portion, jnp.minimum((n + 1) * portion, tiles), build(far_block, far_base), 0
                    )
                return carry

            lax.fori_loop(low, high, step, 0)

        run(0, ahead, near_at=0)
        pass_calls()
        run(0, lag, near_at=ahead, far_at=0)
        run(lag, steps - ahead, near_at=ahead, far_at=0, paired_at=(-lag,))
        run(steps - ahead, steps - ahead + lag, far_at=0, paired_at=(-lag, ahead - lag) if lag else (0,))
        run(steps - ahead + lag, steps, far_at=0, paired_at=(-lag,))
        send_shares()

    def alone(near, far, order):
        near_wait, near_math, near_start = near
        far_wait, far_math, far_start = far

        def local(n, carry):
            for j in forwards(n):
                near_math(j)
                paired(j, outer=True)
            return carry

        def finish(n, carry):
            for j in order(n):
                far_wait(j)
            for j in order(n):
                far_math(j)
            return carry

        lax.fori_loop(0, tiles, build(forward_block, 0), 0)
        lax.fori_loop(0, tiles, build(backward_block, 2), 0)
        lax.fori_loop(0, steps, local, 0)
        close_calls()
        send_shares()
        lax.fori_loop(0, steps, finish, 0)

    up_stage = (up_wait, forward, up_start)
    down_stage = (down_wait, backward, down_start)

    @pl.when(first)
    def _():
        alone(up_stage, down_stage, rotated)

    @pl.when(last)
    def _():
        alone(down_stage, up_stage, forwards)

    @pl.when(here == 1)
    def _():
        lax.fori_loop(0, tiles, build(forward_block, 0), 0)
        sweep(up_stage, down_stage, rotated, backward_block, 2, AHEAD, early_steps)
        lax.fori_loop(0, EARLY, conclude, 0)

    @pl.when(here == 2)
    def _():
        lax.fori_loop(0, tiles, build(backward_block, 2), 0)
        sweep(down_stage, up_stage, forwards, forward_block, 0, BEHIND, 0)

    def chan_copy(i):
        return pltpu.make_async_remote_copy(
            src_ref=chan_out, dst_ref=chan_in.at[i - 1],
            send_sem=chan_send.at[i - 1], recv_sem=chan_recv.at[i - 1],
            device_id={"chan": lax.rem(chan + i, n_chan)}, device_id_type=MESH,
        )

    others(lambda z, n: share_arrival(z, n).wait_recv(), 0, n_seq, shares_from)
    total = shares_out[mine] + jnp.sum(shares_in[...], axis=0)
    squares_out[...] = jnp.sum(total * total, axis=0, keepdims=True)
    squared = jnp.logical_not(last)
    origin = mine == 0

    def cross_copy(i):
        return pltpu.make_async_remote_copy(
            src_ref=squares_out, dst_ref=cross_in.at[i - 1, mine],
            send_sem=cross_send.at[i - 1], recv_sem=cross_recv.at[i - 1, mine],
            device_id={"seq": 0, "batch": 0, "chan": lax.rem(chan + i, n_chan)}, device_id_type=MESH,
        )

    def cross_arrival(i, at):
        return pltpu.make_async_remote_copy(
            src_ref=squares_out, dst_ref=cross_in.at[i - 1, at],
            send_sem=cross_send.at[i - 1], recv_sem=cross_recv.at[i - 1, at],
            device_id={"seq": 0, "batch": 0, "chan": lax.rem(chan + i, n_chan)}, device_id_type=MESH,
        )

    @pl.when(squared)
    def _():
        for i in range(1, n_chan):
            cross_copy(i).start()

    others(lambda z, n: square_copy(z, n).start(), 0, n_seq, lambda z: squared)
    others(lambda z, n: square_arrival(z, n).wait_recv(), 0, n_seq - 1, lambda z: here >= 0)
    chan_out[...] = jnp.sum(squares_in[...], axis=0) + squares_out[...]

    @pl.when(origin)
    def _():
        for i in range(1, n_chan):
            for at in range(beyond):
                cross_arrival(i, at).wait_recv()

    @pl.when(jnp.logical_not(origin))
    def _():
        for i in range(1, n_chan):
            chan_copy(i).start()
        for i in range(1, n_chan):
            chan_copy(i).wait_recv()

    squares = jnp.sum(chan_in[...], axis=0) + jnp.sum(cross_in[...], axis=(0, 1)) + chan_out[...]
    mean = jnp.sum(squares, axis=1, keepdims=True) / (taps * groups * n_chan)
    filter_update[...] = total * jnp.minimum(1.0, 1.0 / jnp.sqrt(mean + 1e-06))

    others(lambda z, n: share_copy(z, n).wait_send(), 0, n_seq - 1, shares_to)
    others(lambda z, n: square_copy(z, n).wait_send(), 0, n_seq, lambda z: squared)

    @pl.when(squared)
    def _():
        for i in range(1, n_chan):
            cross_copy(i).wait_send()

    @pl.when(jnp.logical_not(origin))
    def _():
        for i in range(1, n_chan):
            chan_copy(i).wait_send()

    def drain(copy, count=tiles):
        def step(j, carry):
            copy(j).wait_send()
            return carry

        lax.fori_loop(0, count, step, 0)

    @pl.when(here == 2)
    def _():
        drain(late_copy, EARLY)

    @pl.when(here + 1 < n_seq)
    def _():
        drain(up_copy)

    @pl.when(here >= 1)
    def _():
        drain(down_copy)


def store_kernel(count, *refs):
    sources, targets, sems = refs[:count], refs[count : 2 * count], refs[2 * count]
    copies = [pltpu.make_async_copy(sources[n], targets[n], sems.at[n]) for n in range(count)]
    for copy in copies:
        copy.start()
    for copy in copies:
        copy.wait()


def hub_device(sizes, gate_input, key_input, value_input, cotangent, filters, document_lengths):
    n_seq, n_batch, n_chan = sizes
    seqs, span, width = gate_input.shape
    groups, taps = filters.shape
    tiles = width // LANES
    sharers = n_seq * n_batch
    share = taps // sharers
    both = 2 * span
    per_tile = groups // tiles
    dims = (n_seq, n_batch, n_chan, tiles, seqs, span, groups, taps)
    bf16, f32 = jnp.bfloat16, jnp.float32
    vmem, anywhere = pl.BlockSpec(memory_space=pltpu.VMEM), pl.BlockSpec(memory_space=pl.ANY)
    dma = pltpu.SemaphoreType.DMA
    shape = gate_input.shape
    results = pl.pallas_call(
        functools.partial(hub_kernel, dims),
        out_shape=(pltpu.VMEM(shape, bf16),) * 4 + (pltpu.VMEM((share, groups), f32),),
        in_specs=[pl.BlockSpec(memory_space=pltpu.HBM)] * 6,
        out_specs=(vmem,) * 5,
        scratch_shapes=[
            pltpu.VMEM(shape, bf16), pltpu.VMEM(shape, bf16), pltpu.VMEM(shape, bf16), pltpu.VMEM(shape, bf16),
            pltpu.VMEM((groups, taps), f32), pltpu.SMEM(document_lengths.shape, jnp.int32),
            pltpu.VMEM((tiles, seqs, both, LANES), bf16),
            pltpu.VMEM((tiles, seqs, both, LANES), bf16),
            pltpu.VMEM((tiles, seqs, span, LANES), bf16),
            pltpu.VMEM((tiles, seqs, span, LANES), bf16),
            pltpu.VMEM((tiles, per_tile // 2, both, 2 * both), bf16),
            pltpu.VMEM((tiles, per_tile // 2, both, 2 * both), bf16),
            pltpu.VMEM((4, groups, both), f32),
            pltpu.VMEM((4, both, seqs * LANES), bf16),
            pltpu.VMEM((span, seqs * LANES), bf16),
            pltpu.VMEM((7, span, seqs * LANES), f32),
            pltpu.VMEM((tiles, per_tile, 2 * both), f32),
            pltpu.VMEM((tiles, span, seqs * LANES), f32),
            pltpu.VMEM((EARLY, seqs, span, LANES), bf16),
            pltpu.VMEM((sharers, share, groups), f32),
            pltpu.VMEM((sharers, share, groups), f32),
            pltpu.VMEM((1, groups), f32),
            pltpu.VMEM((sharers, 1, groups), f32),
            pltpu.VMEM((1, groups), f32),
            pltpu.VMEM((n_chan - 1, 1, groups), f32),
            pltpu.VMEM((n_chan - 1, sharers, 1, groups), f32),
            dma((LOADS, 4)), dma((2,)),
            dma((tiles,)), dma((tiles,)), dma((tiles,)), dma((tiles,)), dma((EARLY,)), dma((EARLY,)),
            dma((sharers,)), dma((sharers,)), dma((sharers,)), dma((sharers,)),
            dma((n_chan - 1,)), dma((n_chan - 1,)), dma((n_chan - 1,)), dma((n_chan - 1, sharers)),
            pltpu.SemaphoreType.REGULAR, pltpu.SemaphoreType.REGULAR,
        ],
        compiler_params=pltpu.CompilerParams(
            collective_id=0, has_side_effects=True, vmem_limit_bytes=40 * 1024 * 1024
        ),
    )(*[
        pltpu.with_memory_space_constraint(x, pltpu.HBM)
        for x in (gate_input, key_input, value_input, cotangent, filters, document_lengths)
    ])
    like = jax.ShapeDtypeStruct(shape, bf16)
    return pl.pallas_call(
        functools.partial(store_kernel, 5),
        out_shape=(like, like, like, like, jax.ShapeDtypeStruct((share, groups), f32)),
        in_specs=[vmem] * 5,
        out_specs=(anywhere,) * 5,
        scratch_shapes=[dma((5,))],
    )(*[pltpu.with_memory_space_constraint(x, pltpu.VMEM) for x in results])


def per_device(sizes, gate_input, key_input, value_input, cotangent, filters, document_lengths):
    n_seq = sizes[0]
    span, width = gate_input.shape[1:]
    groups, taps = filters.shape
    two = document_lengths.shape[1] == 2 and n_seq == 4 and taps == n_seq * span and taps % (n_seq * sizes[1]) == 0
    if two and 2 * span == LANES and (width // LANES) % LOADS == 0 and width // LANES > AHEAD * TOGETHER + EARLY:
        device = hub_device
    else:
        device = wide_device
    return device(sizes, gate_input, key_input, value_input, cotangent, filters, document_lengths)


def solution(mesh):
    block = P("batch", "seq", "chan")
    sizes = (mesh.shape["seq"], mesh.shape["batch"], mesh.shape["chan"])
    return jax.shard_map(
        functools.partial(per_device, sizes),
        mesh=mesh,
        in_specs=(block, block, block, block, P("chan", None), P("batch", None)),
        out_specs=(block, block, block, block, P(("seq", "batch"), "chan")),
        check_vma=False,
    )
```

```python
import functools

import jax
import jax.numpy as jnp
from jax import lax
from jax.experimental import pallas as pl
from jax.experimental.pallas import tpu as pltpu
from jax.sharding import PartitionSpec as P

MESH = pl.DeviceIdType.MESH
LANES = 128
HELD = 4
SHARES_AT = 4


def kernel(
    dims, gate, key, value, cotangent, filters, lengths,
    gated_output, gate_gradient, key_gradient, value_gradient, filter_update,
    units, followers, reversed_own, plain, flipped, forward_block, backward_block,
    forward_mask, backward_mask, sums_mask, tap_sums, shares_out, shares_in, squares_out, squares_in,
    chan_out, chan_in,
    unit_send, unit_recv, cot_send, cot_recv, share_send, share_recv, square_send, square_recv,
    chan_send, chan_recv,
):
    n_seq, n_batch, n_chan, reach, wide, chunks, tiles, seqs, span, groups, taps, ndocs = dims
    everyone = n_seq * n_batch * n_chan
    sharers = n_seq * n_batch
    here = lax.axis_index("seq")
    batch = lax.axis_index("batch")
    chan = lax.axis_index("chan")
    me = (here * n_batch + batch) * n_chan + chan
    mine = here * n_batch + batch
    per_tile = LANES * groups // (tiles * chunks * LANES)
    members = LANES // per_tile
    lanes = tiles * LANES
    own = reach * span
    hub = reach == 2

    barrier = pltpu.get_barrier_semaphore()

    rest = wide - own - span
    for c in range(chunks):
        for s in range(seqs):
            units[c, s, pl.ds(0, own), :] = jnp.zeros((own, lanes), jnp.bfloat16)
            units[c, s, pl.ds(own + span, rest), :] = jnp.zeros((rest, lanes), jnp.bfloat16)
            followers[c, s, pl.ds(span, wide - span), :] = jnp.zeros((wide - span, lanes), jnp.bfloat16)

    def greet(i, carry):
        other = lax.rem(me + i, everyone)
        pl.semaphore_signal(
            barrier, inc=1, device_id_type=MESH,
            device_id={
                "seq": other // (n_batch * n_chan),
                "batch": lax.rem(other // n_chan, n_batch),
                "chan": lax.rem(other, n_chan),
            },
        )
        return carry

    lax.fori_loop(1, everyone, greet, 0)

    for c in range(chunks):
        at = pl.ds(c * lanes, lanes)
        for s in range(seqs):
            u = (key[s, :, at].astype(jnp.float32) * value[s, :, at].astype(jnp.float32)).astype(jnp.bfloat16)
            g = (cotangent[s, :, at].astype(jnp.float32) * gate[s, :, at].astype(jnp.float32)).astype(jnp.bfloat16)
            units[c, s, pl.ds(own, span), :] = u
            followers[c, s, pl.ds(0, span), :] = g

    def unit_copy(lag, c):
        source = units.at[c, :, pl.ds((reach - lag + 1) * span, span), :]
        target = units.at[c, :, pl.ds((reach - lag) * span, span), :]
        return pltpu.make_async_remote_copy(
            src_ref=source, dst_ref=target, send_sem=unit_send.at[lag - 1, c], recv_sem=unit_recv.at[lag - 1, c],
            device_id={"seq": here + 1}, device_id_type=MESH,
        )

    def cot_copy(lag, c):
        source = followers.at[c, :, pl.ds((lag - 1) * span, span), :]
        target = followers.at[c, :, pl.ds(lag * span, span), :]
        return pltpu.make_async_remote_copy(
            src_ref=source, dst_ref=target, send_sem=cot_send.at[lag - 1, c], recv_sem=cot_recv.at[lag - 1, c],
            device_id={"seq": here - 1}, device_id_type=MESH,
        )

    def sends_up(lag):
        return (here >= lag - 1) & (here + 1 < n_seq)

    def sends_down(lag):
        return (here + lag - 1 < n_seq) & (here >= 1)

    def send(lag, c):
        @pl.when(sends_up(lag))
        def _():
            unit_copy(lag, c).start()

        @pl.when(sends_down(lag))
        def _():
            cot_copy(lag, c).start()

    def receive(lag, c):
        @pl.when(here >= lag)
        def _():
            unit_copy(lag, c).wait_recv()

        @pl.when(here + lag < n_seq)
        def _():
            cot_copy(lag, c).wait_recv()

    pl.semaphore_wait(barrier, everyone - 1)
    for c in range(chunks):
        send(1, c)

    def documents(positions, s):
        count = jnp.zeros(positions.shape, jnp.int32)
        end = 0
        for n in range(ndocs):
            end = end + lengths[s, n]
            count = count + (positions >= end).astype(jnp.int32)
        return count

    rows = lax.broadcasted_iota(jnp.int32, (span, 1), 0)
    cols = lax.broadcasted_iota(jnp.int32, (1, wide), 1)
    for s in range(seqs):
        earlier = (here - reach) * span + cols
        later = here * span + cols
        target = here * span + rows
        back = here * span + (span - 1 - rows)
        earlier_doc = documents(earlier, s)
        later_doc = documents(later, s)
        target_doc = documents(target, s)
        back_doc = documents(back, s)
        keep = (earlier_doc == target_doc) & (earlier <= target) & (earlier >= 0)
        forward_mask[s] = jnp.where(keep, 1.0, 0.0).astype(jnp.bfloat16)
        if hub:
            first = cols < span
            origin = jnp.where(first, earlier + span, earlier)
            goal = jnp.where(first, back + span, back)
            goal_doc = jnp.where(first, documents(back + span, s), back_doc)
            keep = (documents(origin, s) == goal_doc) & (origin <= goal) & (origin >= 0) & (goal < n_seq * span)
        else:
            keep = (earlier_doc == back_doc) & (earlier <= back) & (earlier >= 0)
        sums_mask[s] = jnp.where(keep, 1.0, 0.0)
        keep = (later_doc == target_doc) & (later >= target) & (later < n_seq * span)
        backward_mask[s] = jnp.where(keep, 1.0, 0.0).astype(jnp.bfloat16)

    rounded = filters[...].astype(jnp.bfloat16)
    a = lax.broadcasted_iota(jnp.int32, (taps, wide), 0)
    b = lax.broadcasted_iota(jnp.int32, (taps, wide), 1)
    flip = own - b
    flip = jnp.where(flip < 0, flip + wide, flip)
    plain[...] = jnp.dot(rounded, jnp.where(a == b, 1.0, 0.0).astype(jnp.bfloat16), preferred_element_type=jnp.float32)
    flipped[...] = jnp.dot(rounded, jnp.where(a == flip, 1.0, 0.0).astype(jnp.bfloat16), preferred_element_type=jnp.float32)

    def build(t, carry):
        for i in range(per_tile):
            g = t * per_tile + i
            at = pl.ds(pl.multiple_of(g * span, span), span)
            row = jnp.broadcast_to(flipped[pl.ds(g, 1), :], (span, wide))
            forward_block[at, :] = pltpu.roll(row, 0, 1, stride=1, stride_axis=0).astype(jnp.bfloat16)
            row = jnp.broadcast_to(plain[pl.ds(g, 1), :], (span, wide))
            backward_block[at, :] = pltpu.roll(row, 0, 1, stride=1, stride_axis=0).astype(jnp.bfloat16)
        return carry

    order_a = lax.broadcasted_iota(jnp.int32, (span, span), 0)
    order_b = lax.broadcasted_iota(jnp.int32, (span, span), 1)
    exchange = jnp.where(order_a + order_b == span - 1, 1.0, 0.0).astype(jnp.bfloat16)
    lane = lax.broadcasted_iota(jnp.int32, (1, LANES), 1) // members

    def members_apart(block):
        return jnp.concatenate(
            [block * jnp.where(lane == i, 1.0, 0.0).astype(jnp.bfloat16) for i in range(per_tile)], axis=0
        )

    def paired(c, j, carry):
        at = pl.ds(pl.multiple_of(j * LANES, LANES), LANES)
        total = None
        for s in range(seqs):
            target = members_apart(reversed_own[c, s, pl.ds(0, span), at])
            if hub:
                target = jnp.concatenate([target, members_apart(reversed_own[c, s, pl.ds(span, span), at])], axis=1)
                past = units[c, s, pl.ds(own - span, span), at]
                blank = jnp.zeros((span, LANES), jnp.bfloat16)
                tail = jnp.zeros((wide - own - span, LANES), jnp.bfloat16)
                source = jnp.concatenate(
                    [
                        jnp.concatenate([blank, past, units[c, s, pl.ds(own, span), at], tail], axis=0),
                        jnp.concatenate([past, blank, blank, tail], axis=0),
                    ],
                    axis=1,
                )
            else:
                source = units[c, s, :, at]
            products = lax.dot_general(
                target, source, (((1,), (1,)), ((), ())), preferred_element_type=jnp.float32
            ).reshape(per_tile, span, wide)
            products = products * sums_mask[s][None]
            total = products if total is None else total + products
        for i in range(per_tile):
            aligned = pltpu.roll(total[i], 0, 1, stride=1, stride_axis=0)
            tap_sums[pl.ds((c * tiles + j) * per_tile + i, 1), :] = jnp.sum(aligned, axis=0, keepdims=True)
        return carry

    def reverse(c):
        for s in range(seqs):
            for n in range(2 if hub else 1):
                at = pl.ds(n * span, span)
                reversed_own[c, s, at, :] = jnp.dot(
                    exchange, followers[c, s, at, :], preferred_element_type=jnp.float32
                ).astype(jnp.bfloat16)

    for c in range(chunks):
        lax.fori_loop(c * tiles, (c + 1) * tiles, build, 0)
        for lag in range(1, reach):
            receive(lag, c)
            if not (hub and c >= HELD):
                send(lag + 1, c)
        if hub:
            reverse(c)
            lax.fori_loop(0, tiles, functools.partial(paired, c), 0)
    if not hub:
        for c in range(chunks):
            receive(reach, c)
            reverse(c)
            lax.fori_loop(0, tiles, functools.partial(paired, c), 0)

    a = lax.broadcasted_iota(jnp.int32, (taps, wide), 0)
    b = lax.broadcasted_iota(jnp.int32, (taps, wide), 1)
    pick = jnp.where(a + b == own + span - 1, 1.0, 0.0)
    by_tap = lax.dot_general(
        pick, tap_sums[...], (((1,), (1,)), ((), ())),
        precision=lax.Precision.HIGHEST, preferred_element_type=jnp.float32,
    )
    share = taps // sharers
    for i in range(sharers):
        shares_out[i] = by_tap[i * share : (i + 1) * share, :]

    def share_copy(i):
        other = lax.rem(mine + i, sharers)
        return pltpu.make_async_remote_copy(
            src_ref=shares_out.at[other], dst_ref=shares_in.at[i - 1],
            send_sem=share_send.at[i - 1], recv_sem=share_recv.at[i - 1],
            device_id={"seq": other // n_batch, "batch": lax.rem(other, n_batch)}, device_id_type=MESH,
        )

    def square_copy(i):
        other = lax.rem(mine + i, sharers)
        return pltpu.make_async_remote_copy(
            src_ref=squares_out, dst_ref=squares_in.at[i - 1],
            send_sem=square_send.at[i - 1], recv_sem=square_recv.at[i - 1],
            device_id={"seq": other // n_batch, "batch": lax.rem(other, n_batch)}, device_id_type=MESH,
        )

    def chan_copy(i):
        return pltpu.make_async_remote_copy(
            src_ref=chan_out, dst_ref=chan_in.at[i - 1],
            send_sem=chan_send.at[i - 1], recv_sem=chan_recv.at[i - 1],
            device_id={"chan": lax.rem(chan + i, n_chan)}, device_id_type=MESH,
        )

    def loop(low, high, act):
        if high <= 32:
            for i in range(low, high):
                act(i)
            return

        def step(i, carry):
            act(i)
            return carry

        lax.fori_loop(low, high, step, 0)

    def convolve(c, j, carry):
        at = pl.ds(pl.multiple_of(j * LANES, LANES), LANES)
        t = c * tiles + j
        out = pl.ds(pl.multiple_of(t * LANES, LANES), LANES)
        height = per_tile * span
        block = pl.ds(pl.multiple_of(t * height, height), height)

        def apply(block_ref, mask_ref, data_ref, s):
            masked = block_ref[block, :].reshape(per_tile, span, wide) * mask_ref[s][None]
            results = jnp.dot(
                masked.reshape(height, wide), data_ref[c, s, :, at], preferred_element_type=jnp.float32
            )
            picked = results[:span]
            for i in range(1, per_tile):
                picked = jnp.where(lane == i, results[i * span : (i + 1) * span], picked)
            return picked

        for s in range(seqs):
            filtered = apply(forward_block, forward_mask, units, s)
            gated_output[s, :, out] = (gate[s, :, out].astype(jnp.float32) * filtered).astype(jnp.bfloat16)
            gate_gradient[s, :, out] = (cotangent[s, :, out].astype(jnp.float32) * filtered).astype(jnp.bfloat16)
            adjoint = apply(backward_block, backward_mask, followers, s)
            key_gradient[s, :, out] = (adjoint * value[s, :, out].astype(jnp.float32)).astype(jnp.bfloat16)
            value_gradient[s, :, out] = (adjoint * key[s, :, out].astype(jnp.float32)).astype(jnp.bfloat16)
        return carry

    loop(1, sharers, lambda i: share_copy(i).start())
    if hub:
        for c in range(HELD, chunks):
            send(reach, c)
    for c in range(chunks):
        if hub:
            receive(reach, c)
        if c == SHARES_AT:
            loop(1, sharers, lambda i: share_copy(i).wait_recv())
            total = shares_out[mine] + jnp.sum(shares_in[...], axis=0)
            filter_update[...] = total
            squares_out[...] = jnp.sum(total * total, axis=0, keepdims=True)
        if c == SHARES_AT + 1:
            loop(1, sharers, lambda i: square_copy(i).start())
        lax.fori_loop(0, tiles, functools.partial(convolve, c), 0)
    loop(1, sharers, lambda i: square_copy(i).wait_recv())
    chan_out[...] = jnp.sum(squares_in[...], axis=0) + squares_out[...]
    loop(1, sharers, lambda i: share_copy(i).wait_send())
    loop(1, sharers, lambda i: square_copy(i).wait_send())
    loop(1, n_chan, lambda i: chan_copy(i).start())
    loop(1, n_chan, lambda i: chan_copy(i).wait_recv())
    squares = jnp.sum(chan_in[...], axis=0) + chan_out[...]
    mean = jnp.sum(squares, axis=1, keepdims=True) / (taps * groups * n_chan)
    filter_update[...] = filter_update[...] * jnp.minimum(1.0, 1.0 / jnp.sqrt(mean + 1e-06))
    loop(1, n_chan, lambda i: chan_copy(i).wait_send())
    for lag in range(1, reach + 1):
        @pl.when(sends_up(lag))
        def _():
            for c in range(chunks):
                unit_copy(lag, c).wait_send()

        @pl.when(sends_down(lag))
        def _():
            for c in range(chunks):
                cot_copy(lag, c).wait_send()


def wide_device(sizes, gate_input, key_input, value_input, cotangent, filters, document_lengths):
    n_seq, n_batch, n_chan = sizes
    seqs, span, width = gate_input.shape
    groups, taps = filters.shape
    ndocs = document_lengths.shape[1]
    longest = min(taps, n_seq * span - span)
    reach = (longest - 1) // span if ndocs == 2 else (longest - 2) // span + 1
    wide = -(-((reach + 2) * span - 1) // LANES) * LANES
    chunks = 8
    tiles = width // (chunks * LANES)
    lanes = tiles * LANES
    sharers = n_seq * n_batch
    share = taps // sharers
    dims = (n_seq, n_batch, n_chan, reach, wide, chunks, tiles, seqs, span, groups, taps, ndocs)
    bf16, f32 = jnp.bfloat16, jnp.float32
    vmem = pl.BlockSpec(memory_space=pltpu.VMEM)
    dma = pltpu.SemaphoreType.DMA
    like = jax.ShapeDtypeStruct(gate_input.shape, bf16)
    return pl.pallas_call(
        functools.partial(kernel, dims),
        out_shape=(like, like, like, like, jax.ShapeDtypeStruct((share, groups), f32)),
        in_specs=[vmem] * 5 + [pl.BlockSpec(memory_space=pltpu.SMEM)],
        out_specs=(vmem,) * 5,
        scratch_shapes=[
            pltpu.VMEM((chunks, seqs, wide, lanes), bf16),
            pltpu.VMEM((chunks, seqs, wide, lanes), bf16),
            pltpu.VMEM((chunks, seqs, 2 * span, lanes), bf16),
            pltpu.VMEM((groups, wide), f32),
            pltpu.VMEM((groups, wide), f32),
            pltpu.VMEM((groups * span, wide), bf16),
            pltpu.VMEM((groups * span, wide), bf16),
            pltpu.VMEM((seqs, span, wide), bf16),
            pltpu.VMEM((seqs, span, wide), bf16),
            pltpu.VMEM((seqs, span, wide), f32),
            pltpu.VMEM((groups, wide), f32),
            pltpu.VMEM((sharers, share, groups), f32),
            pltpu.VMEM((sharers - 1, share, groups), f32),
            pltpu.VMEM((1, groups), f32),
            pltpu.VMEM((sharers - 1, 1, groups), f32),
            pltpu.VMEM((1, groups), f32),
            pltpu.VMEM((n_chan - 1, 1, groups), f32),
            dma((reach, chunks)), dma((reach, chunks)), dma((reach, chunks)), dma((reach, chunks)),
            dma((sharers - 1,)), dma((sharers - 1,)), dma((sharers - 1,)), dma((sharers - 1,)),
            dma((n_chan - 1,)), dma((n_chan - 1,)),
        ],
        compiler_params=pltpu.CompilerParams(
            collective_id=0, has_side_effects=True, vmem_limit_bytes=60 * 1024 * 1024
        ),
    )(gate_input, key_input, value_input, cotangent, filters, document_lengths)


AHEAD = 3
BEHIND = 2
TOGETHER = 2
LOADS = 4
EARLY = 6


def hub_kernel(
    dims, gate_hbm, key_hbm, value_hbm, cotangent_hbm, filters_hbm, lengths_hbm,
    gated_output, gate_gradient, key_gradient, value_gradient, filter_update,
    gate, key, value, cotangent, filters, lengths, units, followers, up_out, down_out,
    forward_block, backward_block, bases, wide_masks, half_masks, blends, tap_sums, kept, late_in,
    shares_out, shares_in, squares_out, squares_in, chan_out, chan_in, cross_in,
    load_sem, small_sem, up_send, up_recv, down_send, down_recv, late_send, late_recv, share_send, share_recv, square_send, square_recv,
    chan_send, chan_recv, cross_send, cross_recv, up_call, down_call,
):
    n_seq, n_batch, n_chan, tiles, seqs, span, groups, taps = dims
    sharers = n_seq * n_batch
    here = lax.axis_index("seq")
    batch = lax.axis_index("batch")
    chan = lax.axis_index("chan")
    mine = here * n_batch + batch
    per_tile = groups // tiles
    members = LANES // per_tile
    both = 2 * span
    f32, bf16 = jnp.float32, jnp.bfloat16

    part = tiles // LOADS * LANES

    def loads(q):
        at = pl.ds(q * part, part)
        pairs = ((key_hbm, key), (value_hbm, value), (cotangent_hbm, cotangent), (gate_hbm, gate))
        return [
            pltpu.make_async_copy(src.at[:, :, at], dst.at[:, :, at], load_sem.at[q, n])
            for n, (src, dst) in enumerate(pairs)
        ]

    for q in range(LOADS):
        for copy in loads(q):
            copy.start()

    filters_copy = pltpu.make_async_copy(filters_hbm, filters, small_sem.at[0])
    lengths_copy = pltpu.make_async_copy(lengths_hbm, lengths, small_sem.at[1])
    lengths_copy.start()
    filters_copy.start()
    shares_in[...] = jnp.zeros(shares_in.shape, f32)
    squares_in[...] = jnp.zeros(squares_in.shape, f32)
    chan_in[...] = jnp.zeros(chan_in.shape, f32)
    cross_in[...] = jnp.zeros(cross_in.shape, f32)
    beyond = (n_seq - 1) * n_batch
    shares_out[pl.ds(beyond, n_batch)] = jnp.zeros((n_batch,) + shares_out.shape[1:], f32)

    first, last = here == 0, here == n_seq - 1
    barrier = pltpu.get_barrier_semaphore()

    def greet(device):
        pl.semaphore_signal(barrier, inc=1, device_id_type=MESH, device_id=device)

    @pl.when(jnp.logical_not(first))
    def _():
        greet({"seq": here - 1})

    @pl.when(jnp.logical_not(last))
    def _():
        greet({"seq": here + 1})

    for i in range(1, n_batch):
        greet({"batch": lax.rem(batch + i, n_batch)})
    for i in range(1, n_chan):
        greet({"chan": lax.rem(chan + i, n_chan)})
    greeted = n_batch - 1 + n_chan - 1 + jnp.where(first | last, 1, 2)

    def call(semaphore, target):
        pl.semaphore_signal(semaphore, inc=1, device_id_type=MESH, device_id={"seq": target})

    def open_calls():
        @pl.when(first)
        def _():
            call(up_call, here + 1)

        @pl.when(last)
        def _():
            call(down_call, here - 1)

    def pass_calls():
        pl.semaphore_wait(up_call, 1)
        call(up_call, here + 1)
        pl.semaphore_wait(down_call, 1)
        call(down_call, here - 1)

    def close_calls():
        @pl.when(first)
        def _():
            pl.semaphore_wait(down_call, 1)

        @pl.when(last)
        def _():
            pl.semaphore_wait(up_call, 1)

    hub = jnp.logical_not(first | last)
    own_units = units.at[:, :, pl.ds(span, span), :]
    own_cots = followers.at[:, :, pl.ds(0, span), :]

    def up_copy(j, source=up_out):
        return pltpu.make_async_remote_copy(
            src_ref=source.at[j], dst_ref=units.at[j, :, pl.ds(0, span), :],
            send_sem=up_send.at[j], recv_sem=up_recv.at[j], device_id={"seq": here + 1}, device_id_type=MESH,
        )

    def down_copy(j, source=down_out):
        return pltpu.make_async_remote_copy(
            src_ref=source.at[j], dst_ref=followers.at[j, :, pl.ds(span, span), :],
            send_sem=down_send.at[j], recv_sem=down_recv.at[j], device_id={"seq": here - 1}, device_id_type=MESH,
        )

    held_back = tiles - EARLY

    def late_copy(k):
        return pltpu.make_async_remote_copy(
            src_ref=down_out.at[held_back + k], dst_ref=late_in.at[k],
            send_sem=late_send.at[k], recv_sem=late_recv.at[k], device_id={"seq": here - 1}, device_id_type=MESH,
        )

    def gather(j, carry):
        at = pl.ds(pl.multiple_of(j * LANES, LANES), LANES)
        for s in range(seqs):
            u = (key[s, :, at].astype(f32) * value[s, :, at].astype(f32)).astype(bf16)
            g = (cotangent[s, :, at].astype(f32) * gate[s, :, at].astype(f32)).astype(bf16)
            units[j, s, pl.ds(span, span), :] = u
            followers[j, s, pl.ds(0, span), :] = g

        @pl.when(first)
        def _():
            up_copy(j, own_units).start()
            for s in range(seqs):
                units[j, s, pl.ds(0, span), :] = jnp.zeros((span, LANES), bf16)

        @pl.when(last)
        def _():
            down_copy(j, own_cots).start()
            for s in range(seqs):
                followers[j, s, pl.ds(span, span), :] = jnp.zeros((span, LANES), bf16)

        @pl.when((here == 2) & (j >= held_back))
        def _():
            down_copy(j, own_cots).start()

        return carry

    for q in range(LOADS):
        for copy in loads(q):
            copy.wait()
        if q == 0:
            pl.semaphore_wait(barrier, greeted)
            open_calls()
        lax.fori_loop(q * (tiles // LOADS), (q + 1) * (tiles // LOADS), gather, 0)

    lengths_copy.wait()
    filters_copy.wait()

    main = jnp.where(here * 2 >= n_seq, 1, 0)
    rows = lax.broadcasted_iota(jnp.int32, (both, LANES), 0)
    half = lax.broadcasted_iota(jnp.int32, (span, LANES), 0)
    one, zero = jnp.ones((), f32), jnp.zeros((), f32)

    def flag(condition):
        return jnp.where(condition, one, zero)

    for s in range(seqs):
        end = lengths[s, 0]
        at = pl.ds(s * LANES, LANES)

        def is_main(positions):
            return jnp.where(positions >= end, 1, 0) == main

        in_front = end <= both
        past_held = (here == 1) | ((here == 2) & in_front)
        next_held = (here == 2) | ((here == 1) & jnp.logical_not(in_front))
        past = (here - 1) * span
        own_main = is_main(here * span + half)
        back = both - 1 - rows
        wide_masks[0, :, at] = flag(is_main(past + rows) & ((rows >= span) | past_held)).astype(bf16)
        wide_masks[1, :, at] = flag(is_main(here * span + rows) & ((rows < span) | next_held)).astype(bf16)
        wide_masks[2, :, at] = flag(is_main(past + back) & ((back >= span) | past_held)).astype(bf16)
        wide_masks[3, :, at] = flag(jnp.logical_not(is_main(past + back)) & (back >= span)).astype(bf16)
        half_masks[:, at] = flag(jnp.logical_not(own_main)).astype(bf16)
        relay = flag((here == 1) & in_front)
        blends[0, :, at] = flag(own_main)
        blends[1, :, at] = jnp.broadcast_to(relay, (span, LANES))
        blends[2, :, at] = (1.0 - relay) * flag(is_main((here + 1) * span + half))
        blends[3, :, at] = jnp.broadcast_to(flag((here == 3) | ((here == 2) & jnp.logical_not(in_front))), (span, LANES))
        relay = flag((here == 2) & jnp.logical_not(in_front))
        blends[4, :, at] = jnp.broadcast_to(relay, (span, LANES))
        blends[5, :, at] = (1.0 - relay) * flag(is_main(past + half))
        blends[6, :, at] = jnp.broadcast_to(flag((here == 0) | ((here == 1) & in_front)), (span, LANES))

    rounded = filters[...].astype(bf16)
    a = lax.broadcasted_iota(jnp.int32, (taps, both), 0)
    b = lax.broadcasted_iota(jnp.int32, (taps, both), 1)
    for n, at in enumerate((span - b, span + both - b, span + b, b - span)):
        bases[n] = jnp.dot(rounded, flag(a == at).astype(bf16), preferred_element_type=f32)

    square_rows = lax.broadcasted_iota(jnp.int32, (both, both), 0)
    square_cols = lax.broadcasted_iota(jnp.int32, (both, both), 1)
    unwrapped = square_cols < both - square_rows

    def build(block, n):
        def tile(t, carry):
            for i in range(per_tile):
                g = pl.ds(t * per_tile + i, 1)
                row = jnp.where(unwrapped, bases[n, g, :], bases[n + 1, g, :])
                rolled = pltpu.roll(row, 0, 1, stride=1, stride_axis=0)
                block[t, i // 2, :, pl.ds(i % 2 * both, both)] = rolled.astype(bf16)
            return carry

        return tile

    pairs = per_tile // 2
    wide = seqs * LANES
    lane = lax.rem(lax.broadcasted_iota(jnp.int32, (1, wide), 1), LANES) // members
    parity = [flag(lax.rem(lane, 2) == e).astype(bf16) for e in range(2)]
    pair_masks = [flag(lane // 2 == k).astype(bf16) for k in range(pairs)]
    blank = jnp.zeros((span, wide), bf16)

    def across(ref, j, at):
        return jnp.concatenate([ref[j, s, at, :] for s in range(seqs)], axis=1)

    def own_lanes(results, height):
        picked = results[:height]
        for k in range(1, pairs):
            picked = jnp.where(lane // 2 == k, results[k * height : (k + 1) * height], picked)
        return picked

    def apply(block, data):
        height = block.shape[1]
        results = jnp.dot(block.reshape(pairs * height, 2 * both), data, preferred_element_type=f32)
        return own_lanes(results, height)

    whole, low, top = pl.ds(0, both), pl.ds(0, span), pl.ds(span, span)

    def forward(j):
        at = pl.ds(pl.multiple_of(j * LANES, LANES), LANES)
        window = across(units, j, whole)
        held = window * wide_masks[0]
        other = window[span:] * half_masks[...]
        result = apply(forward_block[j], jnp.concatenate([held * p for p in parity], axis=0))
        rest = apply(
            forward_block[j, :, low, :],
            jnp.concatenate([blank, other * parity[0], blank, other * parity[1]], axis=0),
        )
        sent = (blends[1] * window[span:].astype(f32) + blends[2] * result[span:]).astype(bf16)
        filtered = jnp.where(blends[0] > 0.5, result[:span], rest) + blends[3] * window[:span].astype(f32)
        for s in range(seqs):
            mine_at = slice(s * LANES, (s + 1) * LANES)
            up_out[j, s] = sent[:, mine_at]
            gated_output[s, :, at] = (gate[s, :, at].astype(f32) * filtered[:, mine_at]).astype(bf16)
            gate_gradient[s, :, at] = (cotangent[s, :, at].astype(f32) * filtered[:, mine_at]).astype(bf16)

    def backward(j):
        at = pl.ds(pl.multiple_of(j * LANES, LANES), LANES)
        window = across(followers, j, whole)
        held = window * wide_masks[1]
        other = window[:span] * half_masks[...]
        result = apply(backward_block[j], jnp.concatenate([held * p for p in parity], axis=0))
        rest = apply(
            backward_block[j, :, top, :],
            jnp.concatenate([other * parity[0], blank, other * parity[1], blank], axis=0),
        )
        late = jnp.where(j >= held_back, one, zero)
        relayed = (1.0 - late) * blends[4]
        added = (1.0 - late * flag(here == 1)) * blends[6]
        sent = (relayed * window[:span].astype(f32) + blends[5] * result[:span]).astype(bf16)
        adjoint = jnp.where(blends[0] > 0.5, result[span:], rest) + added * window[span:].astype(f32)
        kept[j] = adjoint
        for s in range(seqs):
            mine_at = slice(s * LANES, (s + 1) * LANES)
            down_out[j, s] = sent[:, mine_at]
            key_gradient[s, :, at] = (adjoint[:, mine_at] * value[s, :, at].astype(f32)).astype(bf16)
            value_gradient[s, :, at] = (adjoint[:, mine_at] * key[s, :, at].astype(f32)).astype(bf16)

    def conclude(k, carry):
        late_copy(k).wait_recv()
        j = held_back + k
        at = pl.ds(pl.multiple_of(j * LANES, LANES), LANES)
        for s in range(seqs):
            adjoint = kept[j, :, pl.ds(s * LANES, LANES)] + late_in[k, s].astype(f32)
            key_gradient[s, :, at] = (adjoint * value[s, :, at].astype(f32)).astype(bf16)
            value_gradient[s, :, at] = (adjoint * key[s, :, at].astype(f32)).astype(bf16)
        return carry

    exchange = flag(square_rows + square_cols == both - 1).astype(bf16)
    wrapped = flag(square_cols < square_rows)

    def paired(j, outer=False):
        source = jnp.concatenate([blank, across(units, j, top)], axis=0) if outer else across(units, j, whole)
        reversed_units = jnp.dot(exchange, source, preferred_element_type=f32).astype(bf16)
        held = reversed_units * wide_masks[2]
        other = reversed_units * wide_masks[3]
        sources = jnp.concatenate(
            [jnp.concatenate([x * p for p in parity], axis=0) for x in (held, other)], axis=1
        )
        window = across(followers, j, low if outer else whole)
        held = window * (wide_masks[1, low, :] if outer else wide_masks[1])
        other = window[:span] * half_masks[...]

        def by_pair(x):
            repeat = x.shape[1] // wide
            return jnp.concatenate([x * jnp.concatenate([m] * repeat, axis=1) for m in pair_masks], axis=0)

        contract = (((1,), (1,)), ((), ()))
        own = lax.dot_general(
            by_pair(jnp.concatenate([held[:span], other], axis=1)), sources, contract, preferred_element_type=f32
        )
        if not outer:
            next_ones = lax.dot_general(by_pair(held[span:]), sources[:, :wide], contract, preferred_element_type=f32)
        for i in range(per_tile):
            at = slice(i // 2 * span, (i // 2 + 1) * span)
            across_at = slice(i % 2 * both, (i % 2 + 1) * both)
            near = pltpu.roll(own[at, across_at], 0, 1, stride=1, stride_axis=0)
            total, high = near, near * wrapped[:span]
            if not outer:
                far = pltpu.roll(next_ones[at, across_at], span, 1, stride=1, stride_axis=0)
                total, high = total + far, high + far * wrapped[span:]
            total = jnp.sum(total, axis=0, keepdims=True)
            high = jnp.sum(high, axis=0, keepdims=True)
            tap_sums[j, pl.ds(i, 1), pl.ds(0, both)] = total - high
            tap_sums[j, pl.ds(i, 1), pl.ds(both, both)] = high

    def up_wait(j):
        @pl.when(jnp.logical_not(first))
        def _():
            up_copy(j).wait_recv()

    def down_wait(j):
        @pl.when(jnp.logical_not(last))
        def _():
            down_copy(j).wait_recv()

    def up_start(j):
        @pl.when(hub)
        def _():
            up_copy(j).start()

    def down_start(j):
        @pl.when((here == 1) | ((here == 2) & (j < held_back)))
        def _():
            down_copy(j).start()

        @pl.when((here == 2) & (j >= held_back))
        def _():
            late_copy(jnp.maximum(j - held_back, 0)).start()

    steps = tiles // TOGETHER
    early_steps = EARLY // TOGETHER

    def forwards(n):
        return [n * TOGETHER + k for k in range(TOGETHER)]

    def rotated(n):
        return forwards(lax.rem(n + steps - early_steps, steps))

    spread = (n_seq - 1) * span
    a = lax.broadcasted_iota(jnp.int32, (spread, 2 * both), 0)
    b = lax.broadcasted_iota(jnp.int32, (spread, 2 * both), 1)
    pick = flag(((a == b - (span - 1)) & (b < both)) | ((a == b - both + span + 1) & (b >= both))).astype(bf16)
    share = taps // sharers

    def share_copy(z, n):
        return pltpu.make_async_remote_copy(
            src_ref=shares_out.at[z * n_batch + n], dst_ref=shares_in.at[mine],
            send_sem=share_send.at[z * n_batch + n], recv_sem=share_recv.at[mine],
            device_id={"seq": z, "batch": n}, device_id_type=MESH,
        )

    def share_arrival(z, n):
        at = z * n_batch + n
        return pltpu.make_async_remote_copy(
            src_ref=shares_out.at[at], dst_ref=shares_in.at[at], send_sem=share_send.at[at],
            recv_sem=share_recv.at[at], device_id={"seq": z, "batch": n}, device_id_type=MESH,
        )

    def square_copy(z, n):
        return pltpu.make_async_remote_copy(
            src_ref=squares_out, dst_ref=squares_in.at[mine],
            send_sem=square_send.at[z * n_batch + n], recv_sem=square_recv.at[mine],
            device_id={"seq": z, "batch": n}, device_id_type=MESH,
        )

    def square_arrival(z, n):
        at = z * n_batch + n
        return pltpu.make_async_remote_copy(
            src_ref=squares_out, dst_ref=squares_in.at[at], send_sem=square_send.at[at],
            recv_sem=square_recv.at[at], device_id={"seq": z, "batch": n}, device_id_type=MESH,
        )

    def others(act, low, high, allowed):
        for z in range(low, high):
            for n in range(n_batch):
                @pl.when(allowed(z) & (mine != z * n_batch + n))
                def _():
                    act(z, n)

    def shares_to(z):
        return hub if z > 0 else hub | first | last

    def shares_from(z):
        return (first | hub) & (here < n_seq - 1) if 0 < z < n_seq - 1 else first

    def send_shares():
        sums = tap_sums[...].reshape(groups, 2 * both)
        by_tap = jnp.zeros((spread, groups), f32)
        for _ in range(3):
            piece = sums.astype(bf16)
            sums = sums - piece.astype(f32)
            by_tap = by_tap + lax.dot_general(pick, piece, (((1,), (1,)), ((), ())), preferred_element_type=f32)
        for i in range(spread // share):
            shares_out[i] = by_tap[i * share : (i + 1) * share, :]
        others(lambda z, n: share_copy(z, n).start(), 0, n_seq - 1, shares_to)

    def sweep(near, far, order, far_block, far_base, ahead, lag):
        near_wait, near_math, near_start = near
        far_wait, far_math, far_start = far
        portion = -(-tiles // ahead)

        def run(low, high, near_at=None, far_at=None, paired_at=()):
            def step(n, carry):
                nears = forwards(n + near_at) if near_at is not None else []
                fars = order(n) if far_at is not None else []
                pairings = [j for offset in paired_at for j in forwards(n + offset)]
                for j in nears:
                    near_wait(j)
                for j in fars:
                    far_wait(j)
                for j in nears:
                    near_math(j)
                for j in fars:
                    far_math(j)
                for j in pairings:
                    paired(j)
                for j in nears:
                    near_start(j)
                for j in fars:
                    far_start(j)
                if not fars:
                    lax.fori_loop(
                        n * portion, jnp.minimum((n + 1) * portion, tiles), build(far_block, far_base), 0
                    )
                return carry

            lax.fori_loop(low, high, step, 0)

        run(0, ahead, near_at=0)
        pass_calls()
        run(0, lag, near_at=ahead, far_at=0)
        run(lag, steps - ahead, near_at=ahead, far_at=0, paired_at=(-lag,))
        run(steps - ahead, steps - ahead + lag, far_at=0, paired_at=(-lag, ahead - lag) if lag else (0,))
        run(steps - ahead + lag, steps, far_at=0, paired_at=(-lag,))
        send_shares()

    def alone(near, far, order):
        near_wait, near_math, near_start = near
        far_wait, far_math, far_start = far

        def local(n, carry):
            for j in forwards(n):
                near_math(j)
                paired(j, outer=True)
            return carry

        def finish(n, carry):
            for j in order(n):
                far_wait(j)
            for j in order(n):
                far_math(j)
            return carry

        lax.fori_loop(0, tiles, build(forward_block, 0), 0)
        lax.fori_loop(0, tiles, build(backward_block, 2), 0)
        lax.fori_loop(0, steps, local, 0)
        close_calls()
        send_shares()
        lax.fori_loop(0, steps, finish, 0)

    up_stage = (up_wait, forward, up_start)
    down_stage = (down_wait, backward, down_start)

    @pl.when(first)
    def _():
        alone(up_stage, down_stage, rotated)

    @pl.when(last)
    def _():
        alone(down_stage, up_stage, forwards)

    @pl.when(here == 1)
    def _():
        lax.fori_loop(0, tiles, build(forward_block, 0), 0)
        sweep(up_stage, down_stage, rotated, backward_block, 2, AHEAD, early_steps)
        lax.fori_loop(0, EARLY, conclude, 0)

    @pl.when(here == 2)
    def _():
        lax.fori_loop(0, tiles, build(backward_block, 2), 0)
        sweep(down_stage, up_stage, forwards, forward_block, 0, BEHIND, 0)

    def chan_copy(i):
        return pltpu.make_async_remote_copy(
            src_ref=chan_out, dst_ref=chan_in.at[i - 1],
            send_sem=chan_send.at[i - 1], recv_sem=chan_recv.at[i - 1],
            device_id={"chan": lax.rem(chan + i, n_chan)}, device_id_type=MESH,
        )

    others(lambda z, n: share_arrival(z, n).wait_recv(), 0, n_seq, shares_from)
    total = shares_out[mine] + jnp.sum(shares_in[...], axis=0)
    squares_out[...] = jnp.sum(total * total, axis=0, keepdims=True)
    squared = jnp.logical_not(last)
    origin = mine == 0

    def cross_copy(i):
        return pltpu.make_async_remote_copy(
            src_ref=squares_out, dst_ref=cross_in.at[i - 1, mine],
            send_sem=cross_send.at[i - 1], recv_sem=cross_recv.at[i - 1, mine],
            device_id={"seq": 0, "batch": 0, "chan": lax.rem(chan + i, n_chan)}, device_id_type=MESH,
        )

    def cross_arrival(i, at):
        return pltpu.make_async_remote_copy(
            src_ref=squares_out, dst_ref=cross_in.at[i - 1, at],
            send_sem=cross_send.at[i - 1], recv_sem=cross_recv.at[i - 1, at],
            device_id={"seq": 0, "batch": 0, "chan": lax.rem(chan + i, n_chan)}, device_id_type=MESH,
        )

    @pl.when(squared)
    def _():
        for i in range(1, n_chan):
            cross_copy(i).start()

    others(lambda z, n: square_copy(z, n).start(), 0, n_seq, lambda z: squared)
    others(lambda z, n: square_arrival(z, n).wait_recv(), 0, n_seq - 1, lambda z: here >= 0)
    chan_out[...] = jnp.sum(squares_in[...], axis=0) + squares_out[...]

    @pl.when(origin)
    def _():
        for i in range(1, n_chan):
            for at in range(beyond):
                cross_arrival(i, at).wait_recv()

    @pl.when(jnp.logical_not(origin))
    def _():
        for i in range(1, n_chan):
            chan_copy(i).start()
        for i in range(1, n_chan):
            chan_copy(i).wait_recv()

    squares = jnp.sum(chan_in[...], axis=0) + jnp.sum(cross_in[...], axis=(0, 1)) + chan_out[...]
    mean = jnp.sum(squares, axis=1, keepdims=True) / (taps * groups * n_chan)
    filter_update[...] = total * jnp.minimum(1.0, 1.0 / jnp.sqrt(mean + 1e-06))

    others(lambda z, n: share_copy(z, n).wait_send(), 0, n_seq - 1, shares_to)
    others(lambda z, n: square_copy(z, n).wait_send(), 0, n_seq, lambda z: squared)

    @pl.when(squared)
    def _():
        for i in range(1, n_chan):
            cross_copy(i).wait_send()

    @pl.when(jnp.logical_not(origin))
    def _():
        for i in range(1, n_chan):
            chan_copy(i).wait_send()

    def drain(copy, count=tiles):
        def step(j, carry):
            copy(j).wait_send()
            return carry

        lax.fori_loop(0, count, step, 0)

    @pl.when(here == 2)
    def _():
        drain(late_copy, EARLY)

    @pl.when(here + 1 < n_seq)
    def _():
        drain(up_copy)

    @pl.when(here >= 1)
    def _():
        drain(down_copy)


def store_kernel(count, *refs):
    sources, targets, sems = refs[:count], refs[count : 2 * count], refs[2 * count]
    copies = [pltpu.make_async_copy(sources[n], targets[n], sems.at[n]) for n in range(count)]
    for copy in copies:
        copy.start()
    for copy in copies:
        copy.wait()


def hub_device(sizes, gate_input, key_input, value_input, cotangent, filters, document_lengths):
    n_seq, n_batch, n_chan = sizes
    seqs, span, width = gate_input.shape
    groups, taps = filters.shape
    tiles = width // LANES
    sharers = n_seq * n_batch
    share = taps // sharers
    both = 2 * span
    per_tile = groups // tiles
    dims = (n_seq, n_batch, n_chan, tiles, seqs, span, groups, taps)
    bf16, f32 = jnp.bfloat16, jnp.float32
    vmem, anywhere = pl.BlockSpec(memory_space=pltpu.VMEM), pl.BlockSpec(memory_space=pl.ANY)
    dma = pltpu.SemaphoreType.DMA
    shape = gate_input.shape
    results = pl.pallas_call(
        functools.partial(hub_kernel, dims),
        out_shape=(pltpu.VMEM(shape, bf16),) * 4 + (pltpu.VMEM((share, groups), f32),),
        in_specs=[pl.BlockSpec(memory_space=pltpu.HBM)] * 6,
        out_specs=(vmem,) * 5,
        scratch_shapes=[
            pltpu.VMEM(shape, bf16), pltpu.VMEM(shape, bf16), pltpu.VMEM(shape, bf16), pltpu.VMEM(shape, bf16),
            pltpu.VMEM((groups, taps), f32), pltpu.SMEM(document_lengths.shape, jnp.int32),
            pltpu.VMEM((tiles, seqs, both, LANES), bf16),
            pltpu.VMEM((tiles, seqs, both, LANES), bf16),
            pltpu.VMEM((tiles, seqs, span, LANES), bf16),
            pltpu.VMEM((tiles, seqs, span, LANES), bf16),
            pltpu.VMEM((tiles, per_tile // 2, both, 2 * both), bf16),
            pltpu.VMEM((tiles, per_tile // 2, both, 2 * both), bf16),
            pltpu.VMEM((4, groups, both), f32),
            pltpu.VMEM((4, both, seqs * LANES), bf16),
            pltpu.VMEM((span, seqs * LANES), bf16),
            pltpu.VMEM((7, span, seqs * LANES), f32),
            pltpu.VMEM((tiles, per_tile, 2 * both), f32),
            pltpu.VMEM((tiles, span, seqs * LANES), f32),
            pltpu.VMEM((EARLY, seqs, span, LANES), bf16),
            pltpu.VMEM((sharers, share, groups), f32),
            pltpu.VMEM((sharers, share, groups), f32),
            pltpu.VMEM((1, groups), f32),
            pltpu.VMEM((sharers, 1, groups), f32),
            pltpu.VMEM((1, groups), f32),
            pltpu.VMEM((n_chan - 1, 1, groups), f32),
            pltpu.VMEM((n_chan - 1, sharers, 1, groups), f32),
            dma((LOADS, 4)), dma((2,)),
            dma((tiles,)), dma((tiles,)), dma((tiles,)), dma((tiles,)), dma((EARLY,)), dma((EARLY,)),
            dma((sharers,)), dma((sharers,)), dma((sharers,)), dma((sharers,)),
            dma((n_chan - 1,)), dma((n_chan - 1,)), dma((n_chan - 1,)), dma((n_chan - 1, sharers)),
            pltpu.SemaphoreType.REGULAR, pltpu.SemaphoreType.REGULAR,
        ],
        compiler_params=pltpu.CompilerParams(
            collective_id=0, has_side_effects=True, vmem_limit_bytes=40 * 1024 * 1024
        ),
    )(*[
        pltpu.with_memory_space_constraint(x, pltpu.HBM)
        for x in (gate_input, key_input, value_input, cotangent, filters, document_lengths)
    ])
    like = jax.ShapeDtypeStruct(shape, bf16)
    return pl.pallas_call(
        functools.partial(store_kernel, 5),
        out_shape=(like, like, like, like, jax.ShapeDtypeStruct((share, groups), f32)),
        in_specs=[vmem] * 5,
        out_specs=(anywhere,) * 5,
        scratch_shapes=[dma((5,))],
    )(*[pltpu.with_memory_space_constraint(x, pltpu.VMEM) for x in results])


def per_device(sizes, gate_input, key_input, value_input, cotangent, filters, document_lengths):
    n_seq = sizes[0]
    span, width = gate_input.shape[1:]
    groups, taps = filters.shape
    two = document_lengths.shape[1] == 2 and n_seq == 4 and taps == n_seq * span and taps % (n_seq * sizes[1]) == 0
    if two and 2 * span == LANES and (width // LANES) % LOADS == 0 and width // LANES > AHEAD * TOGETHER + EARLY:
        device = hub_device
    else:
        device = wide_device
    return device(sizes, gate_input, key_input, value_input, cotangent, filters, document_lengths)


def solution(mesh):
    block = P("batch", "seq", "chan")
    sizes = (mesh.shape["seq"], mesh.shape["batch"], mesh.shape["chan"])
    return jax.shard_map(
        functools.partial(per_device, sizes),
        mesh=mesh,
        in_specs=(block, block, block, block, P("chan", None), P("batch", None)),
        out_specs=(block, block, block, block, P(("seq", "batch"), "chan")),
        check_vma=False,
    )
```
